32 devices in a mesh: dp: 8 (over z, y), tensor: 4 (over x, core).
Axes of the slice: x: 2, y: 2, z: 4, core: 2. Of those that a mesh axis runs over, the one named last changes fastest.
Arguments:
- inputs: bfloat16 [4096, 512], P('dp'), may hold values from -6 to 6
- query_weight: bfloat16 [512, 512], P(None, 'tensor'), may hold values from -0.25 to 0.25
- key_weight: bfloat16 [512, 512], P(None, 'tensor'), may hold values from -0.25 to 0.25
- value_weight: bfloat16 [512, 512], P(None, 'tensor'), may hold values from -0.25 to 0.25
- query_bias: float32 [512], P('tensor'), may hold values from -3 to 3
- value_bias: float32 [512], P('tensor'), may hold values from -3 to 3
- position_bias: float32 [49, 16], P(None, 'tensor'), may hold values from -4 to 4
- proj_weight: bfloat16 [512, 512], P('tensor'), may hold values from -0.5 to 0.5
- proj_bias: float32 [512], replicated, may hold values from -2 to 2
- norm1_gain: float32 [512], replicated, may hold values from 0.5 to 1.5
- norm1_shift: float32 [512], replicated, may hold values from -2 to 2
- norm2_gain: float32 [512], replicated, may hold values from 0.5 to 1.5
- norm2_shift: float32 [512], replicated, may hold values from -2 to 2
- up_weight: bfloat16 [512, 2048], P(None, 'tensor'), may hold values from -0.25 to 0.25
- up_bias: float32 [2048], P('tensor'), may hold values from -2 to 2
- down_weight: bfloat16 [2048, 512], P('tensor'), may hold values from -0.25 to 0.25
- down_bias: float32 [512], replicated, may hold values from -2 to 2
- segment_ids: int32 [8, 512], P('dp'), may hold values from 0 to 3, never falling along the last dimension, each value on 1 to 256 neighbouring positions
- valid_mask: int32 [8, 512], P('dp'), may hold values 0 or 1
- position_index: int32 [16, 16], replicated, may hold values from 0 to 48
- out_cotangent: bfloat16 [4096, 512], P('dp'), may hold values from -6 to 6
Outputs:
- layer_out: float32 [4096, 512], P('dp')
- input_grad: float32 [4096, 512], P('dp')
- query_weight_grad: float32 [512, 512], P(None, 'tensor')
- key_weight_grad: float32 [512, 512], P(None, 'tensor')
- value_weight_grad: float32 [512, 512], P(None, 'tensor')
- query_bias_grad: float32 [512], P('tensor')
- value_bias_grad: float32 [512], P('tensor')
- position_bias_grad: float32 [49, 16], P(None, 'tensor')
- proj_weight_grad: float32 [512, 512], P('tensor')
- proj_bias_grad: float32 [512], replicated
- norm1_gain_grad: float32 [512], replicated
- norm1_shift_grad: float32 [512], replicated
- norm2_gain_grad: float32 [512], replicated
- norm2_shift_grad: float32 [512], replicated
- up_weight_grad: float32 [512, 2048], P(None, 'tensor')
- up_bias_grad: float32 [2048], P('tensor')
- down_weight_grad: float32 [2048, 512], P('tensor')
- down_bias_grad: float32 [512], replicated
The draws below stay inside these ranges and needn't reach their ends.
Inputs may be any that keep to these rules, and one draw needn't show every extreme that they name: `segment_ids`: within each grid the clip numbers never fall, and each clip has 1 to 256 patches.
All inputs are finite; a program needn't handle non-finite values. No bound on the sum of `valid_mask` on one device may be relied on, other than what follows from the above.
Results may differ from the reference program's by a relative error of at most 0.012.
Values may be sent and summed in bfloat16 or wider, within the bound.
No kernel may reach another device: no remote copies, remote signals or barrier semaphores. Data moves between devices by JAX's collectives and lax.ppermute only.
A program may use at most 64 MiB of HBM per device.

```python
import math
import jax
import jax.numpy as jnp
import numpy as np
from jax import lax

D = 512
HEADS = 16
HD = 32
FF = 2048
GH = 64
GW = 8
WS = 4
CLIPS = 4
WIN = 16
NREL = 49
GT = 512
GRIDS = 8
TOKENS = 4096


def set_ends(drawn, stream_key, smallest, top_value):
    dims = drawn.shape
    spot = [jax.random.randint(jax.random.fold_in(stream_key, axis), (), 0, dims[axis]) for axis in range(len(dims))]
    drawn = drawn.at[tuple(spot)].set(smallest)
    longest = dims.index(max(dims))
    spot[longest] = (spot[longest] + 1) % dims[longest]
    return drawn.at[tuple(spot)].set(top_value)


def shard_levels(key, extent, split, low, largest):
    def one(position, blocks):
        heights = jax.random.uniform(jax.random.fold_in(jax.random.fold_in(key, 6), position), (blocks,), jnp.float32, low / len(split), largest / len(split))
        return jnp.repeat(jnp.exp(heights), extent[position] // blocks).reshape((-1,) + (1,) * (len(extent) - position - 1))

    loudness = one(*split[0])
    for cut in split[1:]:
        loudness = loudness * one(*cut)
    return loudness


def split_up(amount, total, most, slope):
    weights = [(1 << 20) // math.isqrt(rank ** slope) + 1 for rank in range(2, amount + 1)]
    rest, given = total - most - (amount - 1), [1] * (amount - 1)
    while rest > 0:
        candidates = [i for i in range(amount - 1) if given[i] < most]
        pool, left = sum([weights[i] for i in candidates]), rest
        for i in candidates:
            extra = min(most - given[i], max(1, left * weights[i] // pool), rest)
            given[i] = given[i] + extra
            rest = rest - extra
    return np.array([most] + given)


def ragged_sizes(own_key, amount, total, limit, skew):
    if amount == 2:
        one = jax.random.randint(own_key, (), max(1, total - limit), min(limit, total - 1) + 1)
        return jnp.stack([one, total - one])
    sizes = jnp.asarray(split_up(amount, total, limit, skew), jnp.int32)
    pairs = (amount - 1) // 2
    source_of, sink = sizes[1:1 + 2 * pairs:2], sizes[2:2 + 2 * pairs:2]
    slack = jnp.minimum(source_of - 1, limit - sink)
    moved = jax.random.randint(jax.random.fold_in(own_key, 1), (pairs,), 0, 1 << 20) % (slack + 1)
    sizes = sizes.at[1:1 + 2 * pairs:2].set(source_of - moved).at[2:2 + 2 * pairs:2].set(sink + moved)
    return sizes[jax.random.permutation(jax.random.fold_in(own_key, 2), amount)]


def noise(own_key, dims, scale, most, split=(), held_as=jnp.bfloat16):
    drawn = jax.random.normal(own_key, dims, jnp.float32) * scale
    if len(split) > 0:
        drawn = shard_levels(own_key, dims, split, -0.22, 0.18) * drawn
    return jnp.clip(drawn, min=-most, max=most).astype(held_as)


def setup_inputs(seed: int = 0) -> dict:
    keys = jax.random.split(jax.random.key(seed), 22)
    return {
        "inputs": noise(keys[0], (TOKENS, D), 1.0, 6.0, ((0, 8),)),
        "query_weight": noise(keys[1], (D, D), D ** -0.5, 0.25, ((1, 4),)),
        "key_weight": noise(keys[2], (D, D), D ** -0.5, 0.25, ((1, 4),)),
        "value_weight": noise(keys[3], (D, D), D ** -0.5, 0.25, ((1, 4),)),
        "query_bias": noise(keys[4], (D,), 0.5, 3.0, ((0, 4),), jnp.float32),
        "value_bias": noise(keys[5], (D,), 0.5, 3.0, ((0, 4),), jnp.float32),
        "position_bias": noise(keys[6], (NREL, HEADS), 1.0, 4.0, ((1, 4),), jnp.float32),
        "proj_weight": noise(keys[7], (D, D), (D // 4) ** -0.5, 0.5, ((0, 4),)),
        "proj_bias": noise(keys[8], (D,), 0.3, 2.0, (), jnp.float32),
        "norm1_gain": jnp.clip(1.0 + 0.1 * jax.random.normal(keys[9], (D,), jnp.float32), 0.5, 1.5),
        "norm1_shift": noise(keys[10], (D,), 0.3, 2.0, (), jnp.float32),
        "norm2_gain": jnp.clip(1.0 + 0.1 * jax.random.normal(keys[11], (D,), jnp.float32), 0.5, 1.5),
        "norm2_shift": noise(keys[12], (D,), 0.3, 2.0, (), jnp.float32),
        "up_weight": noise(keys[13], (D, FF), D ** -0.5, 0.25, ((1, 4),)),
        "up_bias": noise(keys[14], (FF,), 0.3, 2.0, ((0, 4),), jnp.float32),
        "down_weight": noise(keys[15], (FF, D), (FF // 4) ** -0.5, 0.25, ((0, 4),)),
        "down_bias": noise(keys[16], (D,), 0.3, 2.0, (), jnp.float32),
        "segment_ids": jax.vmap(lambda own: jnp.searchsorted(jnp.cumsum(ragged_sizes(own, CLIPS, GT, GT // 2, 0)), jnp.arange(GT), side="right"))(jax.random.split(keys[17], GRIDS)).reshape((GRIDS, GT)).astype(jnp.int32),
        "valid_mask": set_ends((jax.random.randint(keys[18], (GRIDS, GT), 0, 8) < 7).astype(jnp.int32), jax.random.fold_in(keys[18], 1), 0, 1),
        "position_index": set_ends(jax.random.randint(keys[19], (WIN, WIN), 0, NREL), jax.random.fold_in(keys[19], 1), 0, NREL - 1).astype(jnp.int32),
        "out_cotangent": noise(keys[20], (TOKENS, D), 1.0, 6.0, ((0, 8),)),
    }


@jax.custom_vjp
def low(v):
    return lax.optimization_barrier(v.astype(jnp.bfloat16)).astype(jnp.float32)

@jax.custom_vjp
def low_back(v):
    return v

def low_keep(v):
    return (low(v), None)

def low_pass(kept, grad):
    return (grad,)

def back_keep(v):
    return (v, None)

def back_low(kept, grad):
    return (low(grad),)
low.defvjp(low_keep, low_pass)
low_back.defvjp(back_keep, back_low)
NEG_FILL = -1e+30

def layer_norm(value, gain, shift):
    centre = value - lax.optimization_barrier(jnp.mean(value, axis=-1, keepdims=True))
    spread = lax.optimization_barrier(jnp.mean(centre * centre, axis=-1, keepdims=True))
    return centre * lax.rsqrt(spread + 1e-06) * gain + shift

def dot_high(left, right):
    return jnp.dot(left, right, precision=lax.Precision.HIGHEST)

def to_windows(field):
    grids = field.shape[0] // (GH * GW)
    chans = field.shape[-1]
    shaped = field.reshape(grids, GH // WS, WS, GW // WS, WS, chans)
    return shaped.transpose(0, 1, 3, 2, 4, 5).reshape(-1, WS * WS, chans)

def from_windows(field):
    chans = field.shape[-1]
    grids = field.shape[0] // (GH // WS * (GW // WS))
    shaped = field.reshape(grids, GH // WS, GW // WS, WS, WS, chans)
    return shaped.transpose(0, 1, 3, 2, 4, 5).reshape(-1, chans)

def forward(inputs, params, segs, valid, position_index):
    wq, wk, wv, bq, bv, prel, wo, bo, g1, s1, g2, s2, w1, b1, w2, b2 = params
    first = low(layer_norm(inputs, g1, s1))
    query = low_back(low(dot_high(first, wq) + bq))
    key = low_back(low(dot_high(first, wk)))
    value = low_back(low(dot_high(first, wv) + bv))
    qwin = to_windows(query).reshape(-1, WIN, HEADS, HD)
    kwin = to_windows(key).reshape(-1, WIN, HEADS, HD)
    vwin = to_windows(value).reshape(-1, WIN, HEADS, HD)
    bias = prel[position_index.reshape(-1)].reshape(WIN, WIN, HEADS).transpose(2, 0, 1)
    segwin = to_windows(segs.reshape(-1, 1))[:, :, 0]
    validwin = to_windows(valid.reshape(-1, 1))[:, :, 0]
    same = segwin[:, :, None] == segwin[:, None, :]
    selfs = jnp.eye(WIN, dtype=jnp.int32) > 0
    allowed = same & ((validwin[:, None, :] > 0) | selfs[None])
    scores = jnp.einsum('wqhd,wkhd->whqk', qwin, kwin, precision=lax.Precision.HIGHEST) * HD ** (-0.5) + bias[None]
    scores = low_back(scores)
    scores = jnp.where(allowed[:, None], scores, NEG_FILL)
    probs = low(jax.nn.softmax(scores, axis=-1))
    attended = jnp.einsum('whqk,wkhd->wqhd', probs, vwin, precision=lax.Precision.HIGHEST)
    attended = from_windows(attended.reshape(-1, WIN, HEADS * HD))
    attended = low_back(low(attended))
    mid = inputs + low_back(dot_high(attended, wo)) + bo
    second = low(layer_norm(mid, g2, s2))
    pre = low_back(dot_high(second, w1) + b1)
    hidden = low(jax.nn.gelu(pre, approximate=True))
    return mid + low_back(dot_high(hidden, w2)) + b2

def reference(inputs, query_weight, key_weight, value_weight, query_bias, value_bias, position_bias, proj_weight, proj_bias, norm1_gain, norm1_shift, norm2_gain, norm2_shift, up_weight, up_bias, down_weight, down_bias, segment_ids, valid_mask, position_index, out_cotangent):
    params = tuple((p.astype(jnp.float32) for p in (query_weight, key_weight, value_weight, query_bias, value_bias, position_bias, proj_weight, proj_bias, norm1_gain, norm1_shift, norm2_gain, norm2_shift, up_weight, up_bias, down_weight, down_bias)))
    grids = segment_ids.shape[0]
    xs = inputs.astype(jnp.float32).reshape(grids, GT, D)
    gs = out_cotangent.astype(jnp.float32).reshape(grids, GT, D)

    def step(carry, item):
        xgrid, ggrid, sgrid, vgrid = item
        outs, pull = jax.vjp(lambda xx, pp: forward(xx, pp, sgrid, vgrid, position_index), xgrid, params)
        gx, gp = pull(ggrid)
        return (jax.tree.map(lambda a, b: a + b, carry, gp), (outs, gx))
    zeros = tuple((jnp.zeros(p.shape, jnp.float32) for p in params))
    totals, (outs, grads) = lax.scan(step, zeros, (xs, gs, segment_ids, valid_mask))
    return (outs.reshape(-1, D), grads.reshape(-1, D)) + tuple(totals)
```

```python
import jax
import jax.numpy as jnp
from jax import lax
from jax.experimental import pallas as pl
from jax.experimental.pallas import tpu as pltpu
from jax.sharding import PartitionSpec as P

HD = 32
GW = 8
WS = 4
WIN = WS * WS
BLOCK = 128
NEG_FILL = -1e30
BF = jnp.bfloat16
F32 = jnp.float32
EXACT = lax.Precision.HIGHEST
VMEM_BYTES = 24 * 1024 * 1024


def dot(left, right):
    return jnp.dot(left, right, preferred_element_type=F32)


def dot_nt(left, right):
    return lax.dot_general(left, right, (((1,), (1,)), ((), ())), preferred_element_type=F32)


def dot_tn(left, right):
    return lax.dot_general(left, right, (((0,), (0,)), ((), ())), preferred_element_type=F32)


def normalize(value):
    centre = value - jnp.mean(value, axis=-1, keepdims=True)
    spread = jnp.mean(centre * centre, axis=-1, keepdims=True)
    inverse = lax.rsqrt(spread + 1e-06)
    return centre * inverse, inverse


def norm_back(grad_out, normed, inverse, gain):
    scaled = grad_out * gain
    first_mean = jnp.mean(scaled, axis=-1, keepdims=True)
    second_mean = jnp.mean(scaled * normed, axis=-1, keepdims=True)
    return inverse * (scaled - first_mean - normed * second_mean)


def row(ref):
    return ref[...].reshape(1, -1)


def iota(shape, axis):
    return lax.broadcasted_iota(jnp.int32, shape, axis)


def place(token):
    return (token // GW) % WS * WS + token % WS


def window(token):
    return token // (GW * WS) * (GW // WS) + token % GW // WS


def head_mask(head):
    return iota((BLOCK, BLOCK), 1) // HD == head


def attend_kernel(
    rel, seg, valid, pidx, x, wq, wk, wv, bq, bv, g1, s1, att, first, q, k, v, probs
):
    tokens = x.shape[0]
    heads = wq.shape[1] // HD
    blocks = tokens // BLOCK
    for b in range(blocks):
        rows = pl.ds(b * BLOCK, BLOCK)
        normed, _ = normalize(x[rows, :].astype(F32))
        first[rows, :] = (normed * row(g1) + row(s1)).astype(BF)
    q[...] = (dot(first[...], wq[...]) + row(bq)).astype(BF)
    k[...] = dot(first[...], wk[...]).astype(BF)
    v[...] = (dot(first[...], wv[...]) + row(bv)).astype(BF)
    spread = (place(iota((BLOCK, WIN), 0)) == iota((BLOCK, WIN), 1)).astype(F32)
    index = pidx[...]
    biases = [jnp.zeros((WIN, WIN), F32) for _ in range(heads)]
    for o in range(rel.shape[0]):
        hit = index == o
        biases = [jnp.where(hit, rel[o, h], biases[h]) for h in range(heads)]
    biases = [
        lax.dot_general(
            jnp.dot(spread, bias, precision=EXACT, preferred_element_type=F32),
            spread,
            (((1,), (1,)), ((), ())),
            precision=EXACT,
            preferred_element_type=F32,
        )
        for bias in biases
    ]
    query_at, key_at = iota((BLOCK, BLOCK), 0), iota((BLOCK, BLOCK), 1)
    near = window(query_at) == window(key_at)
    selfs = query_at == key_at
    factor = HD ** (-0.5)
    for b in range(blocks):
        rows = pl.ds(b * BLOCK, BLOCK)
        seg_keys = jnp.broadcast_to(seg[:, rows].astype(F32), (BLOCK, BLOCK))
        valid_keys = jnp.broadcast_to(valid[:, rows], (BLOCK, BLOCK)) > 0
        allowed = near & (seg_keys == seg_keys.T) & (valid_keys | selfs)
        qb, kb, vb = q[rows, :], k[rows, :], v[rows, :]
        total = jnp.zeros((BLOCK, BLOCK), F32)
        for h in range(heads):
            mine = head_mask(h)
            kh = jnp.where(mine, kb, jnp.zeros_like(kb))
            vh = jnp.where(mine, vb, jnp.zeros_like(vb))
            scores = dot_nt(qb, kh) * factor + biases[h]
            scores = jnp.where(allowed, scores, NEG_FILL)
            expo = jnp.exp(scores - jnp.max(scores, axis=-1, keepdims=True))
            prob = expo * (1.0 / jnp.sum(expo, axis=-1, keepdims=True))
            probs[b * heads + h] = prob
            total = total + dot(prob.astype(BF), vh)
        att[rows, :] = total.astype(BF)


def mlp_kernel(
    spot, x, cot, a0, a1, a2, a3, p0, p1, p2, p3, bo, g2, s2, w1, b1, w2,
    mid, second, hidden, gpre, keep, send, att_all, wo_all,
):
    me = spot[0]
    width = a0.shape[1]
    for j, (a, p) in enumerate(((a0, p0), (a1, p1), (a2, p2), (a3, p3))):
        here = pl.ds(pl.multiple_of((me ^ j) * width, width), width)
        att_all[:, here] = a[...]
        wo_all[here, :] = p[...]
    tokens = x.shape[0]
    half = tokens // 2
    curve = (2.0 / jnp.pi) ** 0.5
    for i in range(2):
        rows = pl.ds(i * half, half)
        value = x[rows, :].astype(F32) + dot(att_all[rows, :], wo_all[...]) + row(bo)
        mid[rows, :] = value
        normed, _ = normalize(value)
        second[rows, :] = (normed * row(g2) + row(s2)).astype(BF)
        pre = dot(second[rows, :], w1[...]) + row(b1)
        square = pre * pre
        bend = jnp.tanh(curve * (pre + 0.044715 * (pre * square)))
        upper = 0.5 * (1.0 + bend)
        hidden[rows, :] = (pre * upper).astype(BF)
        slope = upper + 0.5 * pre * (1.0 - bend * bend) * (curve * (1.0 + 0.134145 * square))
        gpre[rows, :] = (dot_nt(cot[rows, :], w2[...]) * slope).astype(BF)
    core = me % 2
    mine = pl.ds(pl.multiple_of(core * half, half), half)
    other = pl.ds(pl.multiple_of((1 - core) * half, half), half)
    send[...] = dot_nt(gpre[other, :], w1[...]).astype(BF)
    keep[...] = dot_nt(gpre[mine, :], w1[...])


def mlp_grad_kernel(
    spot, cot, second, hidden, gpre, w2, w1_grad, w2_grad, keep, send, small
):
    core = spot[0] % 2
    half = cot.shape[0] // 2
    mine = pl.ds(pl.multiple_of(core * half, half), half)
    other = pl.ds(pl.multiple_of((1 - core) * half, half), half)
    w2_grad[...] = dot_tn(hidden[...], cot[...]).astype(BF)
    w1_grad[...] = dot_tn(second[...], gpre[...]).astype(BF)
    send[...] = dot(hidden[other, :], w2[...]).astype(BF)
    keep[...] = dot(hidden[mine, :], w2[...])
    small[...] = jnp.zeros_like(small)
    small[0:1, :] = jnp.sum(gpre[...].astype(F32), axis=0, keepdims=True)
    small[1:2, :] = jnp.sum(cot[...].astype(F32), axis=0, keepdims=True)


def attend_back_kernel(
    spot, pidx, s2a, s2b, cot, mid, x, g2, att, wo, q, k, v, probs, first, wq, wk, wv,
    gmid, pay, keep, send, small, gsec, gproj, gatt, gq, gk, gv,
):
    core = spot[0] % 2
    tokens = x.shape[0]
    half = tokens // 2
    heads = wq.shape[1] // HD
    blocks = tokens // BLOCK
    mine = pl.ds(pl.multiple_of(core * half, half), half)
    other = pl.ds(pl.multiple_of((1 - core) * half, half), half)
    gsec[mine, :] = s2a[...].astype(F32)
    gsec[other, :] = s2b[...].astype(F32)
    width = x.shape[1]
    gain_sum = jnp.zeros((1, width), F32)
    shift_sum = jnp.zeros((1, width), F32)
    proj_sum = jnp.zeros((1, width), F32)
    for b in range(blocks):
        rows = pl.ds(b * BLOCK, BLOCK)
        grad = gsec[rows, :]
        normed, inverse = normalize(mid[rows, :])
        gain_sum += jnp.sum(grad * normed, axis=0, keepdims=True)
        shift_sum += jnp.sum(grad, axis=0, keepdims=True)
        value = cot[rows, :].astype(F32) + norm_back(grad, normed, inverse, row(g2))
        gmid[rows, :] = value
        proj_sum += jnp.sum(value, axis=0, keepdims=True)
        gproj[rows, :] = value.astype(BF)
    gatt[...] = dot_nt(gproj[...], wo[...]).astype(BF)
    factor = HD ** (-0.5)
    score_sums = [jnp.zeros((BLOCK, BLOCK), F32) for _ in range(heads)]
    for b in range(blocks):
        rows = pl.ds(b * BLOCK, BLOCK)
        qb, kb, vb, gb = q[rows, :], k[rows, :], v[rows, :], gatt[rows, :]
        sum_q = jnp.zeros((BLOCK, BLOCK), F32)
        sum_k = jnp.zeros((BLOCK, BLOCK), F32)
        sum_v = jnp.zeros((BLOCK, BLOCK), F32)
        for h in range(heads):
            own = head_mask(h)
            zero = jnp.zeros_like(qb)
            prob = probs[b * heads + h]
            grad = dot_nt(gb, jnp.where(own, vb, zero))
            sum_v += dot_tn(prob.astype(BF), jnp.where(own, gb, zero))
            inner = jnp.sum(prob * grad, axis=-1, keepdims=True)
            gscore = (prob * (grad - inner)).astype(BF)
            sum_q += dot(gscore, jnp.where(own, kb, zero))
            sum_k += dot_tn(gscore, jnp.where(own, qb, zero))
            score_sums[h] += gscore.astype(F32)
        gq[rows, :] = (factor * sum_q).astype(BF)
        gk[rows, :] = (factor * sum_k).astype(BF)
        gv[rows, :] = sum_v.astype(BF)
    span = wq.shape[1]
    for j, part in enumerate((gq, gk, gv)):
        grads = dot_tn(first[...], part[...]).astype(BF)
        for i in range(width // span):
            pay[j * span:(j + 1) * span, i * span:(i + 1) * span] = grads[i * span:(i + 1) * span]
    pay[3 * span:4 * span, :] = dot_tn(att[...], gproj[...]).astype(BF)
    norm1_gain = jnp.zeros((1, width), F32)
    norm1_shift = jnp.zeros((1, width), F32)
    for part, where in ((0, mine), (1, other)):
        grads = (
            dot_nt(gq[where, :], wq[...])
            + dot_nt(gk[where, :], wk[...])
            + dot_nt(gv[where, :], wv[...])
        )
        normed, _ = normalize(x[where, :].astype(F32))
        norm1_gain += jnp.sum(grads * normed, axis=0, keepdims=True)
        norm1_shift += jnp.sum(grads, axis=0, keepdims=True)
        if part == 0:
            keep[0:half, :] = grads
        else:
            send[0:half, :] = grads.astype(BF)
    tail = keep.shape[0] - half
    which = iota((tail, width), 0)
    sums = jnp.where(which == 0, norm1_gain, jnp.where(which == 1, norm1_shift, 0.0))
    keep[half:, :] = sums
    send[half:, :] = sums.astype(BF)
    at = place(iota((BLOCK, WIN), 0)) == iota((BLOCK, WIN), 1)
    fold = at.astype(F32)
    lanes = heads * WIN
    folded = jnp.zeros((WIN, lanes), F32)
    for h in range(heads):
        lane = iota((BLOCK, lanes), 1)
        lay = ((place(iota((BLOCK, lanes), 0)) == lane % WIN) & (lane // WIN == h)).astype(F32)
        once = lax.dot_general(
            fold, score_sums[h], (((0,), (0,)), ((), ())),
            precision=EXACT, preferred_element_type=F32,
        )
        folded += jnp.dot(once, lay, precision=EXACT, preferred_element_type=F32)
    index = jnp.concatenate([pidx[...]] * heads, axis=1)
    slots = 64
    slot = iota((slots, lanes), 0)
    by_offset = jnp.zeros((slots, lanes), F32)
    for o in range(49):
        total = jnp.sum(jnp.where(index == o, folded, 0.0), axis=0, keepdims=True)
        by_offset = jnp.where(slot == o, total, by_offset)
    pick = (iota((8, lanes), 1) // WIN == iota((8, lanes), 0)).astype(F32)
    offsets = lax.dot_general(
        pick, by_offset, (((1,), (1,)), ((), ())), precision=EXACT, preferred_element_type=F32
    )
    small[...] = jnp.zeros_like(small)
    small[0:1, :] = gain_sum
    small[1:2, :] = shift_sum
    small[2:3, :] = proj_sum
    small[3:4, 0:span] = jnp.sum(gq[...].astype(F32), axis=0, keepdims=True)
    small[3:4, span:2 * span] = jnp.sum(gv[...].astype(F32), axis=0, keepdims=True)
    small[8:16, 0:slots] = offsets


def finish_kernel(spot, s4a, s4b, m4a, m4b, gmid, x, g1, mid, b2, layer_out, input_grad):
    core = spot[0] % 2
    half = x.shape[0] // 2
    for part, (gref, mref) in enumerate(((s4a, m4a), (s4b, m4b))):
        start = core if part == 0 else 1 - core
        where = pl.ds(pl.multiple_of(start * half, half), half)
        normed, inverse = normalize(x[where, :].astype(F32))
        grad = gref[0:half, :].astype(F32)
        input_grad[where, :] = gmid[where, :] + norm_back(grad, normed, inverse, row(g1))
        layer_out[where, :] = mid[where, :] + mref[...].astype(F32) + row(b2)


def call(kernel, outs, args, scalars, scratch=(), flops=0):
    in_specs = [
        pl.BlockSpec(memory_space=pltpu.SMEM if i in scalars else pltpu.VMEM)
        for i in range(len(args))
    ]
    shapes = [jax.ShapeDtypeStruct(shape, dtype) for shape, dtype in outs]
    moved = sum(a.size * a.dtype.itemsize for a in list(args) + shapes)
    return pl.pallas_call(
        kernel,
        out_shape=shapes,
        in_specs=in_specs,
        out_specs=[pl.BlockSpec(memory_space=pltpu.VMEM)] * len(shapes),
        scratch_shapes=[pltpu.VMEM(shape, dtype) for shape, dtype in scratch],
        compiler_params=pltpu.CompilerParams(vmem_limit_bytes=VMEM_BYTES),
        cost_estimate=pl.CostEstimate(flops=flops, bytes_accessed=moved, transcendentals=0),
    )(*args)


def swap(value, axis, bit, size):
    return lax.ppermute(value, axis, [(i, i ^ bit) for i in range(size)])


def shards(
    inputs,
    query_weight,
    key_weight,
    value_weight,
    query_bias,
    value_bias,
    position_bias,
    proj_weight,
    proj_bias,
    norm1_gain,
    norm1_shift,
    norm2_gain,
    norm2_shift,
    up_weight,
    up_bias,
    down_weight,
    down_bias,
    segment_ids,
    valid_mask,
    position_index,
    out_cotangent,
    dp,
    tensor,
):
    tokens, width = inputs.shape
    half = tokens // 2
    span = query_weight.shape[1]
    units = up_weight.shape[1]
    heads = span // HD
    blocks = tokens // BLOCK
    me = lax.axis_index("tensor")
    spot = me.astype(jnp.int32).reshape(1)
    mate = lax.axis_index("dp")
    seg = segment_ids.reshape(1, tokens)
    valid = valid_mask.reshape(1, tokens)

    wo_x = swap(proj_weight, "tensor", 2, tensor)
    wo_c = swap(proj_weight, "tensor", 1, tensor)
    wo_d = swap(wo_x, "tensor", 1, tensor)

    att, first, q, k, v, probs = call(
        attend_kernel,
        [
            ((tokens, span), BF), ((tokens, width), BF), ((tokens, span), BF),
            ((tokens, span), BF), ((tokens, span), BF), ((blocks * heads, BLOCK, BLOCK), F32),
        ],
        [
            position_bias, seg, valid, position_index, inputs, query_weight, key_weight,
            value_weight, query_bias, value_bias, norm1_gain, norm1_shift,
        ],
        (0,),
        flops=2 * tokens * width * 3 * span,
    )
    att_x = swap(att, "tensor", 2, tensor)
    att_c = swap(att, "tensor", 1, tensor)
    att_d = swap(att_x, "tensor", 1, tensor)

    mid, second, hidden, gpre, keep3, send3 = call(
        mlp_kernel,
        [
            ((tokens, width), F32), ((tokens, width), BF), ((tokens, units), BF),
            ((tokens, units), BF), ((half, width), F32), ((half, width), BF),
        ],
        [
            spot, inputs, out_cotangent, att, att_c, att_x, att_d, proj_weight, wo_c, wo_x, wo_d,
            proj_bias, norm2_gain, norm2_shift, up_weight, up_bias, down_weight,
        ],
        (0,),
        scratch=[((tokens, tensor * span), BF), ((tensor * span, width), BF)],
        flops=2 * tokens * width * 4 * units,
    )

    def fold(value, other):
        return (value.astype(F32) + other.astype(F32)).astype(BF)

    pair3 = fold(keep3, swap(send3, "tensor", 1, tensor))
    sum3 = fold(pair3, swap(pair3, "tensor", 2, tensor))
    rest3 = swap(sum3, "tensor", 1, tensor)

    w1_pay, w2_pay, keep2, send2, small_a = call(
        mlp_grad_kernel,
        [
            ((width, units), BF), ((units, width), BF), ((half, width), F32),
            ((half, width), BF), ((8, width), F32),
        ],
        [spot, out_cotangent, second, hidden, gpre, down_weight],
        (0,),
        flops=2 * tokens * width * 3 * units,
    )

    gmid, pay, keep4, send4, small_b = call(
        attend_back_kernel,
        [
            ((tokens, width), F32), ((4 * span, width), BF), ((half + 16, width), F32),
            ((half + 16, width), BF), ((16, width), F32),
        ],
        [
            spot, position_index, sum3, rest3, out_cotangent, mid, inputs, norm2_gain, att,
            proj_weight, q, k, v, probs, first, query_weight, key_weight, value_weight,
        ],
        (0,),
        scratch=[
            ((tokens, width), F32), ((tokens, width), BF), ((tokens, span), BF),
            ((tokens, span), BF), ((tokens, span), BF), ((tokens, span), BF),
        ],
        flops=2 * tokens * width * 8 * span,
    )

    keep4 = jnp.concatenate([keep4, keep2])
    send4 = jnp.concatenate([send4, send2])
    pair4 = fold(keep4, swap(send4, "tensor", 1, tensor))
    sum4 = fold(pair4, swap(pair4, "tensor", 2, tensor))
    rest4 = swap(sum4, "tensor", 1, tensor)

    bits = [1 << i for i in range(dp.bit_length() - 1)]

    def scatter(value):
        for bit in bits:
            part = value.shape[0] // 2
            flag = (mate // bit) % 2
            own = lax.dynamic_slice_in_dim(value, flag * part, part)
            away = lax.dynamic_slice_in_dim(value, (1 - flag) * part, part)
            value = fold(own, swap(away, "dp", bit, dp))
        return value

    def join(bit, own, other):
        flag = (mate // bit) % 2
        return jnp.where(
            flag == 0, jnp.concatenate([own, other]), jnp.concatenate([other, own])
        )

    def gather(value, extra=None):
        for bit in reversed(bits):
            if extra is None:
                value = join(bit, value, swap(value, "dp", bit, dp))
            else:
                rows = value.shape[0]
                come = swap(jnp.concatenate([value, extra]), "dp", bit, dp)
                value = join(bit, value, come[:rows])
                extra = fold(extra, come[rows:])
        return value if extra is None else (value, extra)

    mlp_total = gather(scatter(jnp.concatenate([w1_pay, w2_pay])))
    w1_total = mlp_total[:width].astype(F32)
    w2_total = mlp_total[width:].astype(F32)

    small = jnp.concatenate([small_a.astype(BF), small_b.astype(BF), sum4[half:half + 8]])
    att_total, small = gather(scatter(pay), small)
    att_total = att_total.astype(F32)
    small = small.astype(F32)

    def unfold(block):
        return jnp.concatenate([block[:, i * span:(i + 1) * span] for i in range(width // span)])

    wq_total = unfold(att_total[:span])
    wk_total = unfold(att_total[span:2 * span])
    wv_total = unfold(att_total[2 * span:3 * span])
    wo_total = att_total[3 * span:]
    b1_total, b2_total = small[0], small[1]
    g2_total, s2_total, bo_total = small[8], small[9], small[10]
    bq_total, bv_total = small[11, :span], small[11, span:2 * span]
    rel_total = small[16:16 + heads, :position_bias.shape[0]].T
    g1_total, s1_total = small[24], small[25]

    layer_out, input_grad = call(
        finish_kernel,
        [((tokens, width), F32), ((tokens, width), F32)],
        [
            spot, sum4[:half], rest4[:half], sum4[half + 16:], rest4[half + 16:], gmid, inputs,
            norm1_gain, mid, down_bias,
        ],
        (0,),
        flops=tokens * width,
    )
    return (
        layer_out,
        input_grad,
        wq_total,
        wk_total,
        wv_total,
        bq_total,
        bv_total,
        rel_total,
        wo_total,
        bo_total,
        g1_total,
        s1_total,
        g2_total,
        s2_total,
        w1_total,
        b1_total,
        w2_total,
        b2_total,
    )


def solution(mesh):
    dp, tensor = mesh.shape["dp"], mesh.shape["tensor"]

    def body(*args):
        return shards(*args, dp=dp, tensor=tensor)

    column, line, whole = P(None, "tensor"), P("tensor"), P()
    return jax.shard_map(
        body,
        mesh=mesh,
        in_specs=(
            P("dp", None),
            column,
            column,
            column,
            line,
            line,
            column,
            P("tensor", None),
            whole,
            whole,
            whole,
            whole,
            whole,
            column,
            line,
            P("tensor", None),
            whole,
            P("dp", None),
            P("dp", None),
            whole,
            P("dp", None),
        ),
        out_specs=(
            P("dp", None),
            P("dp", None),
            column,
            column,
            column,
            line,
            line,
            column,
            P("tensor", None),
            whole,
            whole,
            whole,
            whole,
            whole,
            column,
            line,
            P("tensor", None),
            whole,
        ),
        check_vma=False,
    )
```

```python
import jax
import jax.numpy as jnp
from jax import lax
from jax.experimental import pallas as pl
from jax.experimental.pallas import tpu as pltpu
from jax.sharding import PartitionSpec as P

HD = 32
GW = 8
WS = 4
WIN = WS * WS
BLOCK = 128
NEG_FILL = -1e30
BF = jnp.bfloat16
F32 = jnp.float32
EXACT = lax.Precision.HIGHEST
VMEM_BYTES = 24 * 1024 * 1024
ROWS = 16


def dot(left, right):
    return jnp.dot(left, right, preferred_element_type=F32)


def dot_nt(left, right):
    return lax.dot_general(left, right, (((1,), (1,)), ((), ())), preferred_element_type=F32)


def dot_tn(left, right):
    return lax.dot_general(left, right, (((0,), (0,)), ((), ())), preferred_element_type=F32)


def normalize(value):
    centre = value - jnp.mean(value, axis=-1, keepdims=True)
    spread = jnp.mean(centre * centre, axis=-1, keepdims=True)
    inverse = lax.rsqrt(spread + 1e-06)
    return centre * inverse, inverse


def norm_back(grad_out, normed, inverse, gain):
    scaled = grad_out * gain
    first_mean = jnp.mean(scaled, axis=-1, keepdims=True)
    second_mean = jnp.mean(scaled * normed, axis=-1, keepdims=True)
    return inverse * (scaled - first_mean - normed * second_mean)


def row(ref):
    return ref[...].reshape(1, -1)


def iota(shape, axis):
    return lax.broadcasted_iota(jnp.int32, shape, axis)


def place(token):
    return (token // GW) % WS * WS + token % WS


def window(token):
    return token // (GW * WS) * (GW // WS) + token % GW // WS


def head_mask(head):
    return iota((BLOCK, BLOCK), 1) // HD == head


class Loaded:
    def __init__(self, source, buffer, sem):
        self.buffer, self.shape, self.dtype = buffer, source.shape, source.dtype
        self.copy = pltpu.make_async_copy(source, buffer, sem)
        self.copy.start()

    def wait(self):
        if self.copy is not None:
            self.copy.wait()
            self.copy = None

    def __getitem__(self, at):
        self.wait()
        return self.buffer[at]


class Stored:
    def __init__(self, buffer, target, sem):
        self.buffer, self.shape, self.dtype = buffer, target.shape, target.dtype
        self.copy, self.sent = pltpu.make_async_copy(buffer, target, sem), False

    def __getitem__(self, at):
        return self.buffer[at]

    def __setitem__(self, at, value):
        self.buffer[at] = value

    def send(self):
        if not self.sent:
            self.copy.start()
            self.sent = True


def send_off(ref):
    if isinstance(ref, Stored):
        ref.send()


def call(kernel, outs, args, scratch=(), flops=0, exports=()):
    spaces = {"smem": pltpu.SMEM, "vmem": pltpu.VMEM, "hbm": pltpu.HBM, "hsmem": pltpu.HBM}
    plain = len(outs)
    outs = list(outs) + [(args[i][0].shape, args[i][0].dtype, "vmem") for i in exports]
    loads = [i for i, (_, where) in enumerate(args) if where[0] == "h"]
    stores = [i for i, (_, _, where) in enumerate(outs) if where == "hbm"]
    shapes = [jax.ShapeDtypeStruct(shape, dtype) for shape, dtype, _ in outs]
    pinned = [spaces[where](shape, dtype) for shape, dtype, where in outs]
    operands = [
        pltpu.with_memory_space_constraint(a, pltpu.HBM) if where[0] == "h" else a
        for a, where in args
    ]
    buffers = []
    for i in loads:
        if i in exports:
            continue
        array, where = args[i]
        space = pltpu.SMEM if where == "hsmem" else pltpu.VMEM
        buffers.append(space(array.shape, array.dtype))
    buffers += [pltpu.VMEM(outs[i][0], outs[i][1]) for i in stores]
    sems = [pltpu.SemaphoreType.DMA] * (len(loads) + len(stores))

    def body(*refs):
        refs = list(refs)
        ins, rest = refs[:len(args)], refs[len(args):]
        results, rest = rest[:len(outs)], rest[len(outs):]
        own, rest = rest[:len(scratch)], rest[len(scratch):]
        holds, marks = list(rest[:len(buffers)]), list(rest[len(buffers):])
        given = dict(zip(exports, results[plain:]))
        for i in loads:
            hold = given[i] if i in given else holds.pop(0)
            ins[i] = Loaded(ins[i], hold, marks.pop(0))
        for i in stores:
            results[i] = Stored(holds.pop(0), results[i], marks.pop(0))
        kernel(*ins, *results[:plain], *own)
        for i in loads:
            ins[i].wait()
        for i in stores:
            results[i].send()
        for i in stores:
            results[i].copy.wait()

    moved = sum(a.size * a.dtype.itemsize for a in [a for a, _ in args] + shapes)
    return pl.pallas_call(
        body,
        name=kernel.__name__,
        out_shape=pinned,
        in_specs=[pl.BlockSpec(memory_space=spaces[where]) for _, where in args],
        out_specs=[pl.BlockSpec(memory_space=spaces[where]) for _, _, where in outs],
        scratch_shapes=[pltpu.VMEM(shape, dtype) for shape, dtype in scratch] + buffers + sems,
        compiler_params=pltpu.CompilerParams(vmem_limit_bytes=VMEM_BYTES),
        cost_estimate=pl.CostEstimate(flops=flops, bytes_accessed=moved, transcendentals=0),
    )(*operands)


def attend_kernel(
    spot, x, g1, s1, rel, pidx, wq, wk, wv, bq, bv, seg, valid, wo, bo, g2, s2, w1, b1, cot, w2, b2,
    att, first, q, k, v, probs
):
    tokens = x.shape[0]
    heads = wq.shape[1] // HD
    blocks = tokens // BLOCK
    for b in range(blocks):
        rows = pl.ds(b * BLOCK, BLOCK)
        normed, _ = normalize(x[rows, :].astype(F32))
        first[rows, :] = (normed * row(g1) + row(s1)).astype(BF)
    send_off(first)
    q[...] = (dot(first[...], wq[...]) + row(bq)).astype(BF)
    send_off(q)
    k[...] = dot(first[...], wk[...]).astype(BF)
    send_off(k)
    v[...] = (dot(first[...], wv[...]) + row(bv)).astype(BF)
    send_off(v)
    spread = (place(iota((BLOCK, WIN), 0)) == iota((BLOCK, WIN), 1)).astype(F32)
    index = pidx[...]
    biases = [jnp.zeros((WIN, WIN), F32) for _ in range(heads)]
    for o in range(rel.shape[1]):
        hit = index == o
        biases = [jnp.where(hit, rel[h, o], biases[h]) for h in range(heads)]
    biases = [
        lax.dot_general(
            jnp.dot(spread, bias, precision=EXACT, preferred_element_type=F32),
            spread,
            (((1,), (1,)), ((), ())),
            precision=EXACT,
            preferred_element_type=F32,
        )
        for bias in biases
    ]
    query_at, key_at = iota((BLOCK, BLOCK), 0), iota((BLOCK, BLOCK), 1)
    near = window(query_at) == window(key_at)
    selfs = query_at == key_at
    factor = HD ** (-0.5)
    for b in range(blocks):
        rows = pl.ds(b * BLOCK, BLOCK)
        seg_keys = jnp.broadcast_to(seg[:, rows].astype(F32), (BLOCK, BLOCK))
        valid_keys = jnp.broadcast_to(valid[:, rows], (BLOCK, BLOCK)) > 0
        allowed = near & (seg_keys == seg_keys.T) & (valid_keys | selfs)
        qb, kb, vb = q[rows, :], k[rows, :], v[rows, :]
        total = jnp.zeros((BLOCK, BLOCK), F32)
        for h in range(heads):
            mine = head_mask(h)
            kh = jnp.where(mine, kb, jnp.zeros_like(kb))
            vh = jnp.where(mine, vb, jnp.zeros_like(vb))
            scores = dot_nt(qb, kh) * factor + biases[h]
            scores = jnp.where(allowed, scores, NEG_FILL)
            expo = jnp.exp(scores - jnp.max(scores, axis=-1, keepdims=True))
            prob = expo * (1.0 / jnp.sum(expo, axis=-1, keepdims=True))
            probs[b * heads + h] = prob
            total = total + dot(prob.astype(BF), vh)
        att[rows, :] = total.astype(BF)
    send_off(probs)


def mlp_kernel(
    spot, a0, a1, a2, a3, p0, p1, p2, p3, x, bo, g2, s2, w1, b1, cot, w2,
    mid, second, hidden, gpre, keep, send, att_all, wo_all,
):
    me = spot[0]
    width = a0.shape[1]
    for j, (a, p) in enumerate(((a0, p0), (a1, p1), (a2, p2), (a3, p3))):
        here = pl.ds(pl.multiple_of((me ^ j) * width, width), width)
        att_all[:, here] = a[...]
        wo_all[here, :] = p[...]
    tokens = x.shape[0]
    half = tokens // 2
    curve = (2.0 / jnp.pi) ** 0.5
    for i in range(2):
        rows = pl.ds(i * half, half)
        value = x[rows, :].astype(F32) + dot(att_all[rows, :], wo_all[...]) + row(bo)
        mid[rows, :] = value
        normed, _ = normalize(value)
        second[rows, :] = (normed * row(g2) + row(s2)).astype(BF)
        pre = dot(second[rows, :], w1[...]) + row(b1)
        square = pre * pre
        bend = jnp.tanh(curve * (pre + 0.044715 * (pre * square)))
        upper = 0.5 * (1.0 + bend)
        hidden[rows, :] = (pre * upper).astype(BF)
        slope = upper + 0.5 * pre * (1.0 - bend * bend) * (curve * (1.0 + 0.134145 * square))
        gpre[rows, :] = (dot_nt(cot[rows, :], w2[...]) * slope).astype(BF)
    send_off(mid)
    core = me % 2
    mine = pl.ds(pl.multiple_of(core * half, half), half)
    other = pl.ds(pl.multiple_of((1 - core) * half, half), half)
    send[...] = dot_nt(gpre[other, :], w1[...]).astype(BF)
    keep[...] = dot_nt(gpre[mine, :], w1[...])


def mlp_grad_kernel(
    spot, second, hidden, gpre, cot, w2, own, away, keep, send, small, grads
):
    core, side = spot[0] % 2, spot[1] % 2
    half = cot.shape[0] // 2
    mine = pl.ds(pl.multiple_of(core * half, half), half)
    other = pl.ds(pl.multiple_of((1 - core) * half, half), half)
    grads[0] = dot_tn(second[...], gpre[...]).astype(BF)
    grads[1] = dot_tn(hidden[...], cot[...]).astype(BF)
    own[...] = grads[side]
    away[...] = grads[1 - side]
    send[...] = dot(hidden[other, :], w2[...]).astype(BF)
    send_off(send)
    keep[...] = dot(hidden[mine, :], w2[...]).astype(BF)
    send_off(keep)
    which = iota(small.shape, 0)
    first = jnp.sum(gpre[...].astype(F32), axis=0, keepdims=True)
    later = jnp.sum(cot[...].astype(F32), axis=0, keepdims=True)
    small[...] = jnp.where(which == 0, first, jnp.where(which == 1, later, 0.0)).astype(BF)


def attend_back_kernel(
    spot, s2a, s2b, keep2, send2, mid, cot, g2, wo, v, probs, k, q, first, att, wq, wk, wv, x, pidx,
    gmid, own, away, keep, send, small, gsec, gproj, gatt, gq, gk, gv, pay, sums,
):
    core, side = spot[0] % 2, spot[1] % 2
    tokens = x.shape[0]
    half = tokens // 2
    heads = wq.shape[1] // HD
    blocks = tokens // BLOCK
    mine = pl.ds(pl.multiple_of(core * half, half), half)
    other = pl.ds(pl.multiple_of((1 - core) * half, half), half)
    gsec[mine, :] = s2a[...].astype(F32)
    gsec[other, :] = s2b[...].astype(F32)
    width = x.shape[1]
    gain_sum = jnp.zeros((1, width), F32)
    shift_sum = jnp.zeros((1, width), F32)
    proj_sum = jnp.zeros((1, width), F32)
    for b in range(blocks):
        rows = pl.ds(b * BLOCK, BLOCK)
        grad = gsec[rows, :]
        normed, inverse = normalize(mid[rows, :])
        gain_sum += jnp.sum(grad * normed, axis=0, keepdims=True)
        shift_sum += jnp.sum(grad, axis=0, keepdims=True)
        value = cot[rows, :].astype(F32) + norm_back(grad, normed, inverse, row(g2))
        gmid[rows, :] = value
        proj_sum += jnp.sum(value, axis=0, keepdims=True)
        gproj[rows, :] = value.astype(BF)
    send_off(gmid)
    gatt[...] = dot_nt(gproj[...], wo[...]).astype(BF)
    factor = HD ** (-0.5)
    score_sums = [jnp.zeros((BLOCK, BLOCK), F32) for _ in range(heads)]
    for b in range(blocks):
        rows = pl.ds(b * BLOCK, BLOCK)
        qb, kb, vb, gb = q[rows, :], k[rows, :], v[rows, :], gatt[rows, :]
        sum_q = jnp.zeros((BLOCK, BLOCK), F32)
        sum_k = jnp.zeros((BLOCK, BLOCK), F32)
        sum_v = jnp.zeros((BLOCK, BLOCK), F32)
        for h in range(heads):
            lane = head_mask(h)
            zero = jnp.zeros_like(qb)
            prob = probs[b * heads + h]
            grad = dot_nt(gb, jnp.where(lane, vb, zero))
            sum_v += dot_tn(prob.astype(BF), jnp.where(lane, gb, zero))
            inner = jnp.sum(prob * grad, axis=-1, keepdims=True)
            gscore = (prob * (grad - inner)).astype(BF)
            sum_q += dot(gscore, jnp.where(lane, kb, zero))
            sum_k += dot_tn(gscore, jnp.where(lane, qb, zero))
            score_sums[h] += gscore.astype(F32)
        gq[rows, :] = (factor * sum_q).astype(BF)
        gk[rows, :] = (factor * sum_k).astype(BF)
        gv[rows, :] = sum_v.astype(BF)
    span = wq.shape[1]
    for j, part in enumerate((gq, gk, gv)):
        grads = dot_tn(first[...], part[...]).astype(BF)
        for i in range(width // span):
            pay[j * span:(j + 1) * span, i * span:(i + 1) * span] = grads[i * span:(i + 1) * span]
    pay[3 * span:4 * span, :] = dot_tn(att[...], gproj[...]).astype(BF)
    part = 2 * span
    own[...] = pay[pl.ds(pl.multiple_of(side * part, part), part), :]
    away[...] = pay[pl.ds(pl.multiple_of((1 - side) * part, part), part), :]
    norm1_gain = jnp.zeros((1, width), F32)
    norm1_shift = jnp.zeros((1, width), F32)
    for part, where in ((0, mine), (1, other)):
        grads = (
            dot_nt(gq[where, :], wq[...])
            + dot_nt(gk[where, :], wk[...])
            + dot_nt(gv[where, :], wv[...])
        )
        normed, _ = normalize(x[where, :].astype(F32))
        norm1_gain += jnp.sum(grads * normed, axis=0, keepdims=True)
        norm1_shift += jnp.sum(grads, axis=0, keepdims=True)
        if part == 0:
            keep[0:half, :] = grads.astype(BF)
        else:
            send[0:half, :] = grads.astype(BF)
    which = iota((ROWS, width), 0)
    pair = jnp.where(which == 0, norm1_gain, jnp.where(which == 1, norm1_shift, 0.0)).astype(BF)
    keep[half:half + ROWS, :] = pair
    send[half:half + ROWS, :] = pair
    keep[half + ROWS:, :] = keep2[...]
    send[half + ROWS:, :] = send2[...]
    at = place(iota((BLOCK, WIN), 0)) == iota((BLOCK, WIN), 1)
    fold = at.astype(F32)
    lanes = heads * WIN
    folded = jnp.zeros((WIN, lanes), F32)
    for h in range(heads):
        lane = iota((BLOCK, lanes), 1)
        lay = ((place(iota((BLOCK, lanes), 0)) == lane % WIN) & (lane // WIN == h)).astype(F32)
        once = lax.dot_general(
            fold, score_sums[h], (((0,), (0,)), ((), ())),
            precision=EXACT, preferred_element_type=F32,
        )
        folded += jnp.dot(once, lay, precision=EXACT, preferred_element_type=F32)
    index = jnp.concatenate([pidx[...]] * heads, axis=1)
    slots = 64
    slot = iota((slots, lanes), 0)
    by_offset = jnp.zeros((slots, lanes), F32)
    for o in range(49):
        total = jnp.sum(jnp.where(index == o, folded, 0.0), axis=0, keepdims=True)
        by_offset = jnp.where(slot == o, total, by_offset)
    pick = (iota((8, lanes), 1) // WIN == iota((8, lanes), 0)).astype(F32)
    offsets = lax.dot_general(
        pick, by_offset, (((1,), (1,)), ((), ())), precision=EXACT, preferred_element_type=F32
    )
    sums[...] = jnp.zeros_like(sums)
    sums[0:1, :] = gain_sum
    sums[1:2, :] = shift_sum
    sums[2:3, :] = proj_sum
    sums[3:4, 0:span] = jnp.sum(gq[...].astype(F32), axis=0, keepdims=True)
    sums[3:4, span:2 * span] = jnp.sum(gv[...].astype(F32), axis=0, keepdims=True)
    sums[8:16, 0:slots] = offsets
    small[...] = sums[...].astype(BF)


def finish_kernel(spot, s4, r4, gmid, x, g1, mid, b2, layer_out, input_grad):
    core = spot[0] % 2
    half = x.shape[0] // 2
    for part, ref in enumerate((s4, r4)):
        start = core if part == 0 else 1 - core
        where = pl.ds(pl.multiple_of(start * half, half), half)
        normed, inverse = normalize(x[where, :].astype(F32))
        grad = ref[0:half, :].astype(F32)
        input_grad[where, :] = gmid[where, :] + norm_back(grad, normed, inverse, row(g1))
        mlp = ref[half + ROWS:, :].astype(F32)
        layer_out[where, :] = mid[where, :] + mlp + row(b2)


def widen_kernel(spot, near, far, first, second):
    side = spot[1] % 2
    @pl.when(side == 0)
    def _():
        first[...] = near[...].astype(F32)
        second[...] = far[...].astype(F32)
    @pl.when(side == 1)
    def _():
        first[...] = far[...].astype(F32)
        second[...] = near[...].astype(F32)


def unpack_kernel(
    spot, near, far, small, wq, wk, wv, wo, b1, b2, g2, s2, bo, bq, bv, rel, g1, s1, both
):
    side = spot[1] % 2
    part = near.shape[0]
    span = part // 2
    width = near.shape[1]
    both[pl.ds(pl.multiple_of(side * part, part), part), :] = near[...]
    both[pl.ds(pl.multiple_of((1 - side) * part, part), part), :] = far[0:part, :]
    for j, ref in enumerate((wq, wk, wv)):
        for i in range(width // span):
            block = both[j * span:(j + 1) * span, i * span:(i + 1) * span]
            ref[i * span:(i + 1) * span, :] = block.astype(F32)
        send_off(ref)
    wo[...] = both[3 * span:, :].astype(F32)
    send_off(wo)
    sums = small[...].astype(F32) + far[part:, :].astype(F32)
    for at, ref in ((0, b1), (1, b2), (8, g2), (9, s2), (10, bo), (24, g1), (25, s1)):
        ref[...] = sums[at].astype(BF).astype(F32)
    bq[...] = sums[11, :span].astype(BF).astype(F32)
    bv[...] = sums[11, span:2 * span].astype(BF).astype(F32)
    rel[...] = sums[16:16 + rel.shape[0], :rel.shape[1]].astype(BF).astype(F32)


def swap(value, axis, bit, size):
    return lax.ppermute(value, axis, [(i, i ^ bit) for i in range(size)])


def shards(
    inputs,
    query_weight,
    key_weight,
    value_weight,
    query_bias,
    value_bias,
    position_bias,
    proj_weight,
    proj_bias,
    norm1_gain,
    norm1_shift,
    norm2_gain,
    norm2_shift,
    up_weight,
    up_bias,
    down_weight,
    down_bias,
    segment_ids,
    valid_mask,
    position_index,
    out_cotangent,
    dp,
    tensor,
):
    tokens, width = inputs.shape
    half = tokens // 2
    span = query_weight.shape[1]
    units = up_weight.shape[1]
    heads = span // HD
    blocks = tokens // BLOCK
    me = lax.axis_index("tensor")
    mate = lax.axis_index("dp")
    bits = [1 << i for i in range(dp.bit_length() - 1)]
    flags = [(mate >> i) & 1 for i in range(len(bits))]
    lower = [flag == 0 for flag in flags]
    sizes = [(width >> (i + 1)) * n for i in range(len(bits)) for n in (1, 2)]
    starts = {
        (i, size): (flags[i] * size).astype(jnp.uint32) for i in range(len(bits)) for size in sizes
    }
    stops = {
        at: ((1 - flags[at[0]]) * at[1]).astype(jnp.uint32) for at in starts
    }
    spot = jnp.stack(
        [me, mate]
        + flags
        + [flag.astype(jnp.int32) for flag in lower]
        + [at.astype(jnp.int32) for at in list(starts.values()) + list(stops.values())]
    )
    seg = segment_ids.reshape(1, tokens)
    valid = valid_mask.reshape(1, tokens)
    wide = (tokens, width)
    narrow = (tokens, span)

    wo_x = swap(proj_weight, "tensor", 2, tensor)
    wo_c = swap(proj_weight, "tensor", 1, tensor)
    wo_d = swap(wo_x, "tensor", 1, tensor)

    (
        att, first, q, k, v, probs, x, norm1_gain, norm1_shift, position_index, query_weight,
        key_weight, value_weight, proj_weight, proj_bias, norm2_gain, norm2_shift, up_weight,
        up_bias, out_cotangent, down_weight, down_bias,
    ) = call(
        attend_kernel,
        [
            (narrow, BF, "vmem"), (wide, BF, "vmem"), (narrow, BF, "vmem"), (narrow, BF, "vmem"),
            (narrow, BF, "vmem"), ((blocks * heads, BLOCK, BLOCK), F32, "vmem"),
        ],
        [
            (spot, "smem"), (inputs, "hbm"), (norm1_gain, "hbm"), (norm1_shift, "hbm"),
            (position_bias.T, "hsmem"), (position_index, "hbm"), (query_weight, "hbm"),
            (key_weight, "hbm"), (value_weight, "hbm"), (query_bias, "hbm"), (value_bias, "hbm"),
            (seg, "hbm"), (valid, "hbm"), (proj_weight, "hbm"), (proj_bias, "hbm"),
            (norm2_gain, "hbm"), (norm2_shift, "hbm"), (up_weight, "hbm"), (up_bias, "hbm"),
            (out_cotangent, "hbm"), (down_weight, "hbm"), (down_bias, "hbm"),
        ],
        exports=(1, 2, 3, 5, 6, 7, 8, 13, 14, 15, 16, 17, 18, 19, 20, 21),
        flops=5 * 10 ** 9,
    )
    inputs = x
    att_x = swap(att, "tensor", 2, tensor)
    att_c = swap(att, "tensor", 1, tensor)
    att_d = swap(att_x, "tensor", 1, tensor)

    mid, second, hidden, gpre, keep3, send3 = call(
        mlp_kernel,
        [
            (wide, F32, "vmem"), (wide, BF, "vmem"), ((tokens, units), BF, "vmem"),
            ((tokens, units), BF, "vmem"), ((half, width), F32, "vmem"), ((half, width), BF, "vmem"),
        ],
        [
            (spot, "smem"), (att, "vmem"), (att_c, "vmem"), (att_x, "vmem"), (att_d, "vmem"),
            (proj_weight, "vmem"), (wo_c, "vmem"), (wo_x, "vmem"), (wo_d, "vmem"),
            (inputs, "vmem"), (proj_bias, "vmem"), (norm2_gain, "vmem"), (norm2_shift, "vmem"),
            (up_weight, "vmem"), (up_bias, "vmem"), (out_cotangent, "vmem"), (down_weight, "vmem"),
        ],
        scratch=[((tokens, tensor * span), BF), ((tensor * span, width), BF)],
        flops=2 * tokens * width * 4 * units,
    )

    def fold(value, other):
        return (value.astype(F32) + other.astype(F32)).astype(BF)

    pair3 = fold(keep3, swap(send3, "tensor", 1, tensor))
    sum3 = fold(pair3, swap(pair3, "tensor", 2, tensor))
    rest3 = swap(sum3, "tensor", 1, tensor)

    mlp_own, mlp_away, keep2, send2, small_a = call(
        mlp_grad_kernel,
        [
            ((width, units), BF, "vmem"), ((units, width), BF, "vmem"), ((half, width), BF, "vmem"),
            ((half, width), BF, "vmem"), ((8, width), BF, "vmem"),
        ],
        [
            (spot, "smem"), (second, "vmem"), (hidden, "vmem"), (gpre, "vmem"),
            (out_cotangent, "vmem"), (down_weight, "vmem"),
        ],
        scratch=[((2, width, units), BF)],
        flops=2 * tokens * width * 3 * units,
    )

    merged = half + ROWS + half
    gmid, att_own, att_away, keep4, send4, small_b = call(
        attend_back_kernel,
        [
            (wide, F32, "vmem"), ((2 * span, width), BF, "vmem"), ((2 * span, width), BF, "vmem"),
            ((merged, width), BF, "vmem"), ((merged, width), BF, "vmem"), ((16, width), BF, "vmem"),
        ],
        [
            (spot, "smem"), (sum3, "vmem"), (rest3, "vmem"), (keep2, "vmem"), (send2, "vmem"),
            (mid, "vmem"), (out_cotangent, "vmem"), (norm2_gain, "vmem"), (proj_weight, "vmem"),
            (v, "vmem"), (probs, "vmem"), (k, "vmem"), (q, "vmem"), (first, "vmem"), (att, "vmem"),
            (query_weight, "vmem"), (key_weight, "vmem"), (value_weight, "vmem"), (inputs, "vmem"),
            (position_index, "vmem"),
        ],
        scratch=[
            (wide, F32), (wide, BF), (narrow, BF), (narrow, BF), (narrow, BF), (narrow, BF),
            ((4 * span, width), BF), ((16, width), F32),
        ],
        flops=2 * tokens * width * 8 * span,
    )

    pair4 = fold(keep4, swap(send4, "tensor", 1, tensor))
    sum4 = fold(pair4, swap(pair4, "tensor", 2, tensor))
    rest4 = swap(sum4, "tensor", 1, tensor)

    left = jnp.uint32(0)

    def scatter(own, away):
        value = fold(own, swap(away, "dp", bits[0], dp))
        for i, bit in enumerate(bits[1:], 1):
            part = value.shape[0] // 2
            own = lax.dynamic_slice(value, (starts[i, part], left), (part, width))
            away = lax.dynamic_slice(value, (stops[i, part], left), (part, width))
            value = fold(own, swap(away, "dp", bit, dp))
        return value

    def join(i, own, other):
        return jnp.where(
            lower[i], jnp.concatenate([own, other]), jnp.concatenate([other, own])
        )

    def gather(value):
        for i in reversed(range(1, len(bits))):
            value = join(i, value, swap(value, "dp", bits[i], dp))
        return value, swap(value, "dp", bits[0], dp)

    def gather_with(value, extra):
        for i in reversed(range(1, len(bits))):
            rows = value.shape[0]
            come = swap(jnp.concatenate([value, extra]), "dp", bits[i], dp)
            value = join(i, value, come[:rows])
            extra = fold(extra, come[rows:])
        return value, extra, swap(jnp.concatenate([value, extra]), "dp", bits[0], dp)

    near, far = gather(scatter(mlp_own, mlp_away))
    w1_total, w2_total = call(
        widen_kernel,
        [((width, units), F32, "hbm"), ((units, width), F32, "hbm")],
        [(spot, "smem"), (near, "vmem"), (far, "vmem")],
    )

    small = jnp.concatenate([small_a, small_b, sum4[half:half + 8]])
    near, small, far = gather_with(scatter(att_own, att_away), small)
    vector, short = ((width,), F32, "hbm"), ((span,), F32, "hbm")
    (
        wq_total, wk_total, wv_total, wo_total, b1_total, b2_total, g2_total, s2_total, bo_total,
        bq_total, bv_total, rel_total, g1_total, s1_total,
    ) = call(
        unpack_kernel,
        [
            ((width, span), F32, "hbm"), ((width, span), F32, "hbm"), ((width, span), F32, "hbm"),
            ((span, width), F32, "hbm"), vector, vector, vector, vector, vector, short, short,
            ((heads, position_bias.shape[0]), F32, "hbm"), vector, vector,
        ],
        [(spot, "smem"), (near, "vmem"), (far, "vmem"), (small, "vmem")],
        scratch=[((4 * span, width), BF)],
    )
    rel_total = rel_total.T

    layer_out, input_grad = call(
        finish_kernel,
        [(wide, F32, "hbm"), (wide, F32, "hbm")],
        [
            (spot, "smem"), (sum4, "vmem"), (rest4, "vmem"), (gmid, "vmem"), (inputs, "vmem"),
            (norm1_gain, "vmem"), (mid, "vmem"), (down_bias, "vmem"),
        ],
        flops=tokens * width,
    )
    return (
        layer_out,
        input_grad,
        wq_total,
        wk_total,
        wv_total,
        bq_total,
        bv_total,
        rel_total,
        wo_total,
        bo_total,
        g1_total,
        s1_total,
        g2_total,
        s2_total,
        w1_total,
        b1_total,
        w2_total,
        b2_total,
    )


def solution(mesh):
    dp, tensor = mesh.shape["dp"], mesh.shape["tensor"]

    def body(*args):
        return shards(*args, dp=dp, tensor=tensor)

    column, line, whole = P(None, "tensor"), P("tensor"), P()
    return jax.shard_map(
        body,
        mesh=mesh,
        in_specs=(
            P("dp", None),
            column,
            column,
            column,
            line,
            line,
            column,
            P("tensor", None),
            whole,
            whole,
            whole,
            whole,
            whole,
            column,
            line,
            P("tensor", None),
            whole,
            P("dp", None),
            P("dp", None),
            whole,
            P("dp", None),
        ),
        out_specs=(
            P("dp", None),
            P("dp", None),
            column,
            column,
            column,
            line,
            line,
            column,
            P("tensor", None),
            whole,
            whole,
            whole,
            whole,
            whole,
            column,
            line,
            P("tensor", None),
            whole,
        ),
        check_vma=False,
    )
```

```python
import jax
import jax.numpy as jnp
from jax import lax
from jax.experimental import pallas as pl
from jax.experimental.pallas import tpu as pltpu
from jax.sharding import PartitionSpec as P

HD = 32
GW = 8
WS = 4
WIN = WS * WS
BLOCK = 128
NEG_FILL = -1e30
BF = jnp.bfloat16
F32 = jnp.float32
EXACT = lax.Precision.HIGHEST
VMEM_BYTES = 24 * 1024 * 1024
ROWS = 16


def dot(left, right):
    return jnp.dot(left, right, preferred_element_type=F32)


def dot_nt(left, right):
    return lax.dot_general(left, right, (((1,), (1,)), ((), ())), preferred_element_type=F32)


def dot_tn(left, right):
    return lax.dot_general(left, right, (((0,), (0,)), ((), ())), preferred_element_type=F32)


def exact_nt(left, right):
    return lax.dot_general(
        left, right, (((1,), (1,)), ((), ())), precision=EXACT, preferred_element_type=F32
    )


def normalize(value):
    centre = value - jnp.mean(value, axis=-1, keepdims=True)
    spread = jnp.mean(centre * centre, axis=-1, keepdims=True)
    inverse = lax.rsqrt(spread + 1e-06)
    return centre * inverse, inverse


def norm_back(grad_out, normed, inverse, gain):
    scaled = grad_out * gain
    first_mean = jnp.mean(scaled, axis=-1, keepdims=True)
    second_mean = jnp.mean(scaled * normed, axis=-1, keepdims=True)
    return inverse * (scaled - first_mean - normed * second_mean)


def row(ref):
    return ref[...].reshape(1, -1)


def iota(shape, axis):
    return lax.broadcasted_iota(jnp.int32, shape, axis)


def place(token):
    return (token // GW) % WS * WS + token % WS


def window(token):
    return token // (GW * WS) * (GW // WS) + token % GW // WS


def by_head(value, heads):
    head = iota(value.shape, 1) // HD
    return jnp.concatenate(
        [jnp.where(head == h, value, jnp.zeros_like(value)) for h in range(heads)]
    )


def own_lanes(value, heads):
    rows = value.shape[0] // heads
    head = iota((rows, value.shape[1]), 1) // HD
    total = value[:rows]
    for h in range(1, heads):
        total = jnp.where(head == h, value[h * rows:(h + 1) * rows], total)
    return total


class Loaded:
    def __init__(self, source, buffer, sem):
        self.buffer, self.shape, self.dtype = buffer, source.shape, source.dtype
        self.copy, self.started = pltpu.make_async_copy(source, buffer, sem), False

    def start(self):
        if not self.started:
            self.copy.start()
            self.started = True

    def wait(self):
        if self.copy is not None:
            self.start()
            self.copy.wait()
            self.copy = None

    def __getitem__(self, at):
        self.wait()
        return self.buffer[at]


class Stored:
    def __init__(self, buffer, target, sem):
        self.buffer, self.shape, self.dtype = buffer, target.shape, target.dtype
        self.copy, self.sent = pltpu.make_async_copy(buffer, target, sem), False

    def __getitem__(self, at):
        return self.buffer[at]

    def __setitem__(self, at, value):
        self.buffer[at] = value

    def send(self):
        if not self.sent:
            self.copy.start()
            self.sent = True


def send_off(ref):
    if isinstance(ref, Stored):
        ref.send()


def call(kernel, outs, args, scratch=(), cost=0, exports=(), later=()):
    spaces = {"smem": pltpu.SMEM, "vmem": pltpu.VMEM, "hbm": pltpu.HBM, "hsmem": pltpu.HBM}
    spaces["keep"] = pltpu.HBM
    plain = len(outs)
    outs = list(outs) + [(args[i][0].shape, args[i][0].dtype, "vmem") for i in exports]
    loads = [i for i, (_, where) in enumerate(args) if where[0] == "h"]
    stores = [i for i, (_, _, where) in enumerate(outs) if where == "hbm"]
    shapes = [jax.ShapeDtypeStruct(shape, dtype) for shape, dtype, _ in outs]
    pinned = [spaces[where](shape, dtype) for shape, dtype, where in outs]
    operands = [
        pltpu.with_memory_space_constraint(a, pltpu.HBM) if spaces[where] == pltpu.HBM else a
        for a, where in args
    ]
    buffers = []
    for i in loads:
        if i in exports:
            continue
        array, where = args[i]
        space = pltpu.SMEM if where == "hsmem" else pltpu.VMEM
        buffers.append(space(array.shape, array.dtype))
    buffers += [pltpu.VMEM(outs[i][0], outs[i][1]) for i in stores]
    sems = [pltpu.SemaphoreType.DMA] * (len(loads) + len(stores))

    def body(*refs):
        refs = list(refs)
        ins, rest = refs[:len(args)], refs[len(args):]
        results, rest = rest[:len(outs)], rest[len(outs):]
        own, rest = rest[:len(scratch)], rest[len(scratch):]
        holds, marks = list(rest[:len(buffers)]), list(rest[len(buffers):])
        given = dict(zip(exports, results[plain:]))
        for i in loads:
            hold = given[i] if i in given else holds.pop(0)
            ins[i] = Loaded(ins[i], hold, marks.pop(0))
            if i not in later:
                ins[i].start()
        for i in stores:
            results[i] = Stored(holds.pop(0), results[i], marks.pop(0))
        kernel(*ins, *results[:plain], *own)
        for i in loads:
            ins[i].wait()
        for i in stores:
            results[i].send()
        for i in stores:
            results[i].copy.wait()

    return pl.pallas_call(
        body,
        name=kernel.__name__,
        out_shape=pinned,
        in_specs=[pl.BlockSpec(memory_space=spaces[where]) for _, where in args],
        out_specs=[pl.BlockSpec(memory_space=spaces[where]) for _, _, where in outs],
        scratch_shapes=[pltpu.VMEM(shape, dtype) for shape, dtype in scratch] + buffers + sems,
        compiler_params=pltpu.CompilerParams(vmem_limit_bytes=VMEM_BYTES),
        cost_estimate=pl.CostEstimate(flops=cost * 10 ** 9, bytes_accessed=0, transcendentals=0),
    )(*operands)


def attend_kernel(
    spot, x, g1, s1, wq, wk, wv, bq, bv, rel, pidx, seg, valid, att, first, q, k, v, probs,
):
    tokens, span = x.shape[0], wq.shape[1]
    heads = span // HD
    blocks = tokens // BLOCK
    for b in range(blocks):
        rows = pl.ds(b * BLOCK, BLOCK)
        normed, _ = normalize(x[rows, :].astype(F32))
        first[rows, :] = (normed * row(g1) + row(s1)).astype(BF)
    weights = jnp.concatenate([wq[...], wk[...], wv[...]], axis=1)
    for i in range(2):
        rows = pl.ds(i * (tokens // 2), tokens // 2)
        mixed = dot(first[rows, :], weights)
        q[rows, :] = (mixed[:, :span] + row(bq)).astype(BF)
        k[rows, :] = mixed[:, span:2 * span].astype(BF)
        v[rows, :] = (mixed[:, 2 * span:] + row(bv)).astype(BF)
    lanes = 2 * heads * WIN
    group = heads * WIN
    table = rel[...]
    coarse = table.astype(BF)
    fine = (table - coarse.astype(F32)).astype(BF)
    lane = iota((heads, lanes), 1)
    mine = lane % group // WIN == iota((heads, lanes), 0)
    rows_by_offset = dot_tn(coarse, (mine & (lane < group)).astype(BF)) + dot_tn(
        fine, (mine & (lane >= group)).astype(BF)
    )
    index = jnp.concatenate([pidx[...]] * (2 * heads), axis=1)
    terms = jnp.zeros((WIN, lanes), F32)
    for o in range(rel.shape[1]):
        terms = jnp.where(index == o, rows_by_offset[o:o + 1, :], terms)
    spread = (place(iota((BLOCK, WIN), 0)) == iota((BLOCK, WIN), 1)).astype(BF)
    terms = dot(spread, terms.astype(BF)).astype(BF)
    lane = iota((lanes, BLOCK), 0)
    here = lane % WIN == place(iota((lanes, BLOCK), 1))
    bias = jnp.concatenate(
        [dot(terms, (here & (lane % group // WIN == h)).astype(BF)) for h in range(heads)]
    )
    query_at, key_at = iota((BLOCK, BLOCK), 0), iota((BLOCK, BLOCK), 1)
    near = window(query_at) == window(key_at)
    selfs = query_at == key_at
    factor = HD ** (-0.5)
    for b in range(blocks):
        rows = pl.ds(b * BLOCK, BLOCK)
        seg_keys = jnp.broadcast_to(seg[:, rows].astype(F32), (BLOCK, BLOCK))
        valid_keys = jnp.broadcast_to(valid[:, rows], (BLOCK, BLOCK)) > 0
        allowed = near & (seg_keys == seg_keys.T) & (valid_keys | selfs)
        wall = jnp.where(allowed, 0.0, NEG_FILL)
        scores = dot_nt(by_head(q[rows, :], heads), k[rows, :]) * factor + bias
        scores = jnp.where(jnp.concatenate([wall] * heads) < 0.0, NEG_FILL, scores)
        expo = jnp.exp(scores - jnp.max(scores, axis=-1, keepdims=True))
        prob = expo * (1.0 / jnp.sum(expo, axis=-1, keepdims=True))
        probs[b] = prob
        att[rows, :] = own_lanes(dot(prob.astype(BF), v[rows, :]), heads).astype(BF)


def fetch_kernel(after, also, *operands):
    for ref in operands[:-1]:
        ref.wait()
    operands[-1][...] = jnp.zeros_like(operands[-1])


def mlp_kernel(
    spot, a0, a1, a2, a3, p0, p1, p2, p3, x, bo, g2, s2, w1, b1, cot, w2,
    mid, second, hidden, gpre, keep, send, att_all, wo_all,
):
    me = spot[0]
    width = a0.shape[1]
    for j, (a, p) in enumerate(((a0, p0), (a1, p1), (a2, p2), (a3, p3))):
        here = pl.ds(pl.multiple_of((me ^ j) * width, width), width)
        att_all[:, here] = a[...]
        wo_all[here, :] = p[...]
    tokens = x.shape[0]
    half = tokens // 2
    curve = (2.0 / jnp.pi) ** 0.5
    for i in range(2):
        rows = pl.ds(i * half, half)
        value = x[rows, :].astype(F32) + dot(att_all[rows, :], wo_all[...]) + row(bo)
        mid[rows, :] = value
        normed, _ = normalize(value)
        second[rows, :] = (normed * row(g2) + row(s2)).astype(BF)
        pre = dot(second[rows, :], w1[...]) + row(b1)
        square = pre * pre
        bend = jnp.tanh(curve * (pre + 0.044715 * (pre * square)))
        upper = 0.5 * (1.0 + bend)
        hidden[rows, :] = (pre * upper).astype(BF)
        slope = upper + 0.5 * pre * (1.0 - bend * bend) * (curve * (1.0 + 0.134145 * square))
        gpre[rows, :] = (dot_nt(cot[rows, :], w2[...]) * slope).astype(BF)
    send_off(mid)
    core = me % 2
    mine = pl.ds(pl.multiple_of(core * half, half), half)
    other = pl.ds(pl.multiple_of((1 - core) * half, half), half)
    send[...] = dot_nt(gpre[other, :], w1[...]).astype(BF)
    keep[...] = dot_nt(gpre[mine, :], w1[...])


def halves(flag, rows):
    near = pl.ds(pl.multiple_of(flag * rows, rows), rows)
    return near, pl.ds(pl.multiple_of((1 - flag) * rows, rows), rows)


def mlp_grad_kernel(spot, second, hidden, gpre, cot, own1, away1, own2, away2, small, grads):
    part = own1.shape[0]
    mine, other = halves(spot[2], part)
    grads[...] = dot_tn(second[...], gpre[...]).astype(BF)
    own1[...] = grads[mine, :]
    away1[...] = grads[other, :]
    mine, other = halves(spot[3], part)
    grads[...] = dot_tn(hidden[...], cot[...]).astype(BF)
    own2[...] = grads[mine, :]
    away2[...] = grads[other, :]
    which = iota(small.shape, 0)
    first = jnp.sum(gpre[...].astype(F32), axis=0, keepdims=True)
    later = jnp.sum(cot[...].astype(F32), axis=0, keepdims=True)
    small[...] = jnp.where(which == 0, first, jnp.where(which == 1, later, 0.0)).astype(BF)


def attend_back_kernel(
    spot, s2a, s2b, mid, cot, g2, wo, v, probs, k, q, first, att, wq, wk, wv, g1, s1,
    gmid, own, to_y, to_z, to_yz, gq, gk, gv, scores, sums, norm1, gsec, gproj, gatt, pay,
):
    core, place_yz = spot[0] % 2, 2 * spot[2] + spot[3]
    tokens, width = cot.shape
    half = tokens // 2
    span = wq.shape[1]
    heads = span // HD
    blocks = tokens // BLOCK
    mine, other = halves(core, half)
    gsec[mine, :] = s2a[...].astype(F32)
    gsec[other, :] = s2b[...].astype(F32)
    gain_sum = jnp.zeros((1, width), F32)
    shift_sum = jnp.zeros((1, width), F32)
    proj_sum = jnp.zeros((1, width), F32)
    for b in range(blocks):
        rows = pl.ds(b * BLOCK, BLOCK)
        grad = gsec[rows, :]
        normed, inverse = normalize(mid[rows, :])
        gain_sum += jnp.sum(grad * normed, axis=0, keepdims=True)
        shift_sum += jnp.sum(grad, axis=0, keepdims=True)
        value = cot[rows, :].astype(F32) + norm_back(grad, normed, inverse, row(g2))
        gmid[rows, :] = value
        proj_sum += jnp.sum(value, axis=0, keepdims=True)
        gproj[rows, :] = value.astype(BF)
    gatt[...] = dot_nt(gproj[...], wo[...]).astype(BF)
    factor = HD ** (-0.5)
    score_sum = jnp.zeros((heads * BLOCK, BLOCK), F32)
    for b in range(blocks):
        rows = pl.ds(b * BLOCK, BLOCK)
        grads = by_head(gatt[rows, :], heads)
        prob = probs[b]
        grad = dot_nt(grads, v[rows, :])
        gv[rows, :] = dot_tn(prob.astype(BF), grads).astype(BF)
        inner = jnp.sum(prob * grad, axis=-1, keepdims=True)
        gscore = (prob * (grad - inner)).astype(BF)
        score_sum += gscore.astype(F32)
        gq[rows, :] = (factor * own_lanes(dot(gscore, k[rows, :]), heads)).astype(BF)
        gk[rows, :] = (factor * dot_tn(gscore, by_head(q[rows, :], heads))).astype(BF)
    scores[...] = score_sum
    shift = jnp.zeros((8, width), F32)
    gain = jnp.zeros((8, width), F32)
    ones = jnp.ones((8, span), BF)
    eight = iota((8, span), 0)
    mixed = dot_tn(first[...], jnp.concatenate([gq[...], gk[...], gv[...]], axis=1))
    for j, (part, weight) in enumerate(((gq, wq), (gk, wk), (gv, wv))):
        grads = mixed[:, j * span:(j + 1) * span]
        total = jnp.sum(part[...].astype(F32), axis=0, keepdims=True)
        if j != 1:
            at = 0 if j == 0 else span
            sums[3:4, at:at + span] = total
        coarse = total.astype(BF)
        fine = (total - coarse.astype(F32)).astype(BF)
        pair = jnp.where(eight == 0, coarse, jnp.where(eight == 1, fine, jnp.zeros_like(coarse)))
        shift += dot_nt(pair, weight[...])
        product = weight[...].astype(F32) * grads
        coarse = product.astype(BF)
        gain += dot_nt(ones, coarse) + dot_nt(ones, (product - coarse.astype(F32)).astype(BF))
        grads = grads.astype(BF)
        for i in range(width // span):
            pay[j * span:(j + 1) * span, i * span:(i + 1) * span] = grads[i * span:(i + 1) * span]
    pay[3 * span:4 * span, :] = dot_tn(att[...], gproj[...]).astype(BF)
    for ref, flip in ((own, 0), (to_y, 2), (to_z, 1), (to_yz, 3)):
        ref[...] = pay[pl.ds(pl.multiple_of((place_yz ^ flip) * span, span), span), :]
    sums[3:4, 2 * span:] = jnp.zeros((1, width - 2 * span), F32)
    which = iota((ROWS, width), 0)
    shift = shift[0:1, :] + shift[1:2, :]
    gain = (gain[0:1, :] - row(s1) * shift) / row(g1)
    norm1[...] = jnp.where(which == 0, gain, jnp.where(which == 1, shift, 0.0)).astype(BF)
    sums[0:1, :] = gain_sum
    sums[1:2, :] = shift_sum
    sums[2:3, :] = proj_sum


def attend_out_kernel(spot, after, gq, gk, gv, wq, wk, wv, hidden, w2, keep, send):
    half = hidden.shape[0] // 2
    for where, ref in zip(halves(spot[0] % 2, half), (keep, send)):
        ref[0:half, :] = (
            dot_nt(gq[where, :], wq[...])
            + dot_nt(gk[where, :], wk[...])
            + dot_nt(gv[where, :], wv[...])
        ).astype(BF)
        ref[half:, :] = dot(hidden[where, :], w2[...]).astype(BF)


def sums_kernel(after, scores, sums, pidx, small, all_sums):
    heads = scores.shape[0] // BLOCK
    at = place(iota((BLOCK, WIN), 0)) == iota((BLOCK, WIN), 1)
    fold = at.astype(F32)
    lanes = heads * WIN
    folded = jnp.zeros((WIN, lanes), F32)
    for h in range(heads):
        lane = iota((BLOCK, lanes), 1)
        lay = ((place(iota((BLOCK, lanes), 0)) == lane % WIN) & (lane // WIN == h)).astype(F32)
        once = lax.dot_general(
            fold, scores[h * BLOCK:(h + 1) * BLOCK, :], (((0,), (0,)), ((), ())),
            precision=EXACT, preferred_element_type=F32,
        )
        folded += jnp.dot(once, lay, precision=EXACT, preferred_element_type=F32)
    index = jnp.concatenate([pidx[...]] * heads, axis=1)
    slots = 64
    slot = iota((slots, lanes), 0)
    by_offset = jnp.zeros((slots, lanes), F32)
    for o in range(49):
        total = jnp.sum(jnp.where(index == o, folded, 0.0), axis=0, keepdims=True)
        by_offset = jnp.where(slot == o, total, by_offset)
    pick = (iota((8, lanes), 1) // WIN == iota((8, lanes), 0)).astype(F32)
    offsets = lax.dot_general(
        pick, by_offset, (((1,), (1,)), ((), ())), precision=EXACT, preferred_element_type=F32
    )
    all_sums[...] = jnp.zeros_like(all_sums)
    all_sums[0:3, :] = sums[0:3, :]
    all_sums[3:4, :] = sums[3:4, :]
    all_sums[8:16, 0:slots] = offsets
    small[...] = all_sums[...].astype(BF)


def finish_kernel(spot, s4, r4, gmid, x, g1, mid, b2, layer_out, input_grad):
    core = spot[0] % 2
    half = x.shape[0] // 2
    for part, ref in enumerate((s4, r4)):
        start = core if part == 0 else 1 - core
        where = pl.ds(pl.multiple_of(start * half, half), half)
        normed, inverse = normalize(x[where, :].astype(F32))
        grad = ref[0:half, :].astype(F32)
        input_grad[where, :] = gmid[where, :] + norm_back(grad, normed, inverse, row(g1))
        mlp = ref[half:, :].astype(F32)
        layer_out[where, :] = mid[where, :] + mlp + row(b2)


def widen_kernel(spot, after, near1, far1, near2, far2, w1, w2):
    part = near1.shape[0]
    for flag, near, far, ref in ((spot[2], near1, far1, w1), (spot[3], near2, far2, w2)):
        mine, other = halves(flag, part)
        ref[mine, :] = near[...].astype(F32)
        ref[other, :] = far[...].astype(F32)
        send_off(ref)


def unpack_kernel(
    spot, after, near, from_y, from_z, from_yz,
    wq, wk, wv, wo, b1, b2, g2, s2, bo, bq, bv, rel, g1, s1, both,
):
    place_yz = 2 * spot[2] + spot[3]
    width = near.shape[1]
    span = wo.shape[0]
    for ref, flip in ((near, 0), (from_y, 2), (from_z, 1), (from_yz, 3)):
        both[place_yz ^ flip] = ref[0:span, :]
    for j, ref in enumerate((wq, wk, wv)):
        for i in range(width // span):
            block = both[j, :, i * span:(i + 1) * span]
            ref[i * span:(i + 1) * span, :] = block.astype(F32)
        send_off(ref)
    wo[...] = both[3].astype(F32)
    send_off(wo)
    sums = (near[span:, :].astype(F32) + from_y[span:, :].astype(F32)) + (
        from_z[span:, :].astype(F32) + from_yz[span:, :].astype(F32)
    )
    for at, ref in ((0, b1), (1, b2), (8, g2), (9, s2), (10, bo), (24, g1), (25, s1)):
        ref[...] = sums[at]
    bq[...] = sums[11, :span]
    bv[...] = sums[11, span:2 * span]
    rel[...] = sums[16:16 + rel.shape[0], :rel.shape[1]]


def swap(value, axis, bit, size):
    return lax.ppermute(value, axis, [(i, i ^ bit) for i in range(size)])


def shards(
    inputs,
    query_weight,
    key_weight,
    value_weight,
    query_bias,
    value_bias,
    position_bias,
    proj_weight,
    proj_bias,
    norm1_gain,
    norm1_shift,
    norm2_gain,
    norm2_shift,
    up_weight,
    up_bias,
    down_weight,
    down_bias,
    segment_ids,
    valid_mask,
    position_index,
    out_cotangent,
    dp,
    tensor,
):
    tokens, width = inputs.shape
    half = tokens // 2
    span = query_weight.shape[1]
    units = up_weight.shape[1]
    heads = span // HD
    blocks = tokens // BLOCK
    me = lax.axis_index("tensor")
    mate = lax.axis_index("dp")
    bits = [1 << i for i in range(dp.bit_length() - 1)]
    flags = [(mate >> i) & 1 for i in range(len(bits))]
    lower = [flag == 0 for flag in flags]
    sizes = [(width >> (i + 1)) * n for i in range(len(bits)) for n in (1, 2)]
    starts = {
        (i, size): (flags[i] * size).astype(jnp.uint32) for i in range(len(bits)) for size in sizes
    }
    stops = {
        at: ((1 - flags[at[0]]) * at[1]).astype(jnp.uint32) for at in starts
    }
    spot = jnp.stack(
        [me, mate]
        + flags
        + [flag.astype(jnp.int32) for flag in lower]
        + [at.astype(jnp.int32) for at in list(starts.values()) + list(stops.values())]
    )
    seg = segment_ids.reshape(1, tokens)
    valid = valid_mask.reshape(1, tokens)
    wide = (tokens, width)
    narrow = (tokens, span)

    wo_x = swap(proj_weight, "tensor", 2, tensor)
    wo_c = swap(proj_weight, "tensor", 1, tensor)
    wo_d = swap(wo_x, "tensor", 1, tensor)

    att, first, q, k, v, probs = call(
        attend_kernel,
        [
            (narrow, BF, "vmem"), (wide, BF, "vmem"), (narrow, BF, "vmem"), (narrow, BF, "vmem"),
            (narrow, BF, "vmem"), ((blocks, heads * BLOCK, BLOCK), F32, "vmem"),
        ],
        [
            (spot, "smem"), (inputs, "hbm"), (norm1_gain, "hbm"), (norm1_shift, "hbm"),
            (query_weight, "hbm"), (key_weight, "hbm"), (value_weight, "hbm"), (query_bias, "hbm"),
            (value_bias, "hbm"), (position_bias.T, "hbm"), (position_index, "hbm"), (seg, "hbm"),
            (valid, "hbm"),
        ],
        cost=20,
    )
    (
        _, inputs, norm1_gain, norm1_shift, position_index, query_weight, key_weight, value_weight,
        proj_weight, proj_bias, norm2_gain, norm2_shift, up_weight, up_bias, out_cotangent,
        down_weight, down_bias,
    ) = call(
        fetch_kernel,
        [((8, BLOCK), F32, "vmem")],
        [(att, "vmem"), (wo_x, "vmem")]
        + [
            (value, "hbm")
            for value in (
                inputs, norm1_gain, norm1_shift, position_index, query_weight, key_weight,
                value_weight, proj_weight, proj_bias, norm2_gain, norm2_shift, up_weight, up_bias,
                out_cotangent, down_weight, down_bias,
            )
        ],
        exports=tuple(range(2, 18)),
        cost=0,
    )
    att_x, down_bias = lax.optimization_barrier((swap(att, "tensor", 2, tensor), down_bias))
    att_c = swap(att, "tensor", 1, tensor)
    att_d = swap(att_x, "tensor", 1, tensor)

    mid, second, hidden, gpre, keep3, send3 = call(
        mlp_kernel,
        [
            (wide, F32, "vmem"), (wide, BF, "vmem"), ((tokens, units), BF, "vmem"),
            ((tokens, units), BF, "vmem"), ((half, width), F32, "vmem"), ((half, width), BF, "vmem"),
        ],
        [
            (spot, "smem"), (att, "vmem"), (att_c, "vmem"), (att_x, "vmem"), (att_d, "vmem"),
            (proj_weight, "vmem"), (wo_c, "vmem"), (wo_x, "vmem"), (wo_d, "vmem"),
            (inputs, "vmem"), (proj_bias, "vmem"), (norm2_gain, "vmem"), (norm2_shift, "vmem"),
            (up_weight, "vmem"), (up_bias, "vmem"), (out_cotangent, "vmem"), (down_weight, "vmem"),
        ],
        scratch=[((tokens, tensor * span), BF), ((tensor * span, width), BF)],
        cost=2,
    )

    def fold(value, other):
        return (value.astype(F32) + other.astype(F32)).astype(BF)

    own1, away1, own2, away2, small_a = call(
        mlp_grad_kernel,
        [((half, width), BF, "vmem")] * 4 + [((8, width), BF, "vmem")],
        [
            (spot, "smem"), (second, "vmem"), (hidden, "vmem"), (gpre, "vmem"),
            (out_cotangent, "vmem"),
        ],
        scratch=[((width, units), BF)],
        cost=2,
    )
    come3 = swap(send3, "tensor", 1, tensor)
    come3, small_a, away1, away2 = lax.optimization_barrier((come3, small_a, away1, away2))
    pair3 = fold(keep3, come3)
    come3, come_a, come_b = lax.optimization_barrier(
        (
            swap(pair3, "tensor", 2, tensor),
            swap(away1, "dp", bits[0], dp),
            swap(away2, "dp", bits[1], dp),
        )
    )
    sum3 = fold(pair3, come3)
    rest3 = swap(sum3, "tensor", 1, tensor)

    def meet(own, along_y, along_z, along_yz):
        return (
            own,
            swap(along_y, "dp", bits[0], dp),
            swap(along_z, "dp", bits[1], dp),
            swap(along_yz, "dp", bits[0] | bits[1], dp),
        )

    def combine(parts):
        own, y, z, yz = [part.astype(F32) for part in parts]
        return ((own + y) + (z + yz)).astype(BF)

    piece = ((span, width), BF, "vmem")
    gmid, att_own, att_y, att_z, att_yz, gq, gk, gv, scores, sums, norm1 = call(
        attend_back_kernel,
        [
            (wide, F32, "vmem"), piece, piece, piece, piece, (narrow, BF, "vmem"),
            (narrow, BF, "vmem"), (narrow, BF, "vmem"), ((heads * BLOCK, BLOCK), F32, "vmem"),
            ((8, width), F32, "vmem"), ((ROWS, width), BF, "vmem"),
        ],
        [
            (spot, "smem"), (sum3, "vmem"), (rest3, "vmem"), (mid, "vmem"),
            (out_cotangent, "vmem"), (norm2_gain, "vmem"), (proj_weight, "vmem"), (v, "vmem"),
            (probs, "vmem"), (k, "vmem"), (q, "vmem"), (first, "vmem"), (att, "vmem"),
            (query_weight, "vmem"), (key_weight, "vmem"), (value_weight, "vmem"),
            (norm1_gain, "vmem"), (norm1_shift, "vmem"),
        ],
        scratch=[(wide, F32), (wide, BF), (narrow, BF), ((4 * span, width), BF)],
        cost=1,
    )
    att_parts = meet(att_own, att_y, att_z, att_yz)
    chunk = combine(att_parts)
    across = [swap(norm1, "tensor", flip, tensor).astype(F32) for flip in (1, 2, 3)]
    norm1 = ((norm1.astype(F32) + across[0]) + (across[1] + across[2])).astype(BF)
    (small_b,) = call(
        sums_kernel,
        [((16, width), BF, "vmem")],
        [(norm1, "vmem"), (scores, "vmem"), (sums, "vmem"), (position_index, "vmem")],
        scratch=[((16, width), F32)],
        cost=1,
    )
    keep4, send4 = call(
        attend_out_kernel,
        [((tokens, width), BF, "vmem"), ((tokens, width), BF, "vmem")],
        [
            (spot, "smem"), (chunk, "vmem"), (gq, "vmem"), (gk, "vmem"), (gv, "vmem"),
            (query_weight, "vmem"), (key_weight, "vmem"), (value_weight, "vmem"),
            (hidden, "vmem"), (down_weight, "vmem"),
        ],
        cost=1,
    )

    pair4 = fold(keep4, swap(send4, "tensor", 1, tensor))
    sum4 = fold(pair4, swap(pair4, "tensor", 2, tensor))
    rest4 = swap(sum4, "tensor", 1, tensor)

    left = jnp.uint32(0)

    def pick(value, i):
        part = value.shape[0] // 2
        return (
            lax.dynamic_slice(value, (starts[i, part], left), (part, width)),
            lax.dynamic_slice(value, (stops[i, part], left), (part, width)),
        )

    def scatter(value, i):
        own, away = pick(value, i)
        return fold(own, swap(away, "dp", bits[i], dp))

    def gather(own, i):
        other = swap(own, "dp", bits[i], dp)
        return jnp.where(
            lower[i], jnp.concatenate([own, other]), jnp.concatenate([other, own])
        )

    more = range(2, len(bits))

    keep_a, away_a = pick(fold(own1, come_a), 1)
    keep_b, away_b = pick(fold(own2, come_b), 0)
    come_a, come_b, gq = lax.optimization_barrier(
        (swap(away_a, "dp", bits[1], dp), swap(away_b, "dp", bits[0], dp), gq)
    )
    mlp_chunk = jnp.concatenate([fold(keep_a, come_a), fold(keep_b, come_b)])
    for i in more:
        mlp_chunk = fold(mlp_chunk, swap(mlp_chunk, "dp", bits[i], dp))
    chunk = jnp.concatenate([chunk, small_a, small_b, norm1[:8]])
    for i in more:
        chunk = fold(chunk, swap(chunk, "dp", bits[i], dp))
    chunks = meet(chunk, chunk, chunk, chunk)
    near1 = gather(mlp_chunk[:mlp_chunk.shape[0] // 2], 1)
    near2 = gather(mlp_chunk[mlp_chunk.shape[0] // 2:], 0)
    far1 = swap(near1, "dp", bits[0], dp)
    far2 = swap(near2, "dp", bits[1], dp)
    layer_out, input_grad = call(
        finish_kernel,
        [(wide, F32, "hbm"), (wide, F32, "hbm")],
        [
            (spot, "smem"), (sum4, "vmem"), (rest4, "vmem"), (gmid, "vmem"), (inputs, "vmem"),
            (norm1_gain, "vmem"), (mid, "vmem"), (down_bias, "vmem"),
        ],
        cost=2,
    )
    vector, short = ((width,), F32, "hbm"), ((span,), F32, "hbm")
    (
        wq_total, wk_total, wv_total, wo_total, b1_total, b2_total, g2_total, s2_total, bo_total,
        bq_total, bv_total, rel_total, g1_total, s1_total,
    ) = call(
        unpack_kernel,
        [
            ((width, span), F32, "hbm"), ((width, span), F32, "hbm"), ((width, span), F32, "hbm"),
            ((span, width), F32, "hbm"), vector, vector, vector, vector, vector, short, short,
            ((heads, position_bias.shape[0]), F32, "hbm"), vector, vector,
        ],
        [(spot, "smem"), (layer_out, "keep")] + [(value, "vmem") for value in chunks],
        scratch=[((4, span, width), BF)],
    )
    rel_total = rel_total.T
    w1_total, w2_total = call(
        widen_kernel,
        [((width, units), F32, "hbm"), ((units, width), F32, "hbm")],
        [(spot, "smem"), (wq_total, "keep")]
        + [(value, "vmem") for value in (near1, far1, near2, far2)],
    )

    return (
        layer_out,
        input_grad,
        wq_total,
        wk_total,
        wv_total,
        bq_total,
        bv_total,
        rel_total,
        wo_total,
        bo_total,
        g1_total,
        s1_total,
        g2_total,
        s2_total,
        w1_total,
        b1_total,
        w2_total,
        b2_total,
    )


def solution(mesh):
    dp, tensor = mesh.shape["dp"], mesh.shape["tensor"]

    def body(*args):
        return shards(*args, dp=dp, tensor=tensor)

    column, line, whole = P(None, "tensor"), P("tensor"), P()
    return jax.shard_map(
        body,
        mesh=mesh,
        in_specs=(
            P("dp", None),
            column,
            column,
            column,
            line,
            line,
            column,
            P("tensor", None),
            whole,
            whole,
            whole,
            whole,
            whole,
            column,
            line,
            P("tensor", None),
            whole,
            P("dp", None),
            P("dp", None),
            whole,
            P("dp", None),
        ),
        out_specs=(
            P("dp", None),
            P("dp", None),
            column,
            column,
            column,
            line,
            line,
            column,
            P("tensor", None),
            whole,
            whole,
            whole,
            whole,
            whole,
            column,
            line,
            P("tensor", None),
            whole,
        ),
        check_vma=False,
    )
```

```python
import jax
import jax.numpy as jnp
from jax import lax
from jax.experimental import pallas as pl
from jax.experimental.pallas import tpu as pltpu
from jax.sharding import PartitionSpec as P

HD = 32
GW = 8
WS = 4
WIN = WS * WS
BLOCK = 128
NEG_FILL = -1e30
BF = jnp.bfloat16
F32 = jnp.float32
EXACT = lax.Precision.HIGHEST
VMEM_BYTES = 24 * 1024 * 1024
ROWS = 16


def dot(left, right):
    return jnp.dot(left, right, preferred_element_type=F32)


def dot_nt(left, right):
    return lax.dot_general(left, right, (((1,), (1,)), ((), ())), preferred_element_type=F32)


def dot_tn(left, right):
    return lax.dot_general(left, right, (((0,), (0,)), ((), ())), preferred_element_type=F32)


def exact_nt(left, right):
    return lax.dot_general(
        left, right, (((1,), (1,)), ((), ())), precision=EXACT, preferred_element_type=F32
    )


def normalize(value):
    centre = value - jnp.mean(value, axis=-1, keepdims=True)
    spread = jnp.mean(centre * centre, axis=-1, keepdims=True)
    inverse = lax.rsqrt(spread + 1e-06)
    return centre * inverse, inverse


def norm_back(grad_out, normed, inverse, gain):
    scaled = grad_out * gain
    first_mean = jnp.mean(scaled, axis=-1, keepdims=True)
    second_mean = jnp.mean(scaled * normed, axis=-1, keepdims=True)
    return inverse * (scaled - first_mean - normed * second_mean)


def row(ref):
    return ref[...].reshape(1, -1)


def iota(shape, axis):
    return lax.broadcasted_iota(jnp.int32, shape, axis)


def place(token):
    return (token // GW) % WS * WS + token % WS


def window(token):
    return token // (GW * WS) * (GW // WS) + token % GW // WS


def by_head(value, heads):
    head = iota(value.shape, 1) // HD
    return jnp.concatenate(
        [jnp.where(head == h, value, jnp.zeros_like(value)) for h in range(heads)]
    )


def own_lanes(value, heads):
    rows = value.shape[0] // heads
    head = iota((rows, value.shape[1]), 1) // HD
    total = value[:rows]
    for h in range(1, heads):
        total = jnp.where(head == h, value[h * rows:(h + 1) * rows], total)
    return total


class Loaded:
    def __init__(self, source, buffer, sem):
        self.buffer, self.shape, self.dtype = buffer, source.shape, source.dtype
        self.copy, self.started = pltpu.make_async_copy(source, buffer, sem), False

    def start(self):
        if not self.started:
            self.copy.start()
            self.started = True

    def wait(self):
        if self.copy is not None:
            self.start()
            self.copy.wait()
            self.copy = None

    def __getitem__(self, at):
        self.wait()
        return self.buffer[at]


class Stored:
    def __init__(self, buffer, target, sem):
        self.buffer, self.shape, self.dtype = buffer, target.shape, target.dtype
        self.copy, self.sent = pltpu.make_async_copy(buffer, target, sem), False

    def __getitem__(self, at):
        return self.buffer[at]

    def __setitem__(self, at, value):
        self.buffer[at] = value

    def send(self):
        if not self.sent:
            self.copy.start()
            self.sent = True


def send_off(ref):
    if isinstance(ref, Stored):
        ref.send()


def call(kernel, outs, args, scratch=(), cost=0, exports=(), later=()):
    spaces = {"smem": pltpu.SMEM, "vmem": pltpu.VMEM, "hbm": pltpu.HBM, "hsmem": pltpu.HBM}
    spaces["keep"] = pltpu.HBM
    plain = len(outs)
    outs = list(outs) + [(args[i][0].shape, args[i][0].dtype, "vmem") for i in exports]
    loads = [i for i, (_, where) in enumerate(args) if where[0] == "h"]
    stores = [i for i, (_, _, where) in enumerate(outs) if where == "hbm"]
    shapes = [jax.ShapeDtypeStruct(shape, dtype) for shape, dtype, _ in outs]
    pinned = [spaces[where](shape, dtype) for shape, dtype, where in outs]
    operands = [
        pltpu.with_memory_space_constraint(a, pltpu.HBM) if spaces[where] == pltpu.HBM else a
        for a, where in args
    ]
    buffers = []
    for i in loads:
        if i in exports:
            continue
        array, where = args[i]
        space = pltpu.SMEM if where == "hsmem" else pltpu.VMEM
        buffers.append(space(array.shape, array.dtype))
    buffers += [pltpu.VMEM(outs[i][0], outs[i][1]) for i in stores]
    sems = [pltpu.SemaphoreType.DMA] * (len(loads) + len(stores))

    def body(*refs):
        refs = list(refs)
        ins, rest = refs[:len(args)], refs[len(args):]
        results, rest = rest[:len(outs)], rest[len(outs):]
        own, rest = rest[:len(scratch)], rest[len(scratch):]
        holds, marks = list(rest[:len(buffers)]), list(rest[len(buffers):])
        given = dict(zip(exports, results[plain:]))
        for i in loads:
            hold = given[i] if i in given else holds.pop(0)
            ins[i] = Loaded(ins[i], hold, marks.pop(0))
            if i not in later:
                ins[i].start()
        for i in stores:
            results[i] = Stored(holds.pop(0), results[i], marks.pop(0))
        kernel(*ins, *results[:plain], *own)
        for i in loads:
            ins[i].wait()
        for i in stores:
            results[i].send()
        for i in stores:
            results[i].copy.wait()

    return pl.pallas_call(
        body,
        name=kernel.__name__,
        out_shape=pinned,
        in_specs=[pl.BlockSpec(memory_space=spaces[where]) for _, where in args],
        out_specs=[pl.BlockSpec(memory_space=spaces[where]) for _, _, where in outs],
        scratch_shapes=[pltpu.VMEM(shape, dtype) for shape, dtype in scratch] + buffers + sems,
        compiler_params=pltpu.CompilerParams(vmem_limit_bytes=VMEM_BYTES),
        cost_estimate=pl.CostEstimate(flops=cost * 10 ** 9, bytes_accessed=0, transcendentals=0),
    )(*operands)


def attend_kernel(
    spot, x, g1, s1, wq, wk, wv, bq, bv, rel, pidx, seg, valid, att, first, q, k, v, probs,
):
    tokens, span = x.shape[0], wq.shape[1]
    heads = span // HD
    blocks = tokens // BLOCK
    for b in range(blocks):
        rows = pl.ds(b * BLOCK, BLOCK)
        normed, _ = normalize(x[rows, :].astype(F32))
        first[rows, :] = (normed * row(g1) + row(s1)).astype(BF)
    weights = jnp.concatenate([wq[...], wk[...], wv[...]], axis=1)
    for i in range(2):
        rows = pl.ds(i * (tokens // 2), tokens // 2)
        mixed = dot(first[rows, :], weights)
        q[rows, :] = (mixed[:, :span] + row(bq)).astype(BF)
        k[rows, :] = mixed[:, span:2 * span].astype(BF)
        v[rows, :] = (mixed[:, 2 * span:] + row(bv)).astype(BF)
    lanes = 2 * heads * WIN
    group = heads * WIN
    table = rel[...]
    coarse = table.astype(BF)
    fine = (table - coarse.astype(F32)).astype(BF)
    lane = iota((heads, lanes), 1)
    mine = lane % group // WIN == iota((heads, lanes), 0)
    rows_by_offset = dot_tn(coarse, (mine & (lane < group)).astype(BF)) + dot_tn(
        fine, (mine & (lane >= group)).astype(BF)
    )
    index = jnp.concatenate([pidx[...]] * (2 * heads), axis=1)
    terms = jnp.zeros((WIN, lanes), F32)
    for o in range(rel.shape[1]):
        terms = jnp.where(index == o, rows_by_offset[o:o + 1, :], terms)
    spread = (place(iota((BLOCK, WIN), 0)) == iota((BLOCK, WIN), 1)).astype(BF)
    terms = dot(spread, terms.astype(BF)).astype(BF)
    lane = iota((lanes, BLOCK), 0)
    here = lane % WIN == place(iota((lanes, BLOCK), 1))
    bias = jnp.concatenate(
        [dot(terms, (here & (lane % group // WIN == h)).astype(BF)) for h in range(heads)]
    )
    query_at, key_at = iota((BLOCK, BLOCK), 0), iota((BLOCK, BLOCK), 1)
    near = window(query_at) == window(key_at)
    selfs = query_at == key_at
    factor = HD ** (-0.5)
    for b in range(blocks):
        rows = pl.ds(b * BLOCK, BLOCK)
        seg_keys = jnp.broadcast_to(seg[:, rows].astype(F32), (BLOCK, BLOCK))
        valid_keys = jnp.broadcast_to(valid[:, rows], (BLOCK, BLOCK)) > 0
        allowed = near & (seg_keys == seg_keys.T) & (valid_keys | selfs)
        wall = jnp.where(allowed, 0.0, NEG_FILL)
        scores = dot_nt(by_head(q[rows, :], heads), k[rows, :]) * factor + bias
        scores = jnp.where(jnp.concatenate([wall] * heads) < 0.0, NEG_FILL, scores)
        expo = jnp.exp(scores - jnp.max(scores, axis=-1, keepdims=True))
        prob = expo * (1.0 / jnp.sum(expo, axis=-1, keepdims=True))
        probs[b] = prob
        att[rows, :] = own_lanes(dot(prob.astype(BF), v[rows, :]), heads).astype(BF)


def fetch_kernel(after, also, *operands):
    for ref in operands[:-1]:
        ref.wait()
    operands[-1][...] = jnp.zeros_like(operands[-1])


def mlp_kernel(
    spot, a0, a1, a2, a3, p0, p1, p2, p3, x, bo, g2, s2, w1, b1, cot, w2,
    mid, second, hidden, gpre, keep, send, att_all, wo_all,
):
    me = spot[0]
    width = a0.shape[1]
    for j, (a, p) in enumerate(((a0, p0), (a1, p1), (a2, p2), (a3, p3))):
        here = pl.ds(pl.multiple_of((me ^ j) * width, width), width)
        att_all[:, here] = a[...]
        wo_all[here, :] = p[...]
    tokens = x.shape[0]
    half = tokens // 2
    curve = (2.0 / jnp.pi) ** 0.5
    for i in range(2):
        rows = pl.ds(i * half, half)
        value = x[rows, :].astype(F32) + dot(att_all[rows, :], wo_all[...]) + row(bo)
        mid[rows, :] = value
        normed, _ = normalize(value)
        second[rows, :] = (normed * row(g2) + row(s2)).astype(BF)
        pre = dot(second[rows, :], w1[...]) + row(b1)
        square = pre * pre
        bend = jnp.tanh(curve * (pre + 0.044715 * (pre * square)))
        upper = 0.5 * (1.0 + bend)
        hidden[rows, :] = (pre * upper).astype(BF)
        slope = upper + 0.5 * pre * (1.0 - bend * bend) * (curve * (1.0 + 0.134145 * square))
        gpre[rows, :] = (dot_nt(cot[rows, :], w2[...]) * slope).astype(BF)
    send_off(mid)
    core = me % 2
    mine = pl.ds(pl.multiple_of(core * half, half), half)
    other = pl.ds(pl.multiple_of((1 - core) * half, half), half)
    send[...] = dot_nt(gpre[other, :], w1[...]).astype(BF)
    keep[...] = dot_nt(gpre[mine, :], w1[...])


def halves(flag, rows):
    near = pl.ds(pl.multiple_of(flag * rows, rows), rows)
    return near, pl.ds(pl.multiple_of((1 - flag) * rows, rows), rows)


def mlp_grad_kernel(spot, second, hidden, gpre, cot, own1, away1, own2, away2, small, grads):
    part = own1.shape[0]
    mine, other = halves(spot[2], part)
    grads[...] = dot_tn(second[...], gpre[...]).astype(BF)
    own1[...] = grads[mine, :]
    away1[...] = grads[other, :]
    mine, other = halves(spot[3], part)
    grads[...] = dot_tn(hidden[...], cot[...]).astype(BF)
    own2[...] = grads[mine, :]
    away2[...] = grads[other, :]
    which = iota(small.shape, 0)
    first = jnp.sum(gpre[...].astype(F32), axis=0, keepdims=True)
    later = jnp.sum(cot[...].astype(F32), axis=0, keepdims=True)
    small[...] = jnp.where(which == 0, first, jnp.where(which == 1, later, 0.0)).astype(BF)


def attend_back_kernel(
    spot, s2a, s2b, mid, cot, g2, wo, v, probs, k, q, first, att, wq, wk, wv, g1, s1,
    gmid, own, to_y, to_z, to_yz, gq, gk, gv, scores, sums, norm1, gsec, gproj, gatt, pay,
):
    core, place_yz = spot[0] % 2, 2 * spot[2] + spot[3]
    tokens, width = cot.shape
    half = tokens // 2
    span = wq.shape[1]
    heads = span // HD
    blocks = tokens // BLOCK
    mine, other = halves(core, half)
    gsec[mine, :] = s2a[...].astype(F32)
    gsec[other, :] = s2b[...].astype(F32)
    gain_sum = jnp.zeros((1, width), F32)
    shift_sum = jnp.zeros((1, width), F32)
    proj_sum = jnp.zeros((1, width), F32)
    for b in range(blocks):
        rows = pl.ds(b * BLOCK, BLOCK)
        grad = gsec[rows, :]
        normed, inverse = normalize(mid[rows, :])
        gain_sum += jnp.sum(grad * normed, axis=0, keepdims=True)
        shift_sum += jnp.sum(grad, axis=0, keepdims=True)
        value = cot[rows, :].astype(F32) + norm_back(grad, normed, inverse, row(g2))
        gmid[rows, :] = value
        proj_sum += jnp.sum(value, axis=0, keepdims=True)
        gproj[rows, :] = value.astype(BF)
    gatt[...] = dot_nt(gproj[...], wo[...]).astype(BF)
    factor = HD ** (-0.5)
    score_sum = jnp.zeros((heads * BLOCK, BLOCK), F32)
    for b in range(blocks):
        rows = pl.ds(b * BLOCK, BLOCK)
        grads = by_head(gatt[rows, :], heads)
        prob = probs[b]
        grad = dot_nt(grads, v[rows, :])
        gv[rows, :] = dot_tn(prob.astype(BF), grads).astype(BF)
        inner = jnp.sum(prob * grad, axis=-1, keepdims=True)
        gscore = (prob * (grad - inner)).astype(BF)
        score_sum += gscore.astype(F32)
        gq[rows, :] = (factor * own_lanes(dot(gscore, k[rows, :]), heads)).astype(BF)
        gk[rows, :] = (factor * dot_tn(gscore, by_head(q[rows, :], heads))).astype(BF)
    scores[...] = score_sum
    shift = jnp.zeros((8, width), F32)
    gain = jnp.zeros((8, width), F32)
    ones = jnp.ones((8, span), BF)
    eight = iota((8, span), 0)
    mixed = dot_tn(first[...], jnp.concatenate([gq[...], gk[...], gv[...]], axis=1))
    for j, (part, weight) in enumerate(((gq, wq), (gk, wk), (gv, wv))):
        grads = mixed[:, j * span:(j + 1) * span]
        total = jnp.sum(part[...].astype(F32), axis=0, keepdims=True)
        if j != 1:
            at = 0 if j == 0 else span
            sums[3:4, at:at + span] = total
        coarse = total.astype(BF)
        fine = (total - coarse.astype(F32)).astype(BF)
        pair = jnp.where(eight == 0, coarse, jnp.where(eight == 1, fine, jnp.zeros_like(coarse)))
        shift += dot_nt(pair, weight[...])
        product = weight[...].astype(F32) * grads
        coarse = product.astype(BF)
        gain += dot_nt(ones, coarse) + dot_nt(ones, (product - coarse.astype(F32)).astype(BF))
        grads = grads.astype(BF)
        for i in range(width // span):
            pay[j * span:(j + 1) * span, i * span:(i + 1) * span] = grads[i * span:(i + 1) * span]
    pay[3 * span:4 * span, :] = dot_tn(att[...], gproj[...]).astype(BF)
    for ref, flip in ((own, 0), (to_y, 2), (to_z, 1), (to_yz, 3)):
        ref[...] = pay[pl.ds(pl.multiple_of((place_yz ^ flip) * span, span), span), :]
    sums[3:4, 2 * span:] = jnp.zeros((1, width - 2 * span), F32)
    which = iota((ROWS, width), 0)
    shift = shift[0:1, :] + shift[1:2, :]
    gain = (gain[0:1, :] - row(s1) * shift) / row(g1)
    norm1[...] = jnp.where(which == 0, gain, jnp.where(which == 1, shift, 0.0)).astype(BF)
    sums[0:1, :] = gain_sum
    sums[1:2, :] = shift_sum
    sums[2:3, :] = proj_sum


def attend_out_kernel(spot, after, also, gq, gk, gv, wq, wk, wv, keep, send):
    half = gq.shape[0] // 2
    for where, ref in zip(halves(spot[0] % 2, half), (keep, send)):
        ref[...] = (
            dot_nt(gq[where, :], wq[...])
            + dot_nt(gk[where, :], wk[...])
            + dot_nt(gv[where, :], wv[...])
        ).astype(BF)


def mlp_out_kernel(spot, hidden, w2, keep, send):
    for where, ref in zip(halves(spot[0] % 2, hidden.shape[0] // 2), (keep, send)):
        ref[...] = dot(hidden[where, :], w2[...]).astype(BF)


def sums_kernel(after, scores, sums, pidx, small, all_sums):
    heads = scores.shape[0] // BLOCK
    at = place(iota((BLOCK, WIN), 0)) == iota((BLOCK, WIN), 1)
    fold = at.astype(F32)
    lanes = heads * WIN
    folded = jnp.zeros((WIN, lanes), F32)
    for h in range(heads):
        lane = iota((BLOCK, lanes), 1)
        lay = ((place(iota((BLOCK, lanes), 0)) == lane % WIN) & (lane // WIN == h)).astype(F32)
        once = lax.dot_general(
            fold, scores[h * BLOCK:(h + 1) * BLOCK, :], (((0,), (0,)), ((), ())),
            precision=EXACT, preferred_element_type=F32,
        )
        folded += jnp.dot(once, lay, precision=EXACT, preferred_element_type=F32)
    index = jnp.concatenate([pidx[...]] * heads, axis=1)
    slots = 64
    slot = iota((slots, lanes), 0)
    by_offset = jnp.zeros((slots, lanes), F32)
    for o in range(49):
        total = jnp.sum(jnp.where(index == o, folded, 0.0), axis=0, keepdims=True)
        by_offset = jnp.where(slot == o, total, by_offset)
    pick = (iota((8, lanes), 1) // WIN == iota((8, lanes), 0)).astype(F32)
    offsets = lax.dot_general(
        pick, by_offset, (((1,), (1,)), ((), ())), precision=EXACT, preferred_element_type=F32
    )
    all_sums[...] = jnp.zeros_like(all_sums)
    all_sums[0:3, :] = sums[0:3, :]
    all_sums[3:4, :] = sums[3:4, :]
    all_sums[8:16, 0:slots] = offsets
    small[...] = all_sums[...].astype(BF)


def finish_kernel(spot, s4, r4, s2, r2, gmid, x, g1, mid, b2, layer_out, input_grad):
    core = spot[0] % 2
    half = x.shape[0] // 2
    for part, (ref, out) in enumerate(((s4, s2), (r4, r2))):
        start = core if part == 0 else 1 - core
        where = pl.ds(pl.multiple_of(start * half, half), half)
        normed, inverse = normalize(x[where, :].astype(F32))
        grad = ref[...].astype(F32)
        input_grad[where, :] = gmid[where, :] + norm_back(grad, normed, inverse, row(g1))
        mlp = out[...].astype(F32)
        layer_out[where, :] = mid[where, :] + mlp + row(b2)


def widen_kernel(spot, after, near1, far1, near2, far2, *others):
    w1, w2 = others[-2:]
    part = near1.shape[0]
    for flag, near, far, ref in ((spot[2], near1, far1, w1), (spot[3], near2, far2, w2)):
        mine, other = halves(flag, part)
        ref[mine, :] = near[...].astype(F32)
        ref[other, :] = far[...].astype(F32)
        send_off(ref)


def unpack_kernel(
    spot, after, near, from_y, from_z, from_yz,
    wq, wk, wv, wo, b1, b2, g2, s2, bo, bq, bv, rel, g1, s1, both,
):
    place_yz = 2 * spot[2] + spot[3]
    width = near.shape[1]
    span = wo.shape[0]
    for ref, flip in ((near, 0), (from_y, 2), (from_z, 1), (from_yz, 3)):
        both[place_yz ^ flip] = ref[0:span, :]
    for j, ref in enumerate((wq, wk, wv)):
        for i in range(width // span):
            block = both[j, :, i * span:(i + 1) * span]
            ref[i * span:(i + 1) * span, :] = block.astype(F32)
        send_off(ref)
    wo[...] = both[3].astype(F32)
    send_off(wo)
    sums = (near[span:, :].astype(F32) + from_y[span:, :].astype(F32)) + (
        from_z[span:, :].astype(F32) + from_yz[span:, :].astype(F32)
    )
    for at, ref in ((0, b1), (1, b2), (8, g2), (9, s2), (10, bo), (24, g1), (25, s1)):
        ref[...] = sums[at]
    bq[...] = sums[11, :span]
    bv[...] = sums[11, span:2 * span]
    rel[...] = sums[16:16 + rel.shape[0], :rel.shape[1]]


def swap(value, axis, bit, size):
    return lax.ppermute(value, axis, [(i, i ^ bit) for i in range(size)])


def shards(
    inputs,
    query_weight,
    key_weight,
    value_weight,
    query_bias,
    value_bias,
    position_bias,
    proj_weight,
    proj_bias,
    norm1_gain,
    norm1_shift,
    norm2_gain,
    norm2_shift,
    up_weight,
    up_bias,
    down_weight,
    down_bias,
    segment_ids,
    valid_mask,
    position_index,
    out_cotangent,
    dp,
    tensor,
):
    tokens, width = inputs.shape
    half = tokens // 2
    span = query_weight.shape[1]
    units = up_weight.shape[1]
    heads = span // HD
    blocks = tokens // BLOCK
    me = lax.axis_index("tensor")
    mate = lax.axis_index("dp")
    bits = [1 << i for i in range(dp.bit_length() - 1)]
    flags = [(mate >> i) & 1 for i in range(len(bits))]
    lower = [flag == 0 for flag in flags]
    sizes = [(width >> (i + 1)) * n for i in range(len(bits)) for n in (1, 2)]
    starts = {
        (i, size): (flags[i] * size).astype(jnp.uint32) for i in range(len(bits)) for size in sizes
    }
    stops = {
        at: ((1 - flags[at[0]]) * at[1]).astype(jnp.uint32) for at in starts
    }
    spot = jnp.stack(
        [me, mate]
        + flags
        + [flag.astype(jnp.int32) for flag in lower]
        + [at.astype(jnp.int32) for at in list(starts.values()) + list(stops.values())]
    )
    seg = segment_ids.reshape(1, tokens)
    valid = valid_mask.reshape(1, tokens)
    wide = (tokens, width)
    narrow = (tokens, span)

    wo_x = swap(proj_weight, "tensor", 2, tensor)
    wo_c = swap(proj_weight, "tensor", 1, tensor)
    wo_d = swap(wo_x, "tensor", 1, tensor)

    att, first, q, k, v, probs = call(
        attend_kernel,
        [
            (narrow, BF, "vmem"), (wide, BF, "vmem"), (narrow, BF, "vmem"), (narrow, BF, "vmem"),
            (narrow, BF, "vmem"), ((blocks, heads * BLOCK, BLOCK), F32, "vmem"),
        ],
        [
            (spot, "smem"), (inputs, "hbm"), (norm1_gain, "hbm"), (norm1_shift, "hbm"),
            (query_weight, "hbm"), (key_weight, "hbm"), (value_weight, "hbm"), (query_bias, "hbm"),
            (value_bias, "hbm"), (position_bias.T, "hbm"), (position_index, "hbm"), (seg, "hbm"),
            (valid, "hbm"),
        ],
        cost=20,
    )
    (
        _, inputs, norm1_gain, norm1_shift, position_index, query_weight, key_weight, value_weight,
        proj_weight, proj_bias, norm2_gain, norm2_shift, up_weight, up_bias, out_cotangent,
        down_weight, down_bias,
    ) = call(
        fetch_kernel,
        [((8, BLOCK), F32, "vmem")],
        [(att, "vmem"), (wo_x, "vmem")]
        + [
            (value, "hbm")
            for value in (
                inputs, norm1_gain, norm1_shift, position_index, query_weight, key_weight,
                value_weight, proj_weight, proj_bias, norm2_gain, norm2_shift, up_weight, up_bias,
                out_cotangent, down_weight, down_bias,
            )
        ],
        exports=tuple(range(2, 18)),
        cost=0,
    )
    att_x, down_bias = lax.optimization_barrier((swap(att, "tensor", 2, tensor), down_bias))
    att_c = swap(att, "tensor", 1, tensor)
    att_d = swap(att_x, "tensor", 1, tensor)

    mid, second, hidden, gpre, keep3, send3 = call(
        mlp_kernel,
        [
            (wide, F32, "vmem"), (wide, BF, "vmem"), ((tokens, units), BF, "vmem"),
            ((tokens, units), BF, "vmem"), ((half, width), F32, "vmem"), ((half, width), BF, "vmem"),
        ],
        [
            (spot, "smem"), (att, "vmem"), (att_c, "vmem"), (att_x, "vmem"), (att_d, "vmem"),
            (proj_weight, "vmem"), (wo_c, "vmem"), (wo_x, "vmem"), (wo_d, "vmem"),
            (inputs, "vmem"), (proj_bias, "vmem"), (norm2_gain, "vmem"), (norm2_shift, "vmem"),
            (up_weight, "vmem"), (up_bias, "vmem"), (out_cotangent, "vmem"), (down_weight, "vmem"),
        ],
        scratch=[((tokens, tensor * span), BF), ((tensor * span, width), BF)],
        cost=2,
    )

    def fold(value, other):
        return (value.astype(F32) + other.astype(F32)).astype(BF)

    own1, away1, own2, away2, small_a = call(
        mlp_grad_kernel,
        [((half, width), BF, "vmem")] * 4 + [((8, width), BF, "vmem")],
        [
            (spot, "smem"), (second, "vmem"), (hidden, "vmem"), (gpre, "vmem"),
            (out_cotangent, "vmem"),
        ],
        scratch=[((width, units), BF)],
        cost=2,
    )
    come3 = swap(send3, "tensor", 1, tensor)
    come3, small_a, away1, away2 = lax.optimization_barrier((come3, small_a, away1, away2))
    pair3 = fold(keep3, come3)
    keep2, send2 = call(
        mlp_out_kernel,
        [((half, width), BF, "vmem"), ((half, width), BF, "vmem")],
        [(spot, "smem"), (hidden, "vmem"), (down_weight, "vmem")],
        cost=1,
    )
    come3, come_a, come_b, keep2, send2 = lax.optimization_barrier(
        (
            swap(pair3, "tensor", 2, tensor),
            swap(away1, "dp", bits[0], dp),
            swap(away2, "dp", bits[1], dp),
            keep2,
            send2,
        )
    )
    sum3 = fold(pair3, come3)
    rest3 = swap(sum3, "tensor", 1, tensor)

    def meet(own, along_y, along_z, along_yz):
        return (
            own,
            swap(along_y, "dp", bits[0], dp),
            swap(along_z, "dp", bits[1], dp),
            swap(along_yz, "dp", bits[0] | bits[1], dp),
        )

    def combine(parts):
        own, y, z, yz = [part.astype(F32) for part in parts]
        return ((own + y) + (z + yz)).astype(BF)

    piece = ((span, width), BF, "vmem")
    gmid, att_own, att_y, att_z, att_yz, gq, gk, gv, scores, sums, norm1 = call(
        attend_back_kernel,
        [
            (wide, F32, "vmem"), piece, piece, piece, piece, (narrow, BF, "vmem"),
            (narrow, BF, "vmem"), (narrow, BF, "vmem"), ((heads * BLOCK, BLOCK), F32, "vmem"),
            ((8, width), F32, "vmem"), ((ROWS, width), BF, "vmem"),
        ],
        [
            (spot, "smem"), (sum3, "vmem"), (rest3, "vmem"), (mid, "vmem"),
            (out_cotangent, "vmem"), (norm2_gain, "vmem"), (proj_weight, "vmem"), (v, "vmem"),
            (probs, "vmem"), (k, "vmem"), (q, "vmem"), (first, "vmem"), (att, "vmem"),
            (query_weight, "vmem"), (key_weight, "vmem"), (value_weight, "vmem"),
            (norm1_gain, "vmem"), (norm1_shift, "vmem"),
        ],
        scratch=[(wide, F32), (wide, BF), (narrow, BF), ((4 * span, width), BF)],
        cost=1,
    )
    left = jnp.uint32(0)

    def pick(value, i):
        part = value.shape[0] // 2
        return (
            lax.dynamic_slice(value, (starts[i, part], left), (part, width)),
            lax.dynamic_slice(value, (stops[i, part], left), (part, width)),
        )

    def settle(value, times):
        for _ in range(times):
            mark = swap(value, "tensor", 1, tensor)
            value, mark = lax.optimization_barrier((value, mark))
            marks.append(mark)
        return value

    marks = []

    def scatter(value, i):
        own, away = pick(value, i)
        return fold(own, swap(away, "dp", bits[i], dp))

    def gather(own, i):
        other = swap(own, "dp", bits[i], dp)
        return jnp.where(
            lower[i], jnp.concatenate([own, other]), jnp.concatenate([other, own])
        )

    more = range(2, len(bits))

    keep_a, away_a = pick(fold(own1, come_a), 1)
    keep_b, away_b = pick(fold(own2, come_b), 0)
    (
        come_a, come_b, att_own, att_y, att_z, att_yz, gq, gk, gv, scores, sums, norm1,
    ) = lax.optimization_barrier(
        (
            swap(away_a, "dp", bits[1], dp), swap(away_b, "dp", bits[0], dp), att_own, att_y,
            att_z, att_yz, gq, gk, gv, scores, sums, norm1,
        )
    )
    mlp_chunk = jnp.concatenate([fold(keep_a, come_a), fold(keep_b, come_b)])
    pair2 = fold(keep2, swap(send2, "tensor", 1, tensor))
    sum2 = fold(pair2, swap(pair2, "tensor", 2, tensor))
    rest2 = swap(sum2, "tensor", 1, tensor)
    att_parts = meet(att_own, att_y, att_z, att_yz)
    chunk = combine(att_parts)
    across = [swap(norm1, "tensor", flip, tensor).astype(F32) for flip in (1, 2, 3)]
    norm1 = ((norm1.astype(F32) + across[0]) + (across[1] + across[2])).astype(BF)
    (small_b,) = call(
        sums_kernel,
        [((16, width), BF, "vmem")],
        [(att_own, "vmem"), (scores, "vmem"), (sums, "vmem"), (position_index, "vmem")],
        scratch=[((16, width), F32)],
        cost=1,
    )
    keep4, send4 = call(
        attend_out_kernel,
        [((half, width), BF, "vmem"), ((half, width), BF, "vmem")],
        [
            (spot, "smem"), (chunk, "vmem"), (sum2, "vmem"), (gq, "vmem"), (gk, "vmem"), (gv, "vmem"),
            (query_weight, "vmem"), (key_weight, "vmem"), (value_weight, "vmem"),
        ],
        cost=1,
    )

    pair4 = fold(keep4, swap(send4, "tensor", 1, tensor))
    sum4 = fold(pair4, swap(pair4, "tensor", 2, tensor))
    rest4 = swap(sum4, "tensor", 1, tensor)

    for i in more:
        mlp_chunk = fold(mlp_chunk, swap(mlp_chunk, "dp", bits[i], dp))
    mlp_chunk = settle(mlp_chunk, 0)
    chunk = jnp.concatenate([chunk, small_a, small_b, norm1[:8]])
    for i in more:
        chunk = fold(chunk, swap(chunk, "dp", bits[i], dp))
    chunk = settle(chunk, 1)
    chunks = meet(chunk, chunk, chunk, chunk)
    near1 = gather(mlp_chunk[:mlp_chunk.shape[0] // 2], 1)
    near2 = gather(mlp_chunk[mlp_chunk.shape[0] // 2:], 0)
    far1 = swap(near1, "dp", bits[0], dp)
    far2 = swap(near2, "dp", bits[1], dp)
    layer_out, input_grad = call(
        finish_kernel,
        [(wide, F32, "hbm"), (wide, F32, "hbm")],
        [
            (spot, "smem"), (sum4, "vmem"), (rest4, "vmem"), (sum2, "vmem"), (rest2, "vmem"), (gmid, "vmem"), (inputs, "vmem"),
            (norm1_gain, "vmem"), (mid, "vmem"), (down_bias, "vmem"),
        ],
        cost=2,
    )
    w1_total, w2_total = call(
        widen_kernel,
        [((width, units), F32, "hbm"), ((units, width), F32, "hbm")],
        [(spot, "smem"), (layer_out, "keep")]
        + [(value, "vmem") for value in [near1, far1, near2, far2] + marks],
    )
    vector, short = ((width,), F32, "hbm"), ((span,), F32, "hbm")
    (
        wq_total, wk_total, wv_total, wo_total, b1_total, b2_total, g2_total, s2_total, bo_total,
        bq_total, bv_total, rel_total, g1_total, s1_total,
    ) = call(
        unpack_kernel,
        [
            ((width, span), F32, "hbm"), ((width, span), F32, "hbm"), ((width, span), F32, "hbm"),
            ((span, width), F32, "hbm"), vector, vector, vector, vector, vector, short, short,
            ((heads, position_bias.shape[0]), F32, "hbm"), vector, vector,
        ],
        [(spot, "smem"), (w1_total, "keep")] + [(value, "vmem") for value in chunks],
        scratch=[((4, span, width), BF)],
    )
    rel_total = rel_total.T

    return (
        layer_out,
        input_grad,
        wq_total,
        wk_total,
        wv_total,
        bq_total,
        bv_total,
        rel_total,
        wo_total,
        bo_total,
        g1_total,
        s1_total,
        g2_total,
        s2_total,
        w1_total,
        b1_total,
        w2_total,
        b2_total,
    )


def solution(mesh):
    dp, tensor = mesh.shape["dp"], mesh.shape["tensor"]

    def body(*args):
        return shards(*args, dp=dp, tensor=tensor)

    column, line, whole = P(None, "tensor"), P("tensor"), P()
    return jax.shard_map(
        body,
        mesh=mesh,
        in_specs=(
            P("dp", None),
            column,
            column,
            column,
            line,
            line,
            column,
            P("tensor", None),
            whole,
            whole,
            whole,
            whole,
            whole,
            column,
            line,
            P("tensor", None),
            whole,
            P("dp", None),
            P("dp", None),
            whole,
            P("dp", None),
        ),
        out_specs=(
            P("dp", None),
            P("dp", None),
            column,
            column,
            column,
            line,
            line,
            column,
            P("tensor", None),
            whole,
            whole,
            whole,
            whole,
            whole,
            column,
            line,
            P("tensor", None),
            whole,
        ),
        check_vma=False,
    )
```

```python
import jax
import jax.numpy as jnp
from jax import lax
from jax.experimental import pallas as pl
from jax.experimental.pallas import tpu as pltpu
from jax.sharding import PartitionSpec as P

HD = 32
GW = 8
WS = 4
WIN = WS * WS
BLOCK = 128
NEG_FILL = -1e30
BF = jnp.bfloat16
F32 = jnp.float32
EXACT = lax.Precision.HIGHEST
VMEM_BYTES = 24 * 1024 * 1024
ROWS = 16


def dot(left, right):
    return jnp.dot(left, right, preferred_element_type=F32)


def dot_nt(left, right):
    return lax.dot_general(left, right, (((1,), (1,)), ((), ())), preferred_element_type=F32)


def dot_tn(left, right):
    return lax.dot_general(left, right, (((0,), (0,)), ((), ())), preferred_element_type=F32)


def exact_nt(left, right):
    return lax.dot_general(
        left, right, (((1,), (1,)), ((), ())), precision=EXACT, preferred_element_type=F32
    )


def normalize(value):
    centre = value - jnp.mean(value, axis=-1, keepdims=True)
    spread = jnp.mean(centre * centre, axis=-1, keepdims=True)
    inverse = lax.rsqrt(spread + 1e-06)
    return centre * inverse, inverse


def norm_back(grad_out, normed, inverse, gain):
    scaled = grad_out * gain
    first_mean = jnp.mean(scaled, axis=-1, keepdims=True)
    second_mean = jnp.mean(scaled * normed, axis=-1, keepdims=True)
    return inverse * (scaled - first_mean - normed * second_mean)


def row(ref):
    return ref[...].reshape(1, -1)


def iota(shape, axis):
    return lax.broadcasted_iota(jnp.int32, shape, axis)


def place(token):
    return (token // GW) % WS * WS + token % WS


def window(token):
    return token // (GW * WS) * (GW // WS) + token % GW // WS


def by_head(value, heads):
    head = iota(value.shape, 1) // HD
    return jnp.concatenate(
        [jnp.where(head == h, value, jnp.zeros_like(value)) for h in range(heads)]
    )


def own_lanes(value, heads):
    rows = value.shape[0] // heads
    head = iota((rows, value.shape[1]), 1) // HD
    total = value[:rows]
    for h in range(1, heads):
        total = jnp.where(head == h, value[h * rows:(h + 1) * rows], total)
    return total


class Loaded:
    def __init__(self, source, buffer, sem):
        self.buffer, self.shape, self.dtype = buffer, source.shape, source.dtype
        self.copy, self.started = pltpu.make_async_copy(source, buffer, sem), False

    def start(self):
        if not self.started:
            self.copy.start()
            self.started = True

    def wait(self):
        if self.copy is not None:
            self.start()
            self.copy.wait()
            self.copy = None

    def __getitem__(self, at):
        self.wait()
        return self.buffer[at]


class Stored:
    def __init__(self, buffer, target, sem):
        self.buffer, self.shape, self.dtype = buffer, target.shape, target.dtype
        self.copy, self.sent = pltpu.make_async_copy(buffer, target, sem), False

    def __getitem__(self, at):
        return self.buffer[at]

    def __setitem__(self, at, value):
        self.buffer[at] = value

    def send(self):
        if not self.sent:
            self.copy.start()
            self.sent = True


def send_off(ref):
    if isinstance(ref, Stored):
        ref.send()


def call(kernel, outs, args, scratch=(), cost=0, exports=(), later=()):
    spaces = {"smem": pltpu.SMEM, "vmem": pltpu.VMEM, "hbm": pltpu.HBM, "hsmem": pltpu.HBM}
    spaces["keep"] = pltpu.HBM
    plain = len(outs)
    outs = list(outs) + [(args[i][0].shape, args[i][0].dtype, "vmem") for i in exports]
    loads = [i for i, (_, where) in enumerate(args) if where[0] == "h"]
    stores = [i for i, (_, _, where) in enumerate(outs) if where == "hbm"]
    shapes = [jax.ShapeDtypeStruct(shape, dtype) for shape, dtype, _ in outs]
    pinned = [spaces[where](shape, dtype) for shape, dtype, where in outs]
    operands = [
        pltpu.with_memory_space_constraint(a, pltpu.HBM) if spaces[where] == pltpu.HBM else a
        for a, where in args
    ]
    buffers = []
    for i in loads:
        if i in exports:
            continue
        array, where = args[i]
        space = pltpu.SMEM if where == "hsmem" else pltpu.VMEM
        buffers.append(space(array.shape, array.dtype))
    buffers += [pltpu.VMEM(outs[i][0], outs[i][1]) for i in stores]
    sems = [pltpu.SemaphoreType.DMA] * (len(loads) + len(stores))

    def body(*refs):
        refs = list(refs)
        ins, rest = refs[:len(args)], refs[len(args):]
        results, rest = rest[:len(outs)], rest[len(outs):]
        own, rest = rest[:len(scratch)], rest[len(scratch):]
        holds, marks = list(rest[:len(buffers)]), list(rest[len(buffers):])
        given = dict(zip(exports, results[plain:]))
        for i in loads:
            hold = given[i] if i in given else holds.pop(0)
            ins[i] = Loaded(ins[i], hold, marks.pop(0))
            if i not in later:
                ins[i].start()
        for i in stores:
            results[i] = Stored(holds.pop(0), results[i], marks.pop(0))
        kernel(*ins, *results[:plain], *own)
        for i in loads:
            ins[i].wait()
        for i in stores:
            results[i].send()
        for i in stores:
            results[i].copy.wait()

    return pl.pallas_call(
        body,
        name=kernel.__name__,
        out_shape=pinned,
        in_specs=[pl.BlockSpec(memory_space=spaces[where]) for _, where in args],
        out_specs=[pl.BlockSpec(memory_space=spaces[where]) for _, _, where in outs],
        scratch_shapes=[pltpu.VMEM(shape, dtype) for shape, dtype in scratch] + buffers + sems,
        compiler_params=pltpu.CompilerParams(vmem_limit_bytes=VMEM_BYTES),
        cost_estimate=pl.CostEstimate(flops=cost * 10 ** 9, bytes_accessed=0, transcendentals=0),
    )(*operands)


def attend_kernel(
    spot, x, g1, s1, wq, wk, wv, bq, bv, rel, pidx, seg, valid, att, first, q, k, v, probs,
):
    tokens, span = x.shape[0], wq.shape[1]
    heads = span // HD
    blocks = tokens // BLOCK
    for b in range(blocks):
        rows = pl.ds(b * BLOCK, BLOCK)
        normed, _ = normalize(x[rows, :].astype(F32))
        first[rows, :] = (normed * row(g1) + row(s1)).astype(BF)
    weights = jnp.concatenate([wq[...], wk[...], wv[...]], axis=1)
    for i in range(2):
        rows = pl.ds(i * (tokens // 2), tokens // 2)
        mixed = dot(first[rows, :], weights)
        q[rows, :] = (mixed[:, :span] + row(bq)).astype(BF)
        k[rows, :] = mixed[:, span:2 * span].astype(BF)
        v[rows, :] = (mixed[:, 2 * span:] + row(bv)).astype(BF)
    lanes = 2 * heads * WIN
    group = heads * WIN
    table = rel[...]
    coarse = table.astype(BF)
    fine = (table - coarse.astype(F32)).astype(BF)
    lane = iota((heads, lanes), 1)
    mine = lane % group // WIN == iota((heads, lanes), 0)
    rows_by_offset = dot_tn(coarse, (mine & (lane < group)).astype(BF)) + dot_tn(
        fine, (mine & (lane >= group)).astype(BF)
    )
    index = jnp.concatenate([pidx[...]] * (2 * heads), axis=1)
    terms = jnp.zeros((WIN, lanes), F32)
    for o in range(rel.shape[1]):
        terms = jnp.where(index == o, rows_by_offset[o:o + 1, :], terms)
    spread = (place(iota((BLOCK, WIN), 0)) == iota((BLOCK, WIN), 1)).astype(BF)
    terms = dot(spread, terms.astype(BF)).astype(BF)
    lane = iota((lanes, BLOCK), 0)
    here = lane % WIN == place(iota((lanes, BLOCK), 1))
    bias = jnp.concatenate(
        [dot(terms, (here & (lane % group // WIN == h)).astype(BF)) for h in range(heads)]
    )
    query_at, key_at = iota((BLOCK, BLOCK), 0), iota((BLOCK, BLOCK), 1)
    near = window(query_at) == window(key_at)
    selfs = query_at == key_at
    factor = HD ** (-0.5)
    for b in range(blocks):
        rows = pl.ds(b * BLOCK, BLOCK)
        seg_keys = jnp.broadcast_to(seg[:, rows].astype(F32), (BLOCK, BLOCK))
        valid_keys = jnp.broadcast_to(valid[:, rows], (BLOCK, BLOCK)) > 0
        allowed = near & (seg_keys == seg_keys.T) & (valid_keys | selfs)
        wall = jnp.where(allowed, 0.0, NEG_FILL)
        scores = dot_nt(by_head(q[rows, :], heads), k[rows, :]) * factor + bias
        scores = jnp.where(jnp.concatenate([wall] * heads) < 0.0, NEG_FILL, scores)
        expo = jnp.exp(scores - jnp.max(scores, axis=-1, keepdims=True))
        prob = expo * (1.0 / jnp.sum(expo, axis=-1, keepdims=True))
        probs[b] = prob
        att[rows, :] = own_lanes(dot(prob.astype(BF), v[rows, :]), heads).astype(BF)


def fetch_kernel(after, also, *operands):
    for ref in operands[:-1]:
        ref.wait()
    operands[-1][...] = jnp.zeros_like(operands[-1])


def mlp_kernel(
    spot, a0, a1, a2, a3, p0, p1, p2, p3, x, bo, g2, s2, w1, b1, cot, w2,
    mid, second, hidden, gpre, keep, send, att_all, wo_all,
):
    me = spot[0]
    width = a0.shape[1]
    for j, (a, p) in enumerate(((a0, p0), (a1, p1), (a2, p2), (a3, p3))):
        here = pl.ds(pl.multiple_of((me ^ j) * width, width), width)
        att_all[:, here] = a[...]
        wo_all[here, :] = p[...]
    tokens = x.shape[0]
    half = tokens // 2
    curve = (2.0 / jnp.pi) ** 0.5
    for i in range(2):
        rows = pl.ds(i * half, half)
        value = x[rows, :].astype(F32) + dot(att_all[rows, :], wo_all[...]) + row(bo)
        mid[rows, :] = value
        normed, _ = normalize(value)
        second[rows, :] = (normed * row(g2) + row(s2)).astype(BF)
        pre = dot(second[rows, :], w1[...]) + row(b1)
        square = pre * pre
        bend = jnp.tanh(curve * (pre + 0.044715 * (pre * square)))
        upper = 0.5 * (1.0 + bend)
        hidden[rows, :] = (pre * upper).astype(BF)
        slope = upper + 0.5 * pre * (1.0 - bend * bend) * (curve * (1.0 + 0.134145 * square))
        gpre[rows, :] = (dot_nt(cot[rows, :], w2[...]) * slope).astype(BF)
    send_off(mid)
    core = me % 2
    mine = pl.ds(pl.multiple_of(core * half, half), half)
    other = pl.ds(pl.multiple_of((1 - core) * half, half), half)
    send[...] = dot_nt(gpre[other, :], w1[...]).astype(BF)
    keep[...] = dot_nt(gpre[mine, :], w1[...])


def halves(flag, rows):
    near = pl.ds(pl.multiple_of(flag * rows, rows), rows)
    return near, pl.ds(pl.multiple_of((1 - flag) * rows, rows), rows)


def mlp_grad_kernel(spot, second, hidden, gpre, cot, own1, away1, own2, away2, small, grads):
    part = own1.shape[0]
    mine, other = halves(spot[2], part)
    grads[...] = dot_tn(second[...], gpre[...]).astype(BF)
    own1[...] = grads[mine, :]
    away1[...] = grads[other, :]
    mine, other = halves(spot[3], part)
    grads[...] = dot_tn(hidden[...], cot[...]).astype(BF)
    own2[...] = grads[mine, :]
    away2[...] = grads[other, :]
    which = iota(small.shape, 0)
    first = jnp.sum(gpre[...].astype(F32), axis=0, keepdims=True)
    later = jnp.sum(cot[...].astype(F32), axis=0, keepdims=True)
    small[...] = jnp.where(which == 0, first, jnp.where(which == 1, later, 0.0)).astype(BF)


def attend_back_kernel(
    spot, s2a, s2b, mid, cot, g2, wo, v, probs, k, q, first, att, wq, wk, wv, g1, s1,
    gmid, own, to_y, to_z, to_yz, gq, gk, gv, scores, sums, norm1, gsec, gproj, gatt, pay,
):
    core, place_yz = spot[0] % 2, 2 * spot[2] + spot[3]
    tokens, width = cot.shape
    half = tokens // 2
    span = wq.shape[1]
    heads = span // HD
    blocks = tokens // BLOCK
    mine, other = halves(core, half)
    gsec[mine, :] = s2a[...].astype(F32)
    gsec[other, :] = s2b[...].astype(F32)
    gain_sum = jnp.zeros((1, width), F32)
    shift_sum = jnp.zeros((1, width), F32)
    proj_sum = jnp.zeros((1, width), F32)
    for b in range(blocks):
        rows = pl.ds(b * BLOCK, BLOCK)
        grad = gsec[rows, :]
        normed, inverse = normalize(mid[rows, :])
        gain_sum += jnp.sum(grad * normed, axis=0, keepdims=True)
        shift_sum += jnp.sum(grad, axis=0, keepdims=True)
        value = cot[rows, :].astype(F32) + norm_back(grad, normed, inverse, row(g2))
        gmid[rows, :] = value
        proj_sum += jnp.sum(value, axis=0, keepdims=True)
        gproj[rows, :] = value.astype(BF)
    gatt[...] = dot_nt(gproj[...], wo[...]).astype(BF)
    factor = HD ** (-0.5)
    score_sum = jnp.zeros((heads * BLOCK, BLOCK), F32)
    for b in range(blocks):
        rows = pl.ds(b * BLOCK, BLOCK)
        grads = by_head(gatt[rows, :], heads)
        prob = probs[b]
        grad = dot_nt(grads, v[rows, :])
        gv[rows, :] = dot_tn(prob.astype(BF), grads).astype(BF)
        inner = jnp.sum(prob * grad, axis=-1, keepdims=True)
        gscore = (prob * (grad - inner)).astype(BF)
        score_sum += gscore.astype(F32)
        gq[rows, :] = (factor * own_lanes(dot(gscore, k[rows, :]), heads)).astype(BF)
        gk[rows, :] = (factor * dot_tn(gscore, by_head(q[rows, :], heads))).astype(BF)
    scores[...] = score_sum
    shift = jnp.zeros((8, width), F32)
    gain = jnp.zeros((8, width), F32)
    ones = jnp.ones((8, span), BF)
    eight = iota((8, span), 0)
    mixed = dot_tn(first[...], jnp.concatenate([gq[...], gk[...], gv[...]], axis=1))
    for j, (part, weight) in enumerate(((gq, wq), (gk, wk), (gv, wv))):
        grads = mixed[:, j * span:(j + 1) * span]
        total = jnp.sum(part[...].astype(F32), axis=0, keepdims=True)
        if j != 1:
            at = 0 if j == 0 else span
            sums[3:4, at:at + span] = total
        coarse = total.astype(BF)
        fine = (total - coarse.astype(F32)).astype(BF)
        pair = jnp.where(eight == 0, coarse, jnp.where(eight == 1, fine, jnp.zeros_like(coarse)))
        shift += dot_nt(pair, weight[...])
        product = weight[...].astype(F32) * grads
        coarse = product.astype(BF)
        gain += dot_nt(ones, coarse) + dot_nt(ones, (product - coarse.astype(F32)).astype(BF))
        grads = grads.astype(BF)
        for i in range(width // span):
            pay[j * span:(j + 1) * span, i * span:(i + 1) * span] = grads[i * span:(i + 1) * span]
    pay[3 * span:4 * span, :] = dot_tn(att[...], gproj[...]).astype(BF)
    for ref, flip in ((own, 0), (to_y, 2), (to_z, 1), (to_yz, 3)):
        ref[...] = pay[pl.ds(pl.multiple_of((place_yz ^ flip) * span, span), span), :]
    sums[3:4, 2 * span:] = jnp.zeros((1, width - 2 * span), F32)
    which = iota((ROWS, width), 0)
    shift = shift[0:1, :] + shift[1:2, :]
    gain = (gain[0:1, :] - row(s1) * shift) / row(g1)
    norm1[...] = jnp.where(which == 0, gain, jnp.where(which == 1, shift, 0.0)).astype(BF)
    sums[0:1, :] = gain_sum
    sums[1:2, :] = shift_sum
    sums[2:3, :] = proj_sum


def attend_out_kernel(spot, after, also, gq, gk, gv, wq, wk, wv, keep, send):
    half = gq.shape[0] // 2
    for where, ref in zip(halves(spot[0] % 2, half), (keep, send)):
        ref[...] = (
            dot_nt(gq[where, :], wq[...])
            + dot_nt(gk[where, :], wk[...])
            + dot_nt(gv[where, :], wv[...])
        ).astype(BF)


def mlp_out_kernel(spot, hidden, w2, keep, send):
    for where, ref in zip(halves(spot[0] % 2, hidden.shape[0] // 2), (keep, send)):
        ref[...] = dot(hidden[where, :], w2[...]).astype(BF)


def sums_kernel(after, scores, sums, pidx, small, all_sums):
    heads = scores.shape[0] // BLOCK
    at = place(iota((BLOCK, WIN), 0)) == iota((BLOCK, WIN), 1)
    fold = at.astype(F32)
    lanes = heads * WIN
    folded = jnp.zeros((WIN, lanes), F32)
    for h in range(heads):
        lane = iota((BLOCK, lanes), 1)
        lay = ((place(iota((BLOCK, lanes), 0)) == lane % WIN) & (lane // WIN == h)).astype(F32)
        once = lax.dot_general(
            fold, scores[h * BLOCK:(h + 1) * BLOCK, :], (((0,), (0,)), ((), ())),
            precision=EXACT, preferred_element_type=F32,
        )
        folded += jnp.dot(once, lay, precision=EXACT, preferred_element_type=F32)
    index = jnp.concatenate([pidx[...]] * heads, axis=1)
    slots = 64
    slot = iota((slots, lanes), 0)
    by_offset = jnp.zeros((slots, lanes), F32)
    for o in range(49):
        total = jnp.sum(jnp.where(index == o, folded, 0.0), axis=0, keepdims=True)
        by_offset = jnp.where(slot == o, total, by_offset)
    pick = (iota((8, lanes), 1) // WIN == iota((8, lanes), 0)).astype(F32)
    offsets = lax.dot_general(
        pick, by_offset, (((1,), (1,)), ((), ())), precision=EXACT, preferred_element_type=F32
    )
    all_sums[...] = jnp.zeros_like(all_sums)
    all_sums[0:3, :] = sums[0:3, :]
    all_sums[3:4, :] = sums[3:4, :]
    all_sums[8:16, 0:slots] = offsets
    small[...] = all_sums[...].astype(BF)


def finish_kernel(spot, s4, r4, s2, r2, gmid, x, g1, mid, b2, layer_out, input_grad):
    core = spot[0] % 2
    half = x.shape[0] // 2
    for part, (ref, out) in enumerate(((s4, s2), (r4, r2))):
        start = core if part == 0 else 1 - core
        where = pl.ds(pl.multiple_of(start * half, half), half)
        normed, inverse = normalize(x[where, :].astype(F32))
        grad = ref[...].astype(F32)
        input_grad[where, :] = gmid[where, :] + norm_back(grad, normed, inverse, row(g1))
        mlp = out[...].astype(F32)
        layer_out[where, :] = mid[where, :] + mlp + row(b2)


def widen_kernel(spot, after, near1, far1, near2, far2, *others):
    w1, w2 = others[-2:]
    part = near1.shape[0]
    for flag, near, far, ref in ((spot[2], near1, far1, w1), (spot[3], near2, far2, w2)):
        mine, other = halves(flag, part)
        ref[mine, :] = near[...].astype(F32)
        ref[other, :] = far[...].astype(F32)
        send_off(ref)


def unpack_kernel(
    spot, after, near, from_y, from_z, from_yz,
    wq, wk, wv, wo, b1, b2, g2, s2, bo, bq, bv, rel, g1, s1, both,
):
    place_yz = 2 * spot[2] + spot[3]
    width = near.shape[1]
    span = wo.shape[0]
    for ref, flip in ((near, 0), (from_y, 2), (from_z, 1), (from_yz, 3)):
        both[place_yz ^ flip] = ref[0:span, :]
    for j, ref in enumerate((wq, wk, wv)):
        for i in range(width // span):
            block = both[j, :, i * span:(i + 1) * span]
            ref[i * span:(i + 1) * span, :] = block.astype(F32)
        send_off(ref)
    wo[...] = both[3].astype(F32)
    send_off(wo)
    sums = (near[span:, :].astype(F32) + from_y[span:, :].astype(F32)) + (
        from_z[span:, :].astype(F32) + from_yz[span:, :].astype(F32)
    )
    for at, ref in ((0, b1), (1, b2), (8, g2), (9, s2), (10, bo), (24, g1), (25, s1)):
        ref[...] = sums[at]
    bq[...] = sums[11, :span]
    bv[...] = sums[11, span:2 * span]
    rel[...] = sums[16:16 + rel.shape[0], :rel.shape[1]]


def swap(value, axis, bit, size):
    return lax.ppermute(value, axis, [(i, i ^ bit) for i in range(size)])


def shards(
    inputs,
    query_weight,
    key_weight,
    value_weight,
    query_bias,
    value_bias,
    position_bias,
    proj_weight,
    proj_bias,
    norm1_gain,
    norm1_shift,
    norm2_gain,
    norm2_shift,
    up_weight,
    up_bias,
    down_weight,
    down_bias,
    segment_ids,
    valid_mask,
    position_index,
    out_cotangent,
    dp,
    tensor,
):
    tokens, width = inputs.shape
    half = tokens // 2
    span = query_weight.shape[1]
    units = up_weight.shape[1]
    heads = span // HD
    blocks = tokens // BLOCK
    me = lax.axis_index("tensor")
    mate = lax.axis_index("dp")
    bits = [1 << i for i in range(dp.bit_length() - 1)]
    flags = [(mate >> i) & 1 for i in range(len(bits))]
    lower = [flag == 0 for flag in flags]
    sizes = [(width >> (i + 1)) * n for i in range(len(bits)) for n in (1, 2)]
    starts = {
        (i, size): (flags[i] * size).astype(jnp.uint32) for i in range(len(bits)) for size in sizes
    }
    stops = {
        at: ((1 - flags[at[0]]) * at[1]).astype(jnp.uint32) for at in starts
    }
    spot = jnp.stack(
        [me, mate]
        + flags
        + [flag.astype(jnp.int32) for flag in lower]
        + [at.astype(jnp.int32) for at in list(starts.values()) + list(stops.values())]
    )
    seg = segment_ids.reshape(1, tokens)
    valid = valid_mask.reshape(1, tokens)
    wide = (tokens, width)
    narrow = (tokens, span)

    wo_x = swap(proj_weight, "tensor", 2, tensor)
    wo_c = swap(proj_weight, "tensor", 1, tensor)
    wo_d = swap(wo_x, "tensor", 1, tensor)

    att, first, q, k, v, probs = call(
        attend_kernel,
        [
            (narrow, BF, "vmem"), (wide, BF, "vmem"), (narrow, BF, "vmem"), (narrow, BF, "vmem"),
            (narrow, BF, "vmem"), ((blocks, heads * BLOCK, BLOCK), F32, "vmem"),
        ],
        [
            (spot, "smem"), (inputs, "hbm"), (norm1_gain, "hbm"), (norm1_shift, "hbm"),
            (query_weight, "hbm"), (key_weight, "hbm"), (value_weight, "hbm"), (query_bias, "hbm"),
            (value_bias, "hbm"), (position_bias.T, "hbm"), (position_index, "hbm"), (seg, "hbm"),
            (valid, "hbm"),
        ],
        cost=20,
    )
    (
        _, inputs, norm1_gain, norm1_shift, position_index, query_weight, key_weight, value_weight,
        proj_weight, proj_bias, norm2_gain, norm2_shift, up_weight, up_bias, out_cotangent,
        down_weight, down_bias,
    ) = call(
        fetch_kernel,
        [((8, BLOCK), F32, "vmem")],
        [(att, "vmem"), (wo_x, "vmem")]
        + [
            (value, "hbm")
            for value in (
                inputs, norm1_gain, norm1_shift, position_index, query_weight, key_weight,
                value_weight, proj_weight, proj_bias, norm2_gain, norm2_shift, up_weight, up_bias,
                out_cotangent, down_weight, down_bias,
            )
        ],
        exports=tuple(range(2, 18)),
        cost=0,
    )
    att_x, down_bias = lax.optimization_barrier((swap(att, "tensor", 2, tensor), down_bias))
    att_c = swap(att, "tensor", 1, tensor)
    att_d = swap(att_x, "tensor", 1, tensor)

    mid, second, hidden, gpre, keep3, send3 = call(
        mlp_kernel,
        [
            (wide, F32, "vmem"), (wide, BF, "vmem"), ((tokens, units), BF, "vmem"),
            ((tokens, units), BF, "vmem"), ((half, width), F32, "vmem"), ((half, width), BF, "vmem"),
        ],
        [
            (spot, "smem"), (att, "vmem"), (att_c, "vmem"), (att_x, "vmem"), (att_d, "vmem"),
            (proj_weight, "vmem"), (wo_c, "vmem"), (wo_x, "vmem"), (wo_d, "vmem"),
            (inputs, "vmem"), (proj_bias, "vmem"), (norm2_gain, "vmem"), (norm2_shift, "vmem"),
            (up_weight, "vmem"), (up_bias, "vmem"), (out_cotangent, "vmem"), (down_weight, "vmem"),
        ],
        scratch=[((tokens, tensor * span), BF), ((tensor * span, width), BF)],
        cost=2,
    )

    def fold(value, other):
        return (value.astype(F32) + other.astype(F32)).astype(BF)

    own1, away1, own2, away2, small_a = call(
        mlp_grad_kernel,
        [((half, width), BF, "vmem")] * 4 + [((8, width), BF, "vmem")],
        [
            (spot, "smem"), (second, "vmem"), (hidden, "vmem"), (gpre, "vmem"),
            (out_cotangent, "vmem"),
        ],
        scratch=[((width, units), BF)],
        cost=2,
    )
    come3 = swap(send3, "tensor", 1, tensor)
    come3, small_a, away1, away2 = lax.optimization_barrier((come3, small_a, away1, away2))
    pair3 = fold(keep3, come3)
    keep2, send2 = call(
        mlp_out_kernel,
        [((half, width), BF, "vmem"), ((half, width), BF, "vmem")],
        [(spot, "smem"), (hidden, "vmem"), (down_weight, "vmem")],
        cost=1,
    )
    come3, come_a, come_b, keep2, send2 = lax.optimization_barrier(
        (
            swap(pair3, "tensor", 2, tensor),
            swap(away1, "dp", bits[0], dp),
            swap(away2, "dp", bits[1], dp),
            keep2,
            send2,
        )
    )
    sum3 = fold(pair3, come3)
    rest3 = swap(sum3, "tensor", 1, tensor)

    def meet(own, along_y, along_z, along_yz):
        return (
            own,
            swap(along_y, "dp", bits[0], dp),
            swap(along_z, "dp", bits[1], dp),
            swap(along_yz, "dp", bits[0] | bits[1], dp),
        )

    def combine(parts):
        own, y, z, yz = [part.astype(F32) for part in parts]
        return ((own + y) + (z + yz)).astype(BF)

    piece = ((span, width), BF, "vmem")
    gmid, att_own, att_y, att_z, att_yz, gq, gk, gv, scores, sums, norm1 = call(
        attend_back_kernel,
        [
            (wide, F32, "vmem"), piece, piece, piece, piece, (narrow, BF, "vmem"),
            (narrow, BF, "vmem"), (narrow, BF, "vmem"), ((heads * BLOCK, BLOCK), F32, "vmem"),
            ((8, width), F32, "vmem"), ((ROWS, width), BF, "vmem"),
        ],
        [
            (spot, "smem"), (sum3, "vmem"), (rest3, "vmem"), (mid, "vmem"),
            (out_cotangent, "vmem"), (norm2_gain, "vmem"), (proj_weight, "vmem"), (v, "vmem"),
            (probs, "vmem"), (k, "vmem"), (q, "vmem"), (first, "vmem"), (att, "vmem"),
            (query_weight, "vmem"), (key_weight, "vmem"), (value_weight, "vmem"),
            (norm1_gain, "vmem"), (norm1_shift, "vmem"),
        ],
        scratch=[(wide, F32), (wide, BF), (narrow, BF), ((4 * span, width), BF)],
        cost=1,
    )
    left = jnp.uint32(0)

    def pick(value, i):
        part = value.shape[0] // 2
        return (
            lax.dynamic_slice(value, (starts[i, part], left), (part, width)),
            lax.dynamic_slice(value, (stops[i, part], left), (part, width)),
        )

    def settle(value, times):
        for _ in range(times):
            mark = swap(value, "tensor", 1, tensor)
            value, mark = lax.optimization_barrier((value, mark))
            marks.append(mark)
        return value

    marks = []

    def scatter(value, i):
        own, away = pick(value, i)
        return fold(own, swap(away, "dp", bits[i], dp))

    def gather(own, i):
        other = swap(own, "dp", bits[i], dp)
        return jnp.where(
            lower[i], jnp.concatenate([own, other]), jnp.concatenate([other, own])
        )

    more = range(2, len(bits))

    keep_a, away_a = pick(fold(own1, come_a), 1)
    keep_b, away_b = pick(fold(own2, come_b), 0)
    (
        come_a, come_b, att_own, att_y, att_z, att_yz, gq, gk, gv, scores, sums, norm1,
    ) = lax.optimization_barrier(
        (
            swap(away_a, "dp", bits[1], dp), swap(away_b, "dp", bits[0], dp), att_own, att_y,
            att_z, att_yz, gq, gk, gv, scores, sums, norm1,
        )
    )
    mlp_chunk = jnp.concatenate([fold(keep_a, come_a), fold(keep_b, come_b)])
    pair2 = fold(keep2, swap(send2, "tensor", 1, tensor))
    sum2 = fold(pair2, swap(pair2, "tensor", 2, tensor))
    rest2 = swap(sum2, "tensor", 1, tensor)
    att_parts = meet(att_own, att_y, att_z, att_yz)
    chunk = combine(att_parts)
    (small_b,) = call(
        sums_kernel,
        [((16, width), BF, "vmem")],
        [(att_parts[1], "vmem"), (scores, "vmem"), (sums, "vmem"), (position_index, "vmem")],
        scratch=[((16, width), F32)],
        cost=1,
    )
    norm1, small_b = lax.optimization_barrier((norm1, small_b))
    across = [swap(norm1, "tensor", flip, tensor).astype(F32) for flip in (1, 2, 3)]
    norm1 = ((norm1.astype(F32) + across[0]) + (across[1] + across[2])).astype(BF)
    keep4, send4 = call(
        attend_out_kernel,
        [((half, width), BF, "vmem"), ((half, width), BF, "vmem")],
        [
            (spot, "smem"), (chunk, "vmem"), (small_b, "vmem"), (gq, "vmem"), (gk, "vmem"), (gv, "vmem"),
            (query_weight, "vmem"), (key_weight, "vmem"), (value_weight, "vmem"),
        ],
        cost=1,
    )

    pair4 = fold(keep4, swap(send4, "tensor", 1, tensor))
    sum4 = fold(pair4, swap(pair4, "tensor", 2, tensor))
    rest4 = swap(sum4, "tensor", 1, tensor)

    for i in more:
        mlp_chunk = fold(mlp_chunk, swap(mlp_chunk, "dp", bits[i], dp))
    mlp_chunk = settle(mlp_chunk, 0)
    chunk = jnp.concatenate([chunk, small_a, small_b, norm1[:8]])
    for i in more:
        chunk = fold(chunk, swap(chunk, "dp", bits[i], dp))
    chunk = settle(chunk, 1)
    chunks = meet(chunk, chunk, chunk, chunk)
    near1 = gather(mlp_chunk[:mlp_chunk.shape[0] // 2], 1)
    near2 = gather(mlp_chunk[mlp_chunk.shape[0] // 2:], 0)
    far1 = swap(near1, "dp", bits[0], dp)
    far2 = swap(near2, "dp", bits[1], dp)
    layer_out, input_grad = call(
        finish_kernel,
        [(wide, F32, "hbm"), (wide, F32, "hbm")],
        [
            (spot, "smem"), (sum4, "vmem"), (rest4, "vmem"), (sum2, "vmem"), (rest2, "vmem"), (gmid, "vmem"), (inputs, "vmem"),
            (norm1_gain, "vmem"), (mid, "vmem"), (down_bias, "vmem"),
        ],
        cost=2,
    )
    w1_total, w2_total = call(
        widen_kernel,
        [((width, units), F32, "hbm"), ((units, width), F32, "hbm")],
        [(spot, "smem"), (layer_out, "keep")]
        + [(value, "vmem") for value in [near1, far1, near2, far2] + marks],
    )
    vector, short = ((width,), F32, "hbm"), ((span,), F32, "hbm")
    (
        wq_total, wk_total, wv_total, wo_total, b1_total, b2_total, g2_total, s2_total, bo_total,
        bq_total, bv_total, rel_total, g1_total, s1_total,
    ) = call(
        unpack_kernel,
        [
            ((width, span), F32, "hbm"), ((width, span), F32, "hbm"), ((width, span), F32, "hbm"),
            ((span, width), F32, "hbm"), vector, vector, vector, vector, vector, short, short,
            ((heads, position_bias.shape[0]), F32, "hbm"), vector, vector,
        ],
        [(spot, "smem"), (w1_total, "keep")] + [(value, "vmem") for value in chunks],
        scratch=[((4, span, width), BF)],
    )
    rel_total = rel_total.T

    return (
        layer_out,
        input_grad,
        wq_total,
        wk_total,
        wv_total,
        bq_total,
        bv_total,
        rel_total,
        wo_total,
        bo_total,
        g1_total,
        s1_total,
        g2_total,
        s2_total,
        w1_total,
        b1_total,
        w2_total,
        b2_total,
    )


def solution(mesh):
    dp, tensor = mesh.shape["dp"], mesh.shape["tensor"]

    def body(*args):
        return shards(*args, dp=dp, tensor=tensor)

    column, line, whole = P(None, "tensor"), P("tensor"), P()
    return jax.shard_map(
        body,
        mesh=mesh,
        in_specs=(
            P("dp", None),
            column,
            column,
            column,
            line,
            line,
            column,
            P("tensor", None),
            whole,
            whole,
            whole,
            whole,
            whole,
            column,
            line,
            P("tensor", None),
            whole,
            P("dp", None),
            P("dp", None),
            whole,
            P("dp", None),
        ),
        out_specs=(
            P("dp", None),
            P("dp", None),
            column,
            column,
            column,
            line,
            line,
            column,
            P("tensor", None),
            whole,
            whole,
            whole,
            whole,
            whole,
            column,
            line,
            P("tensor", None),
            whole,
        ),
        check_vma=False,
    )
```

```python
import jax
import jax.numpy as jnp
from jax import lax
from jax.experimental import pallas as pl
from jax.experimental.pallas import tpu as pltpu
from jax.sharding import PartitionSpec as P

HD = 32
GW = 8
WS = 4
WIN = WS * WS
BLOCK = 128
NEG_FILL = -1e30
BF = jnp.bfloat16
F32 = jnp.float32
EXACT = lax.Precision.HIGHEST
VMEM_BYTES = 24 * 1024 * 1024
ROWS = 16


def dot(left, right):
    return jnp.dot(left, right, preferred_element_type=F32)


def dot_nt(left, right):
    return lax.dot_general(left, right, (((1,), (1,)), ((), ())), preferred_element_type=F32)


def dot_tn(left, right):
    return lax.dot_general(left, right, (((0,), (0,)), ((), ())), preferred_element_type=F32)


def exact_nt(left, right):
    return lax.dot_general(
        left, right, (((1,), (1,)), ((), ())), precision=EXACT, preferred_element_type=F32
    )


def normalize(value):
    centre = value - jnp.mean(value, axis=-1, keepdims=True)
    spread = jnp.mean(centre * centre, axis=-1, keepdims=True)
    inverse = lax.rsqrt(spread + 1e-06)
    return centre * inverse, inverse


def norm_back(grad_out, normed, inverse, gain):
    scaled = grad_out * gain
    first_mean = jnp.mean(scaled, axis=-1, keepdims=True)
    second_mean = jnp.mean(scaled * normed, axis=-1, keepdims=True)
    return inverse * (scaled - first_mean - normed * second_mean)


def row(ref):
    return ref[...].reshape(1, -1)


def iota(shape, axis):
    return lax.broadcasted_iota(jnp.int32, shape, axis)


def place(token):
    return (token // GW) % WS * WS + token % WS


def window(token):
    return token // (GW * WS) * (GW // WS) + token % GW // WS


def by_head(value, heads):
    head = iota(value.shape, 1) // HD
    return jnp.concatenate(
        [jnp.where(head == h, value, jnp.zeros_like(value)) for h in range(heads)]
    )


def own_lanes(value, heads):
    rows = value.shape[0] // heads
    head = iota((rows, value.shape[1]), 1) // HD
    total = value[:rows]
    for h in range(1, heads):
        total = jnp.where(head == h, value[h * rows:(h + 1) * rows], total)
    return total


class Loaded:
    def __init__(self, source, buffer, sem):
        self.buffer, self.shape, self.dtype = buffer, source.shape, source.dtype
        self.copy, self.started = pltpu.make_async_copy(source, buffer, sem), False

    def start(self):
        if not self.started:
            self.copy.start()
            self.started = True

    def wait(self):
        if self.copy is not None:
            self.start()
            self.copy.wait()
            self.copy = None

    def __getitem__(self, at):
        self.wait()
        return self.buffer[at]


class Stored:
    def __init__(self, buffer, target, sem):
        self.buffer, self.shape, self.dtype = buffer, target.shape, target.dtype
        self.copy, self.sent = pltpu.make_async_copy(buffer, target, sem), False

    def __getitem__(self, at):
        return self.buffer[at]

    def __setitem__(self, at, value):
        self.buffer[at] = value

    def send(self):
        if not self.sent:
            self.copy.start()
            self.sent = True


def send_off(ref):
    if isinstance(ref, Stored):
        ref.send()


def call(kernel, outs, args, scratch=(), cost=0, exports=(), later=()):
    spaces = {"smem": pltpu.SMEM, "vmem": pltpu.VMEM, "hbm": pltpu.HBM, "hsmem": pltpu.HBM}
    spaces["keep"] = pltpu.HBM
    plain = len(outs)
    outs = list(outs) + [(args[i][0].shape, args[i][0].dtype, "vmem") for i in exports]
    loads = [i for i, (_, where) in enumerate(args) if where[0] == "h"]
    stores = [i for i, (_, _, where) in enumerate(outs) if where == "hbm"]
    shapes = [jax.ShapeDtypeStruct(shape, dtype) for shape, dtype, _ in outs]
    pinned = [spaces[where](shape, dtype) for shape, dtype, where in outs]
    operands = [
        pltpu.with_memory_space_constraint(a, pltpu.HBM) if spaces[where] == pltpu.HBM else a
        for a, where in args
    ]
    buffers = []
    for i in loads:
        if i in exports:
            continue
        array, where = args[i]
        space = pltpu.SMEM if where == "hsmem" else pltpu.VMEM
        buffers.append(space(array.shape, array.dtype))
    buffers += [pltpu.VMEM(outs[i][0], outs[i][1]) for i in stores]
    sems = [pltpu.SemaphoreType.DMA] * (len(loads) + len(stores))

    def body(*refs):
        refs = list(refs)
        ins, rest = refs[:len(args)], refs[len(args):]
        results, rest = rest[:len(outs)], rest[len(outs):]
        own, rest = rest[:len(scratch)], rest[len(scratch):]
        holds, marks = list(rest[:len(buffers)]), list(rest[len(buffers):])
        given = dict(zip(exports, results[plain:]))
        for i in loads:
            hold = given[i] if i in given else holds.pop(0)
            ins[i] = Loaded(ins[i], hold, marks.pop(0))
            if i not in later:
                ins[i].start()
        for i in stores:
            results[i] = Stored(holds.pop(0), results[i], marks.pop(0))
        kernel(*ins, *results[:plain], *own)
        for i in loads:
            ins[i].wait()
        for i in stores:
            results[i].send()
        for i in stores:
            results[i].copy.wait()

    return pl.pallas_call(
        body,
        name=kernel.__name__,
        out_shape=pinned,
        in_specs=[pl.BlockSpec(memory_space=spaces[where]) for _, where in args],
        out_specs=[pl.BlockSpec(memory_space=spaces[where]) for _, _, where in outs],
        scratch_shapes=[pltpu.VMEM(shape, dtype) for shape, dtype in scratch] + buffers + sems,
        compiler_params=pltpu.CompilerParams(vmem_limit_bytes=VMEM_BYTES),
        cost_estimate=pl.CostEstimate(flops=cost * 10 ** 9, bytes_accessed=0, transcendentals=0),
    )(*operands)


def attend_kernel(
    spot, x, g1, s1, wq, wk, wv, bq, bv, rel, pidx, seg, valid, att, first, q, k, v, probs,
):
    tokens, span = x.shape[0], wq.shape[1]
    heads = span // HD
    blocks = tokens // BLOCK
    for b in range(blocks):
        rows = pl.ds(b * BLOCK, BLOCK)
        normed, _ = normalize(x[rows, :].astype(F32))
        first[rows, :] = (normed * row(g1) + row(s1)).astype(BF)
    weights = jnp.concatenate([wq[...], wk[...], wv[...]], axis=1)
    for i in range(2):
        rows = pl.ds(i * (tokens // 2), tokens // 2)
        mixed = dot(first[rows, :], weights)
        q[rows, :] = (mixed[:, :span] + row(bq)).astype(BF)
        k[rows, :] = mixed[:, span:2 * span].astype(BF)
        v[rows, :] = (mixed[:, 2 * span:] + row(bv)).astype(BF)
    lanes = 2 * heads * WIN
    group = heads * WIN
    table = rel[...]
    coarse = table.astype(BF)
    fine = (table - coarse.astype(F32)).astype(BF)
    lane = iota((heads, lanes), 1)
    mine = lane % group // WIN == iota((heads, lanes), 0)
    rows_by_offset = dot_tn(coarse, (mine & (lane < group)).astype(BF)) + dot_tn(
        fine, (mine & (lane >= group)).astype(BF)
    )
    index = jnp.concatenate([pidx[...]] * (2 * heads), axis=1)
    terms = jnp.zeros((WIN, lanes), F32)
    for o in range(rel.shape[1]):
        terms = jnp.where(index == o, rows_by_offset[o:o + 1, :], terms)
    spread = (place(iota((BLOCK, WIN), 0)) == iota((BLOCK, WIN), 1)).astype(BF)
    terms = dot(spread, terms.astype(BF)).astype(BF)
    lane = iota((lanes, BLOCK), 0)
    here = lane % WIN == place(iota((lanes, BLOCK), 1))
    bias = jnp.concatenate(
        [dot(terms, (here & (lane % group // WIN == h)).astype(BF)) for h in range(heads)]
    )
    query_at, key_at = iota((BLOCK, BLOCK), 0), iota((BLOCK, BLOCK), 1)
    near = window(query_at) == window(key_at)
    selfs = query_at == key_at
    factor = HD ** (-0.5)
    for b in range(blocks):
        rows = pl.ds(b * BLOCK, BLOCK)
        seg_keys = jnp.broadcast_to(seg[:, rows].astype(F32), (BLOCK, BLOCK))
        valid_keys = jnp.broadcast_to(valid[:, rows], (BLOCK, BLOCK)) > 0
        allowed = near & (seg_keys == seg_keys.T) & (valid_keys | selfs)
        wall = jnp.where(allowed, 0.0, NEG_FILL)
        scores = dot_nt(by_head(q[rows, :], heads), k[rows, :]) * factor + bias
        scores = jnp.where(jnp.concatenate([wall] * heads) < 0.0, NEG_FILL, scores)
        expo = jnp.exp(scores - jnp.max(scores, axis=-1, keepdims=True))
        prob = expo * (1.0 / jnp.sum(expo, axis=-1, keepdims=True))
        probs[b] = prob
        att[rows, :] = own_lanes(dot(prob.astype(BF), v[rows, :]), heads).astype(BF)


def fetch_kernel(after, also, cot, w2, *operands):
    grad_hidden = operands[-1]
    grad_hidden[...] = dot_nt(cot[...], w2[...])
    for ref in operands[:-1]:
        ref.wait()


def mlp_kernel(
    spot, a0, a1, a2, a3, p0, p1, p2, p3, x, bo, g2, s2, w1, b1, gh,
    mid, second, hidden, gpre, keep, send, att_all, wo_all,
):
    me = spot[0]
    width = a0.shape[1]
    for j, (a, p) in enumerate(((a0, p0), (a1, p1), (a2, p2), (a3, p3))):
        here = pl.ds(pl.multiple_of((me ^ j) * width, width), width)
        att_all[:, here] = a[...]
        wo_all[here, :] = p[...]
    tokens = x.shape[0]
    half = tokens // 2
    curve = (2.0 / jnp.pi) ** 0.5
    for i in range(2):
        rows = pl.ds(i * half, half)
        value = x[rows, :].astype(F32) + dot(att_all[rows, :], wo_all[...]) + row(bo)
        mid[rows, :] = value
        normed, _ = normalize(value)
        second[rows, :] = (normed * row(g2) + row(s2)).astype(BF)
        pre = dot(second[rows, :], w1[...]) + row(b1)
        square = pre * pre
        bend = jnp.tanh(curve * (pre + 0.044715 * (pre * square)))
        upper = 0.5 * (1.0 + bend)
        hidden[rows, :] = (pre * upper).astype(BF)
        slope = upper + 0.5 * pre * (1.0 - bend * bend) * (curve * (1.0 + 0.134145 * square))
        gpre[rows, :] = (gh[rows, :] * slope).astype(BF)
    send_off(mid)
    core = me % 2
    mine = pl.ds(pl.multiple_of(core * half, half), half)
    other = pl.ds(pl.multiple_of((1 - core) * half, half), half)
    send[...] = dot_nt(gpre[other, :], w1[...]).astype(BF)
    keep[...] = dot_nt(gpre[mine, :], w1[...])


def halves(flag, rows):
    near = pl.ds(pl.multiple_of(flag * rows, rows), rows)
    return near, pl.ds(pl.multiple_of((1 - flag) * rows, rows), rows)


def mlp_grad_kernel(spot, second, hidden, gpre, cot, own1, away1, own2, away2, small, grads):
    part = own1.shape[0]
    mine, other = halves(spot[2], part)
    grads[...] = dot_tn(second[...], gpre[...]).astype(BF)
    own1[...] = grads[mine, :]
    away1[...] = grads[other, :]
    mine, other = halves(spot[3], part)
    grads[...] = dot_tn(hidden[...], cot[...]).astype(BF)
    own2[...] = grads[mine, :]
    away2[...] = grads[other, :]
    which = iota(small.shape, 0)
    first = jnp.sum(gpre[...].astype(F32), axis=0, keepdims=True)
    later = jnp.sum(cot[...].astype(F32), axis=0, keepdims=True)
    small[...] = jnp.where(which == 0, first, jnp.where(which == 1, later, 0.0)).astype(BF)


def attend_back_kernel(
    spot, s2a, s2b, mid, cot, g2, wo, v, probs, k, q, first, att, wq, wk, wv, g1, s1,
    gmid, own, to_y, to_z, to_yz, gq, gk, gv, scores, sums, norm1, gsec, gproj, gatt, pay,
):
    core, place_yz = spot[0] % 2, 2 * spot[2] + spot[3]
    tokens, width = cot.shape
    half = tokens // 2
    span = wq.shape[1]
    heads = span // HD
    blocks = tokens // BLOCK
    mine, other = halves(core, half)
    gsec[mine, :] = s2a[...].astype(F32)
    gsec[other, :] = s2b[...].astype(F32)
    gain_sum = jnp.zeros((1, width), F32)
    shift_sum = jnp.zeros((1, width), F32)
    proj_sum = jnp.zeros((1, width), F32)
    for b in range(blocks):
        rows = pl.ds(b * BLOCK, BLOCK)
        grad = gsec[rows, :]
        normed, inverse = normalize(mid[rows, :])
        gain_sum += jnp.sum(grad * normed, axis=0, keepdims=True)
        shift_sum += jnp.sum(grad, axis=0, keepdims=True)
        value = cot[rows, :].astype(F32) + norm_back(grad, normed, inverse, row(g2))
        gmid[rows, :] = value
        proj_sum += jnp.sum(value, axis=0, keepdims=True)
        gproj[rows, :] = value.astype(BF)
    gatt[...] = dot_nt(gproj[...], wo[...]).astype(BF)
    factor = HD ** (-0.5)
    score_sum = jnp.zeros((heads * BLOCK, BLOCK), F32)
    for b in range(blocks):
        rows = pl.ds(b * BLOCK, BLOCK)
        grads = by_head(gatt[rows, :], heads)
        prob = probs[b]
        grad = dot_nt(grads, v[rows, :])
        gv[rows, :] = dot_tn(prob.astype(BF), grads).astype(BF)
        inner = jnp.sum(prob * grad, axis=-1, keepdims=True)
        gscore = (prob * (grad - inner)).astype(BF)
        score_sum += gscore.astype(F32)
        gq[rows, :] = (factor * own_lanes(dot(gscore, k[rows, :]), heads)).astype(BF)
        gk[rows, :] = (factor * dot_tn(gscore, by_head(q[rows, :], heads))).astype(BF)
    scores[...] = score_sum
    shift = jnp.zeros((8, width), F32)
    gain = jnp.zeros((8, width), F32)
    ones = jnp.ones((8, span), BF)
    eight = iota((8, span), 0)
    mixed = dot_tn(first[...], jnp.concatenate([gq[...], gk[...], gv[...]], axis=1))
    for j, (part, weight) in enumerate(((gq, wq), (gk, wk), (gv, wv))):
        grads = mixed[:, j * span:(j + 1) * span]
        total = jnp.sum(part[...].astype(F32), axis=0, keepdims=True)
        if j != 1:
            at = 0 if j == 0 else span
            sums[3:4, at:at + span] = total
        coarse = total.astype(BF)
        fine = (total - coarse.astype(F32)).astype(BF)
        pair = jnp.where(eight == 0, coarse, jnp.where(eight == 1, fine, jnp.zeros_like(coarse)))
        shift += dot_nt(pair, weight[...])
        product = weight[...].astype(F32) * grads
        coarse = product.astype(BF)
        gain += dot_nt(ones, coarse) + dot_nt(ones, (product - coarse.astype(F32)).astype(BF))
        grads = grads.astype(BF)
        for i in range(width // span):
            pay[j * span:(j + 1) * span, i * span:(i + 1) * span] = grads[i * span:(i + 1) * span]
    pay[3 * span:4 * span, :] = dot_tn(att[...], gproj[...]).astype(BF)
    for ref, flip in ((own, 0), (to_y, 2), (to_z, 1), (to_yz, 3)):
        ref[...] = pay[pl.ds(pl.multiple_of((place_yz ^ flip) * span, span), span), :]
    sums[3:4, 2 * span:] = jnp.zeros((1, width - 2 * span), F32)
    which = iota((ROWS, width), 0)
    shift = shift[0:1, :] + shift[1:2, :]
    gain = (gain[0:1, :] - row(s1) * shift) / row(g1)
    norm1[...] = jnp.where(which == 6, gain, jnp.where(which == 7, shift, 0.0)).astype(BF)
    sums[0:1, :] = gain_sum
    sums[1:2, :] = shift_sum
    sums[2:3, :] = proj_sum


def attend_out_kernel(spot, after, also, gq, gk, gv, wq, wk, wv, keep, send):
    half = gq.shape[0] // 2
    for where, ref in zip(halves(spot[0] % 2, half), (keep, send)):
        ref[...] = (
            dot_nt(gq[where, :], wq[...])
            + dot_nt(gk[where, :], wk[...])
            + dot_nt(gv[where, :], wv[...])
        ).astype(BF)


def mlp_out_kernel(spot, hidden, w2, keep, send):
    for where, ref in zip(halves(spot[0] % 2, hidden.shape[0] // 2), (keep, send)):
        ref[...] = dot(hidden[where, :], w2[...]).astype(BF)


def sums_kernel(after, scores, sums, pidx, small_a, small, all_sums):
    heads = scores.shape[0] // BLOCK
    at = place(iota((BLOCK, WIN), 0)) == iota((BLOCK, WIN), 1)
    fold = at.astype(F32)
    lanes = heads * WIN
    folded = jnp.zeros((WIN, lanes), F32)
    for h in range(heads):
        lane = iota((BLOCK, lanes), 1)
        lay = ((place(iota((BLOCK, lanes), 0)) == lane % WIN) & (lane // WIN == h)).astype(F32)
        once = lax.dot_general(
            fold, scores[h * BLOCK:(h + 1) * BLOCK, :], (((0,), (0,)), ((), ())),
            precision=EXACT, preferred_element_type=F32,
        )
        folded += jnp.dot(once, lay, precision=EXACT, preferred_element_type=F32)
    index = jnp.concatenate([pidx[...]] * heads, axis=1)
    slots = 64
    slot = iota((slots, lanes), 0)
    by_offset = jnp.zeros((slots, lanes), F32)
    for o in range(49):
        total = jnp.sum(jnp.where(index == o, folded, 0.0), axis=0, keepdims=True)
        by_offset = jnp.where(slot == o, total, by_offset)
    pick = (iota((8, lanes), 1) // WIN == iota((8, lanes), 0)).astype(F32)
    offsets = lax.dot_general(
        pick, by_offset, (((1,), (1,)), ((), ())), precision=EXACT, preferred_element_type=F32
    )
    all_sums[...] = jnp.zeros_like(all_sums)
    all_sums[0:2, :] = small_a[0:2, :].astype(F32)
    all_sums[2:6, :] = sums[0:4, :]
    all_sums[8:16, 0:slots] = offsets
    small[...] = all_sums[...].astype(BF)


def finish_kernel(spot, s4, r4, s2, r2, gmid, x, g1, mid, b2, layer_out, input_grad):
    core = spot[0] % 2
    half = x.shape[0] // 2
    for part, (ref, out) in enumerate(((s4, s2), (r4, r2))):
        start = core if part == 0 else 1 - core
        where = pl.ds(pl.multiple_of(start * half, half), half)
        normed, inverse = normalize(x[where, :].astype(F32))
        grad = ref[...].astype(F32)
        input_grad[where, :] = gmid[where, :] + norm_back(grad, normed, inverse, row(g1))
        mlp = out[...].astype(F32)
        layer_out[where, :] = mid[where, :] + mlp + row(b2)


def widen_kernel(spot, after, near1, far1, near2, far2, *others):
    w1, w2 = others[-2:]
    part = near1.shape[0]
    for flag, near, far, ref in ((spot[2], near1, far1, w1), (spot[3], near2, far2, w2)):
        mine, other = halves(flag, part)
        ref[mine, :] = near[...].astype(F32)
        ref[other, :] = far[...].astype(F32)
        send_off(ref)


def unpack_kernel(
    spot, after, near, from_y, from_z, from_yz,
    wq, wk, wv, wo, b1, b2, g2, s2, bo, bq, bv, rel, g1, s1, both,
):
    place_yz = 2 * spot[2] + spot[3]
    width = near.shape[1]
    span = wo.shape[0]
    for ref, flip in ((near, 0), (from_y, 2), (from_z, 1), (from_yz, 3)):
        both[place_yz ^ flip] = ref[0:span, :]
    for j, ref in enumerate((wq, wk, wv)):
        for i in range(width // span):
            block = both[j, :, i * span:(i + 1) * span]
            ref[i * span:(i + 1) * span, :] = block.astype(F32)
        send_off(ref)
    wo[...] = both[3].astype(F32)
    send_off(wo)
    sums = (near[span:, :].astype(F32) + from_y[span:, :].astype(F32)) + (
        from_z[span:, :].astype(F32) + from_yz[span:, :].astype(F32)
    )
    for at, ref in ((0, b1), (1, b2), (2, g2), (3, s2), (4, bo), (6, g1), (7, s1)):
        ref[...] = sums[at]
    bq[...] = sums[5, :span]
    bv[...] = sums[5, span:2 * span]
    rel[...] = sums[8:8 + rel.shape[0], :rel.shape[1]]


def swap(value, axis, bit, size):
    return lax.ppermute(value, axis, [(i, i ^ bit) for i in range(size)])


def shards(
    inputs,
    query_weight,
    key_weight,
    value_weight,
    query_bias,
    value_bias,
    position_bias,
    proj_weight,
    proj_bias,
    norm1_gain,
    norm1_shift,
    norm2_gain,
    norm2_shift,
    up_weight,
    up_bias,
    down_weight,
    down_bias,
    segment_ids,
    valid_mask,
    position_index,
    out_cotangent,
    dp,
    tensor,
):
    tokens, width = inputs.shape
    half = tokens // 2
    span = query_weight.shape[1]
    units = up_weight.shape[1]
    heads = span // HD
    blocks = tokens // BLOCK
    me = lax.axis_index("tensor")
    mate = lax.axis_index("dp")
    bits = [1 << i for i in range(dp.bit_length() - 1)]
    flags = [(mate >> i) & 1 for i in range(len(bits))]
    lower = [flag == 0 for flag in flags]
    sizes = [(width >> (i + 1)) * n for i in range(len(bits)) for n in (1, 2)]
    starts = {
        (i, size): (flags[i] * size).astype(jnp.uint32) for i in range(len(bits)) for size in sizes
    }
    stops = {
        at: ((1 - flags[at[0]]) * at[1]).astype(jnp.uint32) for at in starts
    }
    spot = jnp.stack(
        [me, mate]
        + flags
        + [flag.astype(jnp.int32) for flag in lower]
        + [at.astype(jnp.int32) for at in list(starts.values()) + list(stops.values())]
    )
    seg = segment_ids.reshape(1, tokens)
    valid = valid_mask.reshape(1, tokens)
    wide = (tokens, width)
    narrow = (tokens, span)

    wo_x = swap(proj_weight, "tensor", 2, tensor)
    wo_c = swap(proj_weight, "tensor", 1, tensor)
    wo_d = swap(wo_x, "tensor", 1, tensor)

    att, first, q, k, v, probs = call(
        attend_kernel,
        [
            (narrow, BF, "vmem"), (wide, BF, "vmem"), (narrow, BF, "vmem"), (narrow, BF, "vmem"),
            (narrow, BF, "vmem"), ((blocks, heads * BLOCK, BLOCK), F32, "vmem"),
        ],
        [
            (spot, "smem"), (inputs, "hbm"), (norm1_gain, "hbm"), (norm1_shift, "hbm"),
            (query_weight, "hbm"), (key_weight, "hbm"), (value_weight, "hbm"), (query_bias, "hbm"),
            (value_bias, "hbm"), (position_bias.T, "hbm"), (position_index, "hbm"), (seg, "hbm"),
            (valid, "hbm"),
        ],
        cost=20,
    )
    (
        grad_hidden, out_cotangent, down_weight, inputs, norm1_gain, norm1_shift, position_index,
        query_weight, key_weight, value_weight, proj_weight, proj_bias, norm2_gain, norm2_shift,
        up_weight, up_bias, down_bias,
    ) = call(
        fetch_kernel,
        [((tokens, units), F32, "vmem")],
        [(att, "vmem"), (wo_x, "vmem")]
        + [
            (value, "hbm")
            for value in (
                out_cotangent, down_weight, inputs, norm1_gain, norm1_shift, position_index,
                query_weight, key_weight, value_weight, proj_weight, proj_bias, norm2_gain,
                norm2_shift, up_weight, up_bias, down_bias,
            )
        ],
        exports=tuple(range(2, 18)),
        cost=0,
    )
    att_x, down_bias = lax.optimization_barrier((swap(att, "tensor", 2, tensor), down_bias))
    att_c = swap(att, "tensor", 1, tensor)
    att_d = swap(att_x, "tensor", 1, tensor)

    mid, second, hidden, gpre, keep3, send3 = call(
        mlp_kernel,
        [
            (wide, F32, "vmem"), (wide, BF, "vmem"), ((tokens, units), BF, "vmem"),
            ((tokens, units), BF, "vmem"), ((half, width), F32, "vmem"), ((half, width), BF, "vmem"),
        ],
        [
            (spot, "smem"), (att, "vmem"), (att_c, "vmem"), (att_x, "vmem"), (att_d, "vmem"),
            (proj_weight, "vmem"), (wo_c, "vmem"), (wo_x, "vmem"), (wo_d, "vmem"),
            (inputs, "vmem"), (proj_bias, "vmem"), (norm2_gain, "vmem"), (norm2_shift, "vmem"),
            (up_weight, "vmem"), (up_bias, "vmem"), (grad_hidden, "vmem"),
        ],
        scratch=[((tokens, tensor * span), BF), ((tensor * span, width), BF)],
        cost=2,
    )

    def fold(value, other):
        return (value.astype(F32) + other.astype(F32)).astype(BF)

    own1, away1, own2, away2, small_a = call(
        mlp_grad_kernel,
        [((half, width), BF, "vmem")] * 4 + [((8, width), BF, "vmem")],
        [
            (spot, "smem"), (second, "vmem"), (hidden, "vmem"), (gpre, "vmem"),
            (out_cotangent, "vmem"),
        ],
        scratch=[((width, units), BF)],
        cost=2,
    )
    come3 = swap(send3, "tensor", 1, tensor)
    come3, small_a, away1, away2 = lax.optimization_barrier((come3, small_a, away1, away2))
    pair3 = fold(keep3, come3)
    keep2, send2 = call(
        mlp_out_kernel,
        [((half, width), BF, "vmem"), ((half, width), BF, "vmem")],
        [(spot, "smem"), (hidden, "vmem"), (down_weight, "vmem")],
        cost=1,
    )
    come3, come_a, come_b, keep2, send2 = lax.optimization_barrier(
        (
            swap(pair3, "tensor", 2, tensor),
            swap(away1, "dp", bits[0], dp),
            swap(away2, "dp", bits[1], dp),
            keep2,
            send2,
        )
    )
    sum3 = fold(pair3, come3)
    rest3 = swap(sum3, "tensor", 1, tensor)

    def meet(own, along_y, along_z, along_yz):
        return (
            own,
            swap(along_y, "dp", bits[0], dp),
            swap(along_z, "dp", bits[1], dp),
            swap(along_yz, "dp", bits[0] | bits[1], dp),
        )

    def combine(parts):
        own, y, z, yz = [part.astype(F32) for part in parts]
        return ((own + y) + (z + yz)).astype(BF)

    piece = ((span, width), BF, "vmem")
    gmid, att_own, att_y, att_z, att_yz, gq, gk, gv, scores, sums, norm1 = call(
        attend_back_kernel,
        [
            (wide, F32, "vmem"), piece, piece, piece, piece, (narrow, BF, "vmem"),
            (narrow, BF, "vmem"), (narrow, BF, "vmem"), ((heads * BLOCK, BLOCK), F32, "vmem"),
            ((8, width), F32, "vmem"), ((ROWS, width), BF, "vmem"),
        ],
        [
            (spot, "smem"), (sum3, "vmem"), (rest3, "vmem"), (mid, "vmem"),
            (out_cotangent, "vmem"), (norm2_gain, "vmem"), (proj_weight, "vmem"), (v, "vmem"),
            (probs, "vmem"), (k, "vmem"), (q, "vmem"), (first, "vmem"), (att, "vmem"),
            (query_weight, "vmem"), (key_weight, "vmem"), (value_weight, "vmem"),
            (norm1_gain, "vmem"), (norm1_shift, "vmem"),
        ],
        scratch=[(wide, F32), (wide, BF), (narrow, BF), ((4 * span, width), BF)],
        cost=1,
    )
    left = jnp.uint32(0)

    def pick(value, i):
        part = value.shape[0] // 2
        return (
            lax.dynamic_slice(value, (starts[i, part], left), (part, width)),
            lax.dynamic_slice(value, (stops[i, part], left), (part, width)),
        )

    def settle(value, times):
        for _ in range(times):
            mark = swap(value, "tensor", 1, tensor)
            value, mark = lax.optimization_barrier((value, mark))
            marks.append(mark)
        return value

    marks = []

    def scatter(value, i):
        own, away = pick(value, i)
        return fold(own, swap(away, "dp", bits[i], dp))

    def gather(own, i):
        other = swap(own, "dp", bits[i], dp)
        return jnp.where(
            lower[i], jnp.concatenate([own, other]), jnp.concatenate([other, own])
        )

    more = range(2, len(bits))

    keep_a, away_a = pick(fold(own1, come_a), 1)
    keep_b, away_b = pick(fold(own2, come_b), 0)
    (
        come_a, come_b, att_own, att_y, att_z, att_yz, gq, gk, gv, scores, sums, norm1,
    ) = lax.optimization_barrier(
        (
            swap(away_a, "dp", bits[1], dp), swap(away_b, "dp", bits[0], dp), att_own, att_y,
            att_z, att_yz, gq, gk, gv, scores, sums, norm1,
        )
    )
    mlp_chunk = jnp.concatenate([fold(keep_a, come_a), fold(keep_b, come_b)])
    pair2 = fold(keep2, swap(send2, "tensor", 1, tensor))
    sum2 = fold(pair2, swap(pair2, "tensor", 2, tensor))
    rest2 = swap(sum2, "tensor", 1, tensor)
    att_parts = meet(att_own, att_y, att_z, att_yz)
    chunk = combine(att_parts)
    (small_b,) = call(
        sums_kernel,
        [((16, width), BF, "vmem")],
        [(att_parts[1], "vmem"), (scores, "vmem"), (sums, "vmem"), (position_index, "vmem"),
            (small_a, "vmem"),
        ],
        scratch=[((16, width), F32)],
        cost=1,
    )
    norm1, small_b = lax.optimization_barrier((norm1, small_b))
    across = [swap(norm1, "tensor", flip, tensor).astype(F32) for flip in (1, 2, 3)]
    norm1 = ((norm1.astype(F32) + across[0]) + (across[1] + across[2])).astype(BF)
    keep4, send4 = call(
        attend_out_kernel,
        [((half, width), BF, "vmem"), ((half, width), BF, "vmem")],
        [
            (spot, "smem"), (chunk, "vmem"), (small_b, "vmem"), (gq, "vmem"), (gk, "vmem"), (gv, "vmem"),
            (query_weight, "vmem"), (key_weight, "vmem"), (value_weight, "vmem"),
        ],
        cost=1,
    )

    pair4 = fold(keep4, swap(send4, "tensor", 1, tensor))
    sum4 = fold(pair4, swap(pair4, "tensor", 2, tensor))
    rest4 = swap(sum4, "tensor", 1, tensor)

    for i in more:
        mlp_chunk = fold(mlp_chunk, swap(mlp_chunk, "dp", bits[i], dp))
    mlp_chunk = settle(mlp_chunk, 0)
    chunk = jnp.concatenate([chunk, small_b + norm1])
    for i in more:
        chunk = fold(chunk, swap(chunk, "dp", bits[i], dp))
    chunk = settle(chunk, 1)
    chunks = meet(chunk, chunk, chunk, chunk)
    near1 = gather(mlp_chunk[:mlp_chunk.shape[0] // 2], 1)
    near2 = gather(mlp_chunk[mlp_chunk.shape[0] // 2:], 0)
    far1 = swap(near1, "dp", bits[0], dp)
    far2 = swap(near2, "dp", bits[1], dp)
    layer_out, input_grad = call(
        finish_kernel,
        [(wide, F32, "hbm"), (wide, F32, "hbm")],
        [
            (spot, "smem"), (sum4, "vmem"), (rest4, "vmem"), (sum2, "vmem"), (rest2, "vmem"), (gmid, "vmem"), (inputs, "vmem"),
            (norm1_gain, "vmem"), (mid, "vmem"), (down_bias, "vmem"),
        ],
        cost=2,
    )
    w1_total, w2_total = call(
        widen_kernel,
        [((width, units), F32, "hbm"), ((units, width), F32, "hbm")],
        [(spot, "smem"), (layer_out, "keep")]
        + [(value, "vmem") for value in [near1, far1, near2, far2] + marks],
    )
    vector, short = ((width,), F32, "hbm"), ((span,), F32, "hbm")
    (
        wq_total, wk_total, wv_total, wo_total, b1_total, b2_total, g2_total, s2_total, bo_total,
        bq_total, bv_total, rel_total, g1_total, s1_total,
    ) = call(
        unpack_kernel,
        [
            ((width, span), F32, "hbm"), ((width, span), F32, "hbm"), ((width, span), F32, "hbm"),
            ((span, width), F32, "hbm"), vector, vector, vector, vector, vector, short, short,
            ((heads, position_bias.shape[0]), F32, "hbm"), vector, vector,
        ],
        [(spot, "smem"), (w1_total, "keep")] + [(value, "vmem") for value in chunks],
        scratch=[((4, span, width), BF)],
    )
    rel_total = rel_total.T

    return (
        layer_out,
        input_grad,
        wq_total,
        wk_total,
        wv_total,
        bq_total,
        bv_total,
        rel_total,
        wo_total,
        bo_total,
        g1_total,
        s1_total,
        g2_total,
        s2_total,
        w1_total,
        b1_total,
        w2_total,
        b2_total,
    )


def solution(mesh):
    dp, tensor = mesh.shape["dp"], mesh.shape["tensor"]

    def body(*args):
        return shards(*args, dp=dp, tensor=tensor)

    column, line, whole = P(None, "tensor"), P("tensor"), P()
    return jax.shard_map(
        body,
        mesh=mesh,
        in_specs=(
            P("dp", None),
            column,
            column,
            column,
            line,
            line,
            column,
            P("tensor", None),
            whole,
            whole,
            whole,
            whole,
            whole,
            column,
            line,
            P("tensor", None),
            whole,
            P("dp", None),
            P("dp", None),
            whole,
            P("dp", None),
        ),
        out_specs=(
            P("dp", None),
            P("dp", None),
            column,
            column,
            column,
            line,
            line,
            column,
            P("tensor", None),
            whole,
            whole,
            whole,
            whole,
            whole,
            column,
            line,
            P("tensor", None),
            whole,
        ),
        check_vma=False,
    )
```

```python
import jax
import jax.numpy as jnp
from jax import lax
from jax.experimental import pallas as pl
from jax.experimental.pallas import tpu as pltpu
from jax.sharding import PartitionSpec as P

HD = 32
GW = 8
WS = 4
WIN = WS * WS
BLOCK = 128
NEG_FILL = -1e30
BF = jnp.bfloat16
F32 = jnp.float32
EXACT = lax.Precision.HIGHEST
VMEM_BYTES = 24 * 1024 * 1024
ROWS = 16


def dot(left, right):
    return jnp.dot(left, right, preferred_element_type=F32)


def dot_nt(left, right):
    return lax.dot_general(left, right, (((1,), (1,)), ((), ())), preferred_element_type=F32)


def dot_tn(left, right):
    return lax.dot_general(left, right, (((0,), (0,)), ((), ())), preferred_element_type=F32)


def exact_nt(left, right):
    return lax.dot_general(
        left, right, (((1,), (1,)), ((), ())), precision=EXACT, preferred_element_type=F32
    )


def normalize(value):
    centre = value - jnp.mean(value, axis=-1, keepdims=True)
    spread = jnp.mean(centre * centre, axis=-1, keepdims=True)
    inverse = lax.rsqrt(spread + 1e-06)
    return centre * inverse, inverse


def norm_back(grad_out, normed, inverse, gain):
    scaled = grad_out * gain
    first_mean = jnp.mean(scaled, axis=-1, keepdims=True)
    second_mean = jnp.mean(scaled * normed, axis=-1, keepdims=True)
    return inverse * (scaled - first_mean - normed * second_mean)


def row(ref):
    return ref[...].reshape(1, -1)


def iota(shape, axis):
    return lax.broadcasted_iota(jnp.int32, shape, axis)


def place(token):
    return (token // GW) % WS * WS + token % WS


def window(token):
    return token // (GW * WS) * (GW // WS) + token % GW // WS


def by_head(value, heads):
    head = iota(value.shape, 1) // HD
    return jnp.concatenate(
        [jnp.where(head == h, value, jnp.zeros_like(value)) for h in range(heads)]
    )


def own_lanes(value, heads):
    rows = value.shape[0] // heads
    head = iota((rows, value.shape[1]), 1) // HD
    total = value[:rows]
    for h in range(1, heads):
        total = jnp.where(head == h, value[h * rows:(h + 1) * rows], total)
    return total


class Loaded:
    def __init__(self, source, buffer, sem):
        self.buffer, self.shape, self.dtype = buffer, source.shape, source.dtype
        self.copy, self.started = pltpu.make_async_copy(source, buffer, sem), False

    def start(self):
        if not self.started:
            self.copy.start()
            self.started = True

    def wait(self):
        if self.copy is not None:
            self.start()
            self.copy.wait()
            self.copy = None

    def __getitem__(self, at):
        self.wait()
        return self.buffer[at]


class Stored:
    def __init__(self, buffer, target, sem):
        self.buffer, self.shape, self.dtype = buffer, target.shape, target.dtype
        self.copy, self.sent = pltpu.make_async_copy(buffer, target, sem), False

    def __getitem__(self, at):
        return self.buffer[at]

    def __setitem__(self, at, value):
        self.buffer[at] = value

    def send(self):
        if not self.sent:
            self.copy.start()
            self.sent = True


def send_off(ref):
    if isinstance(ref, Stored):
        ref.send()


def call(kernel, outs, args, scratch=(), cost=0, exports=(), later=()):
    spaces = {"smem": pltpu.SMEM, "vmem": pltpu.VMEM, "hbm": pltpu.HBM, "hsmem": pltpu.HBM}
    spaces["keep"] = pltpu.HBM
    plain = len(outs)
    outs = list(outs) + [(args[i][0].shape, args[i][0].dtype, "vmem") for i in exports]
    loads = [i for i, (_, where) in enumerate(args) if where[0] == "h"]
    stores = [i for i, (_, _, where) in enumerate(outs) if where == "hbm"]
    shapes = [jax.ShapeDtypeStruct(shape, dtype) for shape, dtype, _ in outs]
    pinned = [spaces[where](shape, dtype) for shape, dtype, where in outs]
    operands = [
        pltpu.with_memory_space_constraint(a, pltpu.HBM) if spaces[where] == pltpu.HBM else a
        for a, where in args
    ]
    buffers = []
    for i in loads:
        if i in exports:
            continue
        array, where = args[i]
        space = pltpu.SMEM if where == "hsmem" else pltpu.VMEM
        buffers.append(space(array.shape, array.dtype))
    buffers += [pltpu.VMEM(outs[i][0], outs[i][1]) for i in stores]
    sems = [pltpu.SemaphoreType.DMA] * (len(loads) + len(stores))

    def body(*refs):
        refs = list(refs)
        ins, rest = refs[:len(args)], refs[len(args):]
        results, rest = rest[:len(outs)], rest[len(outs):]
        own, rest = rest[:len(scratch)], rest[len(scratch):]
        holds, marks = list(rest[:len(buffers)]), list(rest[len(buffers):])
        given = dict(zip(exports, results[plain:]))
        for i in loads:
            hold = given[i] if i in given else holds.pop(0)
            ins[i] = Loaded(ins[i], hold, marks.pop(0))
            if i not in later:
                ins[i].start()
        for i in stores:
            results[i] = Stored(holds.pop(0), results[i], marks.pop(0))
        kernel(*ins, *results[:plain], *own)
        for i in loads:
            ins[i].wait()
        for i in stores:
            results[i].send()
        for i in stores:
            results[i].copy.wait()

    return pl.pallas_call(
        body,
        name=kernel.__name__,
        out_shape=pinned,
        in_specs=[pl.BlockSpec(memory_space=spaces[where]) for _, where in args],
        out_specs=[pl.BlockSpec(memory_space=spaces[where]) for _, _, where in outs],
        scratch_shapes=[pltpu.VMEM(shape, dtype) for shape, dtype in scratch] + buffers + sems,
        compiler_params=pltpu.CompilerParams(vmem_limit_bytes=VMEM_BYTES),
        cost_estimate=pl.CostEstimate(flops=cost * 10 ** 9, bytes_accessed=0, transcendentals=0),
    )(*operands)


def attend_kernel(
    spot, x, g1, s1, wq, wk, wv, bq, bv, rel, pidx, seg, valid, att, first, q, k, v, probs,
):
    tokens, span = x.shape[0], wq.shape[1]
    heads = span // HD
    blocks = tokens // BLOCK
    for b in range(blocks):
        rows = pl.ds(b * BLOCK, BLOCK)
        normed, _ = normalize(x[rows, :].astype(F32))
        first[rows, :] = (normed * row(g1) + row(s1)).astype(BF)
    weights = jnp.concatenate([wq[...], wk[...], wv[...]], axis=1)
    for i in range(2):
        rows = pl.ds(i * (tokens // 2), tokens // 2)
        mixed = dot(first[rows, :], weights)
        q[rows, :] = (mixed[:, :span] + row(bq)).astype(BF)
        k[rows, :] = mixed[:, span:2 * span].astype(BF)
        v[rows, :] = (mixed[:, 2 * span:] + row(bv)).astype(BF)
    lanes = 2 * heads * WIN
    group = heads * WIN
    table = rel[...]
    coarse = table.astype(BF)
    fine = (table - coarse.astype(F32)).astype(BF)
    lane = iota((heads, lanes), 1)
    mine = lane % group // WIN == iota((heads, lanes), 0)
    rows_by_offset = dot_tn(coarse, (mine & (lane < group)).astype(BF)) + dot_tn(
        fine, (mine & (lane >= group)).astype(BF)
    )
    index = jnp.concatenate([pidx[...]] * (2 * heads), axis=1)
    terms = jnp.zeros((WIN, lanes), F32)
    for o in range(rel.shape[1]):
        terms = jnp.where(index == o, rows_by_offset[o:o + 1, :], terms)
    spread = (place(iota((BLOCK, WIN), 0)) == iota((BLOCK, WIN), 1)).astype(BF)
    terms = dot(spread, terms.astype(BF)).astype(BF)
    lane = iota((lanes, BLOCK), 0)
    here = lane % WIN == place(iota((lanes, BLOCK), 1))
    bias = jnp.concatenate(
        [dot(terms, (here & (lane % group // WIN == h)).astype(BF)) for h in range(heads)]
    )
    query_at, key_at = iota((BLOCK, BLOCK), 0), iota((BLOCK, BLOCK), 1)
    near = window(query_at) == window(key_at)
    selfs = query_at == key_at
    factor = HD ** (-0.5)
    for b in range(blocks):
        rows = pl.ds(b * BLOCK, BLOCK)
        seg_keys = jnp.broadcast_to(seg[:, rows].astype(F32), (BLOCK, BLOCK))
        valid_keys = jnp.broadcast_to(valid[:, rows], (BLOCK, BLOCK)) > 0
        allowed = near & (seg_keys == seg_keys.T) & (valid_keys | selfs)
        wall = jnp.where(allowed, 0.0, NEG_FILL)
        scores = dot_nt(by_head(q[rows, :], heads), k[rows, :]) * factor + bias
        scores = jnp.where(jnp.concatenate([wall] * heads) < 0.0, NEG_FILL, scores)
        expo = jnp.exp(scores - jnp.max(scores, axis=-1, keepdims=True))
        prob = expo * (1.0 / jnp.sum(expo, axis=-1, keepdims=True))
        probs[b] = prob
        att[rows, :] = own_lanes(dot(prob.astype(BF), v[rows, :]), heads).astype(BF)


def fetch_kernel(after, also, cot, w2, *operands):
    grad_hidden = operands[-1]
    grad_hidden[...] = dot_nt(cot[...], w2[...])
    for ref in operands[:-1]:
        ref.wait()


def mlp_kernel(
    spot, a0, a1, a2, a3, p0, p1, p2, p3, x, bo, g2, s2, w1, b1, gh,
    mid, second, hidden, gpre, keep, send, att_all, wo_all,
):
    me = spot[0]
    width = a0.shape[1]
    for j, (a, p) in enumerate(((a0, p0), (a1, p1), (a2, p2), (a3, p3))):
        here = pl.ds(pl.multiple_of((me ^ j) * width, width), width)
        att_all[:, here] = a[...]
        wo_all[here, :] = p[...]
    tokens = x.shape[0]
    half = tokens // 2
    curve = (2.0 / jnp.pi) ** 0.5
    for i in range(2):
        rows = pl.ds(i * half, half)
        value = x[rows, :].astype(F32) + dot(att_all[rows, :], wo_all[...]) + row(bo)
        mid[rows, :] = value
        normed, _ = normalize(value)
        second[rows, :] = (normed * row(g2) + row(s2)).astype(BF)
        pre = dot(second[rows, :], w1[...]) + row(b1)
        square = pre * pre
        bend = jnp.tanh(curve * (pre + 0.044715 * (pre * square)))
        upper = 0.5 * (1.0 + bend)
        hidden[rows, :] = (pre * upper).astype(BF)
        slope = upper + 0.5 * pre * (1.0 - bend * bend) * (curve * (1.0 + 0.134145 * square))
        gpre[rows, :] = (gh[rows, :] * slope).astype(BF)
    send_off(mid)
    core = me % 2
    mine = pl.ds(pl.multiple_of(core * half, half), half)
    other = pl.ds(pl.multiple_of((1 - core) * half, half), half)
    send[...] = dot_nt(gpre[other, :], w1[...]).astype(BF)
    keep[...] = dot_nt(gpre[mine, :], w1[...])


def halves(flag, rows):
    near = pl.ds(pl.multiple_of(flag * rows, rows), rows)
    return near, pl.ds(pl.multiple_of((1 - flag) * rows, rows), rows)


def mlp_grad_kernel(spot, second, hidden, gpre, cot, own1, away1, own2, away2, small, grads):
    part = own1.shape[0]
    mine, other = halves(spot[2], part)
    grads[...] = dot_tn(second[...], gpre[...]).astype(BF)
    own1[...] = grads[mine, :]
    away1[...] = grads[other, :]
    mine, other = halves(spot[3], part)
    grads[...] = dot_tn(hidden[...], cot[...]).astype(BF)
    own2[...] = grads[mine, :]
    away2[...] = grads[other, :]
    which = iota(small.shape, 0)
    first = jnp.sum(gpre[...].astype(F32), axis=0, keepdims=True)
    later = jnp.sum(cot[...].astype(F32), axis=0, keepdims=True)
    small[...] = jnp.where(which == 0, first, jnp.where(which == 1, later, 0.0)).astype(BF)


def attend_back_kernel(
    spot, s2a, s2b, mid, cot, g2, wo, v, probs, k, q, first, att, wq, wk, wv, g1, s1,
    gmid, own, to_y, to_z, to_yz, gq, gk, gv, scores, sums, norm1, gsec, gproj, gatt, pay,
):
    core, place_yz = spot[0] % 2, 2 * spot[2] + spot[3]
    tokens, width = cot.shape
    half = tokens // 2
    span = wq.shape[1]
    heads = span // HD
    blocks = tokens // BLOCK
    mine, other = halves(core, half)
    gsec[mine, :] = s2a[...].astype(F32)
    gsec[other, :] = s2b[...].astype(F32)
    gain_sum = jnp.zeros((1, width), F32)
    shift_sum = jnp.zeros((1, width), F32)
    proj_sum = jnp.zeros((1, width), F32)
    for b in range(blocks):
        rows = pl.ds(b * BLOCK, BLOCK)
        grad = gsec[rows, :]
        normed, inverse = normalize(mid[rows, :])
        gain_sum += jnp.sum(grad * normed, axis=0, keepdims=True)
        shift_sum += jnp.sum(grad, axis=0, keepdims=True)
        value = cot[rows, :].astype(F32) + norm_back(grad, normed, inverse, row(g2))
        gmid[rows, :] = value
        proj_sum += jnp.sum(value, axis=0, keepdims=True)
        gproj[rows, :] = value.astype(BF)
    gatt[...] = dot_nt(gproj[...], wo[...]).astype(BF)
    factor = HD ** (-0.5)
    score_sum = jnp.zeros((heads * BLOCK, BLOCK), F32)
    for b in range(blocks):
        rows = pl.ds(b * BLOCK, BLOCK)
        grads = by_head(gatt[rows, :], heads)
        prob = probs[b]
        grad = dot_nt(grads, v[rows, :])
        gv[rows, :] = dot_tn(prob.astype(BF), grads).astype(BF)
        inner = jnp.sum(prob * grad, axis=-1, keepdims=True)
        gscore = (prob * (grad - inner)).astype(BF)
        score_sum += gscore.astype(F32)
        gq[rows, :] = (factor * own_lanes(dot(gscore, k[rows, :]), heads)).astype(BF)
        gk[rows, :] = (factor * dot_tn(gscore, by_head(q[rows, :], heads))).astype(BF)
    scores[...] = score_sum
    shift = jnp.zeros((8, width), F32)
    gain = jnp.zeros((8, width), F32)
    ones = jnp.ones((8, span), BF)
    eight = iota((8, span), 0)
    mixed = dot_tn(first[...], jnp.concatenate([gq[...], gk[...], gv[...]], axis=1))
    for j, (part, weight) in enumerate(((gq, wq), (gk, wk), (gv, wv))):
        grads = mixed[:, j * span:(j + 1) * span]
        total = jnp.sum(part[...].astype(F32), axis=0, keepdims=True)
        if j != 1:
            at = 0 if j == 0 else span
            sums[3:4, at:at + span] = total
        coarse = total.astype(BF)
        fine = (total - coarse.astype(F32)).astype(BF)
        pair = jnp.where(eight == 0, coarse, jnp.where(eight == 1, fine, jnp.zeros_like(coarse)))
        shift += dot_nt(pair, weight[...])
        product = weight[...].astype(F32) * grads
        coarse = product.astype(BF)
        gain += dot_nt(ones, coarse) + dot_nt(ones, (product - coarse.astype(F32)).astype(BF))
        grads = grads.astype(BF)
        for i in range(width // span):
            pay[j * span:(j + 1) * span, i * span:(i + 1) * span] = grads[i * span:(i + 1) * span]
    pay[3 * span:4 * span, :] = dot_tn(att[...], gproj[...]).astype(BF)
    for ref, flip in ((own, 0), (to_y, 2), (to_z, 1), (to_yz, 3)):
        ref[...] = pay[pl.ds(pl.multiple_of((place_yz ^ flip) * span, span), span), :]
    sums[3:4, 2 * span:] = jnp.zeros((1, width - 2 * span), F32)
    which = iota((ROWS, width), 0)
    shift = shift[0:1, :] + shift[1:2, :]
    gain = (gain[0:1, :] - row(s1) * shift) / row(g1)
    norm1[...] = jnp.where(which == 6, gain, jnp.where(which == 7, shift, 0.0)).astype(BF)
    sums[0:1, :] = gain_sum
    sums[1:2, :] = shift_sum
    sums[2:3, :] = proj_sum


def attend_out_kernel(spot, after, also, gq, gk, gv, wq, wk, wv, keep, send):
    half = gq.shape[0] // 2
    for where, ref in zip(halves(spot[0] % 2, half), (keep, send)):
        ref[...] = (
            dot_nt(gq[where, :], wq[...])
            + dot_nt(gk[where, :], wk[...])
            + dot_nt(gv[where, :], wv[...])
        ).astype(BF)


def mlp_out_kernel(spot, hidden, w2, keep, send):
    for where, ref in zip(halves(spot[0] % 2, hidden.shape[0] // 2), (keep, send)):
        ref[...] = dot(hidden[where, :], w2[...]).astype(BF)


def sums_kernel(after, scores, sums, pidx, small_a, small, all_sums):
    heads = scores.shape[0] // BLOCK
    at = place(iota((BLOCK, WIN), 0)) == iota((BLOCK, WIN), 1)
    fold = at.astype(F32)
    lanes = heads * WIN
    folded = jnp.zeros((WIN, lanes), F32)
    for h in range(heads):
        lane = iota((BLOCK, lanes), 1)
        lay = ((place(iota((BLOCK, lanes), 0)) == lane % WIN) & (lane // WIN == h)).astype(F32)
        once = lax.dot_general(
            fold, scores[h * BLOCK:(h + 1) * BLOCK, :], (((0,), (0,)), ((), ())),
            precision=EXACT, preferred_element_type=F32,
        )
        folded += jnp.dot(once, lay, precision=EXACT, preferred_element_type=F32)
    index = jnp.concatenate([pidx[...]] * heads, axis=1)
    slots = 64
    slot = iota((slots, lanes), 0)
    by_offset = jnp.zeros((slots, lanes), F32)
    for o in range(49):
        total = jnp.sum(jnp.where(index == o, folded, 0.0), axis=0, keepdims=True)
        by_offset = jnp.where(slot == o, total, by_offset)
    pick = (iota((8, lanes), 1) // WIN == iota((8, lanes), 0)).astype(F32)
    offsets = lax.dot_general(
        pick, by_offset, (((1,), (1,)), ((), ())), precision=EXACT, preferred_element_type=F32
    )
    all_sums[...] = jnp.zeros_like(all_sums)
    all_sums[0:2, :] = small_a[0:2, :].astype(F32)
    all_sums[2:6, :] = sums[0:4, :]
    all_sums[8:16, 0:slots] = offsets
    small[...] = all_sums[...].astype(BF)


def finish_kernel(spot, s4, r4, s2, r2, gmid, x, g1, mid, b2, layer_out, input_grad):
    core = spot[0] % 2
    half = x.shape[0] // 2
    for part, (ref, out) in enumerate(((s4, s2), (r4, r2))):
        start = core if part == 0 else 1 - core
        where = pl.ds(pl.multiple_of(start * half, half), half)
        normed, inverse = normalize(x[where, :].astype(F32))
        grad = ref[...].astype(F32)
        input_grad[where, :] = gmid[where, :] + norm_back(grad, normed, inverse, row(g1))
        mlp = out[...].astype(F32)
        layer_out[where, :] = mid[where, :] + mlp + row(b2)


def widen_kernel(spot, after, near1, far1, near2, far2, w1, w2):
    part = near1.shape[0]
    for flag, near, far, ref in ((spot[2], near1, far1, w1), (spot[3], near2, far2, w2)):
        mine, other = halves(flag, part)
        ref[mine, :] = near[...].astype(F32)
        ref[other, :] = far[...].astype(F32)
        send_off(ref)


def unpack_kernel(
    spot, after, near, from_y, from_z, from_yz,
    wq, wk, wv, wo, b1, b2, g2, s2, bo, bq, bv, rel, g1, s1, both,
):
    place_yz = 2 * spot[2] + spot[3]
    width = near.shape[1]
    span = wo.shape[0]
    for ref, flip in ((near, 0), (from_y, 2), (from_z, 1), (from_yz, 3)):
        both[place_yz ^ flip] = ref[0:span, :]
    for j, ref in enumerate((wq, wk, wv)):
        for i in range(width // span):
            block = both[j, :, i * span:(i + 1) * span]
            ref[i * span:(i + 1) * span, :] = block.astype(F32)
        send_off(ref)
    wo[...] = both[3].astype(F32)
    send_off(wo)
    sums = (near[span:, :].astype(F32) + from_y[span:, :].astype(F32)) + (
        from_z[span:, :].astype(F32) + from_yz[span:, :].astype(F32)
    )
    for at, ref in ((0, b1), (1, b2), (2, g2), (3, s2), (4, bo), (6, g1), (7, s1)):
        ref[...] = sums[at]
    bq[...] = sums[5, :span]
    bv[...] = sums[5, span:2 * span]
    rel[...] = sums[8:8 + rel.shape[0], :rel.shape[1]]


def swap(value, axis, bit, size):
    return lax.ppermute(value, axis, [(i, i ^ bit) for i in range(size)])


def shards(
    inputs,
    query_weight,
    key_weight,
    value_weight,
    query_bias,
    value_bias,
    position_bias,
    proj_weight,
    proj_bias,
    norm1_gain,
    norm1_shift,
    norm2_gain,
    norm2_shift,
    up_weight,
    up_bias,
    down_weight,
    down_bias,
    segment_ids,
    valid_mask,
    position_index,
    out_cotangent,
    dp,
    tensor,
):
    tokens, width = inputs.shape
    half = tokens // 2
    span = query_weight.shape[1]
    units = up_weight.shape[1]
    heads = span // HD
    blocks = tokens // BLOCK
    me = lax.axis_index("tensor")
    mate = lax.axis_index("dp")
    bits = [1 << i for i in range(dp.bit_length() - 1)]
    flags = [(mate >> i) & 1 for i in range(len(bits))]
    lower = [flag == 0 for flag in flags]
    sizes = [(width >> (i + 1)) * n for i in range(len(bits)) for n in (1, 2)]
    starts = {
        (i, size): (flags[i] * size).astype(jnp.uint32) for i in range(len(bits)) for size in sizes
    }
    stops = {
        at: ((1 - flags[at[0]]) * at[1]).astype(jnp.uint32) for at in starts
    }
    spot = jnp.stack(
        [me, mate]
        + flags
        + [flag.astype(jnp.int32) for flag in lower]
        + [at.astype(jnp.int32) for at in list(starts.values()) + list(stops.values())]
    )
    seg = segment_ids.reshape(1, tokens)
    valid = valid_mask.reshape(1, tokens)
    wide = (tokens, width)
    narrow = (tokens, span)

    wo_x = swap(proj_weight, "tensor", 2, tensor)
    wo_c = swap(proj_weight, "tensor", 1, tensor)
    wo_d = swap(wo_x, "tensor", 1, tensor)

    att, first, q, k, v, probs = call(
        attend_kernel,
        [
            (narrow, BF, "vmem"), (wide, BF, "vmem"), (narrow, BF, "vmem"), (narrow, BF, "vmem"),
            (narrow, BF, "vmem"), ((blocks, heads * BLOCK, BLOCK), F32, "vmem"),
        ],
        [
            (spot, "smem"), (inputs, "hbm"), (norm1_gain, "hbm"), (norm1_shift, "hbm"),
            (query_weight, "hbm"), (key_weight, "hbm"), (value_weight, "hbm"), (query_bias, "hbm"),
            (value_bias, "hbm"), (position_bias.T, "hbm"), (position_index, "hbm"), (seg, "hbm"),
            (valid, "hbm"),
        ],
        cost=20,
    )
    (
        grad_hidden, out_cotangent, down_weight, inputs, norm1_gain, norm1_shift, position_index,
        query_weight, key_weight, value_weight, proj_weight, proj_bias, norm2_gain, norm2_shift,
        up_weight, up_bias, down_bias,
    ) = call(
        fetch_kernel,
        [((tokens, units), F32, "vmem")],
        [(att, "vmem"), (wo_x, "vmem")]
        + [
            (value, "hbm")
            for value in (
                out_cotangent, down_weight, inputs, norm1_gain, norm1_shift, position_index,
                query_weight, key_weight, value_weight, proj_weight, proj_bias, norm2_gain,
                norm2_shift, up_weight, up_bias, down_bias,
            )
        ],
        exports=tuple(range(2, 18)),
        cost=0,
    )
    att_x, down_bias = lax.optimization_barrier((swap(att, "tensor", 2, tensor), down_bias))
    att_c = swap(att, "tensor", 1, tensor)
    att_d = swap(att_x, "tensor", 1, tensor)

    mid, second, hidden, gpre, keep3, send3 = call(
        mlp_kernel,
        [
            (wide, F32, "vmem"), (wide, BF, "vmem"), ((tokens, units), BF, "vmem"),
            ((tokens, units), BF, "vmem"), ((half, width), F32, "vmem"), ((half, width), BF, "vmem"),
        ],
        [
            (spot, "smem"), (att, "vmem"), (att_c, "vmem"), (att_x, "vmem"), (att_d, "vmem"),
            (proj_weight, "vmem"), (wo_c, "vmem"), (wo_x, "vmem"), (wo_d, "vmem"),
            (inputs, "vmem"), (proj_bias, "vmem"), (norm2_gain, "vmem"), (norm2_shift, "vmem"),
            (up_weight, "vmem"), (up_bias, "vmem"), (grad_hidden, "vmem"),
        ],
        scratch=[((tokens, tensor * span), BF), ((tensor * span, width), BF)],
        cost=2,
    )

    def fold(value, other):
        return (value.astype(F32) + other.astype(F32)).astype(BF)

    own1, away1, own2, away2, small_a = call(
        mlp_grad_kernel,
        [((half, width), BF, "vmem")] * 4 + [((8, width), BF, "vmem")],
        [
            (spot, "smem"), (second, "vmem"), (hidden, "vmem"), (gpre, "vmem"),
            (out_cotangent, "vmem"),
        ],
        scratch=[((width, units), BF)],
        cost=2,
    )
    come3 = swap(send3, "tensor", 1, tensor)
    come3, small_a, away1, away2 = lax.optimization_barrier((come3, small_a, away1, away2))
    pair3 = fold(keep3, come3)
    keep2, send2 = call(
        mlp_out_kernel,
        [((half, width), BF, "vmem"), ((half, width), BF, "vmem")],
        [(spot, "smem"), (hidden, "vmem"), (down_weight, "vmem")],
        cost=1,
    )
    come3, come_a, come_b, keep2, send2 = lax.optimization_barrier(
        (
            swap(pair3, "tensor", 2, tensor),
            swap(away1, "dp", bits[0], dp),
            swap(away2, "dp", bits[1], dp),
            keep2,
            send2,
        )
    )
    sum3 = fold(pair3, come3)
    rest3 = swap(sum3, "tensor", 1, tensor)

    def meet(own, along_y, along_z, along_yz):
        return (
            own,
            swap(along_y, "dp", bits[0], dp),
            swap(along_z, "dp", bits[1], dp),
            swap(along_yz, "dp", bits[0] | bits[1], dp),
        )

    def combine(parts):
        own, y, z, yz = [part.astype(F32) for part in parts]
        return ((own + y) + (z + yz)).astype(BF)

    piece = ((span, width), BF, "vmem")
    gmid, att_own, att_y, att_z, att_yz, gq, gk, gv, scores, sums, norm1 = call(
        attend_back_kernel,
        [
            (wide, F32, "vmem"), piece, piece, piece, piece, (narrow, BF, "vmem"),
            (narrow, BF, "vmem"), (narrow, BF, "vmem"), ((heads * BLOCK, BLOCK), F32, "vmem"),
            ((8, width), F32, "vmem"), ((ROWS, width), BF, "vmem"),
        ],
        [
            (spot, "smem"), (sum3, "vmem"), (rest3, "vmem"), (mid, "vmem"),
            (out_cotangent, "vmem"), (norm2_gain, "vmem"), (proj_weight, "vmem"), (v, "vmem"),
            (probs, "vmem"), (k, "vmem"), (q, "vmem"), (first, "vmem"), (att, "vmem"),
            (query_weight, "vmem"), (key_weight, "vmem"), (value_weight, "vmem"),
            (norm1_gain, "vmem"), (norm1_shift, "vmem"),
        ],
        scratch=[(wide, F32), (wide, BF), (narrow, BF), ((4 * span, width), BF)],
        cost=1,
    )
    left = jnp.uint32(0)

    def pick(value, i):
        part = value.shape[0] // 2
        return (
            lax.dynamic_slice(value, (starts[i, part], left), (part, width)),
            lax.dynamic_slice(value, (stops[i, part], left), (part, width)),
        )

    def gather(own, i):
        other = swap(own, "dp", bits[i], dp)
        return jnp.where(
            lower[i], jnp.concatenate([own, other]), jnp.concatenate([other, own])
        )

    more = range(2, len(bits))

    keep_a, away_a = pick(fold(own1, come_a), 1)
    keep_b, away_b = pick(fold(own2, come_b), 0)
    (
        come_a, come_b, att_own, att_y, att_z, att_yz, gq, gk, gv, scores, sums, norm1,
    ) = lax.optimization_barrier(
        (
            swap(away_a, "dp", bits[1], dp), swap(away_b, "dp", bits[0], dp), att_own, att_y,
            att_z, att_yz, gq, gk, gv, scores, sums, norm1,
        )
    )
    mlp_chunk = jnp.concatenate([fold(keep_a, come_a), fold(keep_b, come_b)])
    pair2 = fold(keep2, swap(send2, "tensor", 1, tensor))
    sum2 = fold(pair2, swap(pair2, "tensor", 2, tensor))
    rest2 = swap(sum2, "tensor", 1, tensor)
    att_parts = meet(att_own, att_y, att_z, att_yz)
    chunk = combine(att_parts)
    (small_b,) = call(
        sums_kernel,
        [((16, width), BF, "vmem")],
        [(att_parts[1], "vmem"), (scores, "vmem"), (sums, "vmem"), (position_index, "vmem"),
            (small_a, "vmem"),
        ],
        scratch=[((16, width), F32)],
        cost=1,
    )
    norm1, small_b = lax.optimization_barrier((norm1, small_b))
    across = [swap(norm1, "tensor", flip, tensor).astype(F32) for flip in (1, 2, 3)]
    norm1 = ((norm1.astype(F32) + across[0]) + (across[1] + across[2])).astype(BF)
    keep4, send4 = call(
        attend_out_kernel,
        [((half, width), BF, "vmem"), ((half, width), BF, "vmem")],
        [
            (spot, "smem"), (chunk, "vmem"), (small_b, "vmem"), (gq, "vmem"), (gk, "vmem"), (gv, "vmem"),
            (query_weight, "vmem"), (key_weight, "vmem"), (value_weight, "vmem"),
        ],
        cost=1,
    )

    pair4 = fold(keep4, swap(send4, "tensor", 1, tensor))
    sum4 = fold(pair4, swap(pair4, "tensor", 2, tensor))
    rest4 = swap(sum4, "tensor", 1, tensor)

    for i in more:
        mlp_chunk = fold(mlp_chunk, swap(mlp_chunk, "dp", bits[i], dp))
    chunk = jnp.concatenate([chunk, small_b + norm1])
    for i in more:
        chunk = fold(chunk, swap(chunk, "dp", bits[i], dp))
    chunks = meet(chunk, chunk, chunk, chunk)
    near1 = gather(mlp_chunk[:mlp_chunk.shape[0] // 2], 1)
    near2 = gather(mlp_chunk[mlp_chunk.shape[0] // 2:], 0)
    far1 = swap(near1, "dp", bits[0], dp)
    far2 = swap(near2, "dp", bits[1], dp)
    layer_out, input_grad = call(
        finish_kernel,
        [(wide, F32, "hbm"), (wide, F32, "hbm")],
        [
            (spot, "smem"), (sum4, "vmem"), (rest4, "vmem"), (sum2, "vmem"), (rest2, "vmem"), (gmid, "vmem"), (inputs, "vmem"),
            (norm1_gain, "vmem"), (mid, "vmem"), (down_bias, "vmem"),
        ],
        cost=2,
    )
    w1_total, w2_total = call(
        widen_kernel,
        [((width, units), F32, "hbm"), ((units, width), F32, "hbm")],
        [(spot, "smem"), (layer_out, "keep")]
        + [(value, "vmem") for value in (near1, far1, near2, far2)],
    )
    vector, short = ((width,), F32, "hbm"), ((span,), F32, "hbm")
    (
        wq_total, wk_total, wv_total, wo_total, b1_total, b2_total, g2_total, s2_total, bo_total,
        bq_total, bv_total, rel_total, g1_total, s1_total,
    ) = call(
        unpack_kernel,
        [
            ((width, span), F32, "hbm"), ((width, span), F32, "hbm"), ((width, span), F32, "hbm"),
            ((span, width), F32, "hbm"), vector, vector, vector, vector, vector, short, short,
            ((heads, position_bias.shape[0]), F32, "hbm"), vector, vector,
        ],
        [(spot, "smem"), (w1_total, "keep")] + [(value, "vmem") for value in chunks],
        scratch=[((4, span, width), BF)],
    )
    rel_total = rel_total.T

    return (
        layer_out,
        input_grad,
        wq_total,
        wk_total,
        wv_total,
        bq_total,
        bv_total,
        rel_total,
        wo_total,
        bo_total,
        g1_total,
        s1_total,
        g2_total,
        s2_total,
        w1_total,
        b1_total,
        w2_total,
        b2_total,
    )


def solution(mesh):
    dp, tensor = mesh.shape["dp"], mesh.shape["tensor"]

    def body(*args):
        return shards(*args, dp=dp, tensor=tensor)

    column, line, whole = P(None, "tensor"), P("tensor"), P()
    return jax.shard_map(
        body,
        mesh=mesh,
        in_specs=(
            P("dp", None),
            column,
            column,
            column,
            line,
            line,
            column,
            P("tensor", None),
            whole,
            whole,
            whole,
            whole,
            whole,
            column,
            line,
            P("tensor", None),
            whole,
            P("dp", None),
            P("dp", None),
            whole,
            P("dp", None),
        ),
        out_specs=(
            P("dp", None),
            P("dp", None),
            column,
            column,
            column,
            line,
            line,
            column,
            P("tensor", None),
            whole,
            whole,
            whole,
            whole,
            whole,
            column,
            line,
            P("tensor", None),
            whole,
        ),
        check_vma=False,
    )
```

```python
import jax
import jax.numpy as jnp
from jax import lax
from jax.experimental import pallas as pl
from jax.experimental.pallas import tpu as pltpu
from jax.sharding import PartitionSpec as P

HD = 32
GW = 8
WS = 4
WIN = WS * WS
BLOCK = 128
NEG_FILL = -1e30
BF = jnp.bfloat16
F32 = jnp.float32
EXACT = lax.Precision.HIGHEST
VMEM_BYTES = 24 * 1024 * 1024
ROWS = 16


def dot(left, right):
    return jnp.dot(left, right, preferred_element_type=F32)


def dot_nt(left, right):
    return lax.dot_general(left, right, (((1,), (1,)), ((), ())), preferred_element_type=F32)


def dot_tn(left, right):
    return lax.dot_general(left, right, (((0,), (0,)), ((), ())), preferred_element_type=F32)


def exact_nt(left, right):
    return lax.dot_general(
        left, right, (((1,), (1,)), ((), ())), precision=EXACT, preferred_element_type=F32
    )


def normalize(value):
    centre = value - jnp.mean(value, axis=-1, keepdims=True)
    spread = jnp.mean(centre * centre, axis=-1, keepdims=True)
    inverse = lax.rsqrt(spread + 1e-06)
    return centre * inverse, inverse


def norm_back(grad_out, normed, inverse, gain):
    scaled = grad_out * gain
    first_mean = jnp.mean(scaled, axis=-1, keepdims=True)
    second_mean = jnp.mean(scaled * normed, axis=-1, keepdims=True)
    return inverse * (scaled - first_mean - normed * second_mean)


def row(ref):
    return ref[...].reshape(1, -1)


def iota(shape, axis):
    return lax.broadcasted_iota(jnp.int32, shape, axis)


def place(token):
    return (token // GW) % WS * WS + token % WS


def window(token):
    return token // (GW * WS) * (GW // WS) + token % GW // WS


def by_head(value, heads):
    head = iota(value.shape, 1) // HD
    return jnp.concatenate(
        [jnp.where(head == h, value, jnp.zeros_like(value)) for h in range(heads)]
    )


def own_lanes(value, heads):
    rows = value.shape[0] // heads
    head = iota((rows, value.shape[1]), 1) // HD
    total = value[:rows]
    for h in range(1, heads):
        total = jnp.where(head == h, value[h * rows:(h + 1) * rows], total)
    return total


class Loaded:
    def __init__(self, source, buffer, sem):
        self.buffer, self.shape, self.dtype = buffer, source.shape, source.dtype
        self.copy, self.started = pltpu.make_async_copy(source, buffer, sem), False

    def start(self):
        if not self.started:
            self.copy.start()
            self.started = True

    def wait(self):
        if self.copy is not None:
            self.start()
            self.copy.wait()
            self.copy = None

    def __getitem__(self, at):
        self.wait()
        return self.buffer[at]


class Stored:
    def __init__(self, buffer, target, sem):
        self.buffer, self.shape, self.dtype = buffer, target.shape, target.dtype
        self.copy, self.sent = pltpu.make_async_copy(buffer, target, sem), False

    def __getitem__(self, at):
        return self.buffer[at]

    def __setitem__(self, at, value):
        self.buffer[at] = value

    def send(self):
        if not self.sent:
            self.copy.start()
            self.sent = True


def send_off(ref):
    if isinstance(ref, Stored):
        ref.send()


def call(kernel, outs, args, scratch=(), cost=0, exports=(), later=()):
    spaces = {"smem": pltpu.SMEM, "vmem": pltpu.VMEM, "hbm": pltpu.HBM, "hsmem": pltpu.HBM}
    spaces["keep"] = pltpu.HBM
    plain = len(outs)
    outs = list(outs) + [(args[i][0].shape, args[i][0].dtype, "vmem") for i in exports]
    loads = [i for i, (_, where) in enumerate(args) if where[0] == "h"]
    stores = [i for i, (_, _, where) in enumerate(outs) if where == "hbm"]
    shapes = [jax.ShapeDtypeStruct(shape, dtype) for shape, dtype, _ in outs]
    pinned = [spaces[where](shape, dtype) for shape, dtype, where in outs]
    operands = [
        pltpu.with_memory_space_constraint(a, pltpu.HBM) if spaces[where] == pltpu.HBM else a
        for a, where in args
    ]
    buffers = []
    for i in loads:
        if i in exports:
            continue
        array, where = args[i]
        space = pltpu.SMEM if where == "hsmem" else pltpu.VMEM
        buffers.append(space(array.shape, array.dtype))
    buffers += [pltpu.VMEM(outs[i][0], outs[i][1]) for i in stores]
    sems = [pltpu.SemaphoreType.DMA] * (len(loads) + len(stores))

    def body(*refs):
        refs = list(refs)
        ins, rest = refs[:len(args)], refs[len(args):]
        results, rest = rest[:len(outs)], rest[len(outs):]
        own, rest = rest[:len(scratch)], rest[len(scratch):]
        holds, marks = list(rest[:len(buffers)]), list(rest[len(buffers):])
        given = dict(zip(exports, results[plain:]))
        for i in loads:
            hold = given[i] if i in given else holds.pop(0)
            ins[i] = Loaded(ins[i], hold, marks.pop(0))
            if i not in later:
                ins[i].start()
        for i in stores:
            results[i] = Stored(holds.pop(0), results[i], marks.pop(0))
        kernel(*ins, *results[:plain], *own)
        for i in loads:
            ins[i].wait()
        for i in stores:
            results[i].send()
        for i in stores:
            results[i].copy.wait()

    return pl.pallas_call(
        body,
        name=kernel.__name__,
        out_shape=pinned,
        in_specs=[pl.BlockSpec(memory_space=spaces[where]) for _, where in args],
        out_specs=[pl.BlockSpec(memory_space=spaces[where]) for _, _, where in outs],
        scratch_shapes=[pltpu.VMEM(shape, dtype) for shape, dtype in scratch] + buffers + sems,
        compiler_params=pltpu.CompilerParams(vmem_limit_bytes=VMEM_BYTES),
        cost_estimate=pl.CostEstimate(flops=cost * 10 ** 9, bytes_accessed=0, transcendentals=0),
    )(*operands)


def attend_kernel(
    spot, x, g1, s1, wq, wk, wv, bq, bv, rel, pidx, seg, valid, att, first, q, k, v, probs,
):
    tokens, span = x.shape[0], wq.shape[1]
    heads = span // HD
    blocks = tokens // BLOCK
    for b in range(blocks):
        rows = pl.ds(b * BLOCK, BLOCK)
        normed, _ = normalize(x[rows, :].astype(F32))
        first[rows, :] = (normed * row(g1) + row(s1)).astype(BF)
    weights = jnp.concatenate([wq[...], wk[...], wv[...]], axis=1)
    for i in range(2):
        rows = pl.ds(i * (tokens // 2), tokens // 2)
        mixed = dot(first[rows, :], weights)
        q[rows, :] = (mixed[:, :span] + row(bq)).astype(BF)
        k[rows, :] = mixed[:, span:2 * span].astype(BF)
        v[rows, :] = (mixed[:, 2 * span:] + row(bv)).astype(BF)
    lanes = 2 * heads * WIN
    group = heads * WIN
    table = rel[...]
    coarse = table.astype(BF)
    fine = (table - coarse.astype(F32)).astype(BF)
    lane = iota((heads, lanes), 1)
    mine = lane % group // WIN == iota((heads, lanes), 0)
    rows_by_offset = dot_tn(coarse, (mine & (lane < group)).astype(BF)) + dot_tn(
        fine, (mine & (lane >= group)).astype(BF)
    )
    index = jnp.concatenate([pidx[...]] * (2 * heads), axis=1)
    terms = jnp.zeros((WIN, lanes), F32)
    for o in range(rel.shape[1]):
        terms = jnp.where(index == o, rows_by_offset[o:o + 1, :], terms)
    spread = (place(iota((BLOCK, WIN), 0)) == iota((BLOCK, WIN), 1)).astype(BF)
    terms = dot(spread, terms.astype(BF)).astype(BF)
    lane = iota((lanes, BLOCK), 0)
    here = lane % WIN == place(iota((lanes, BLOCK), 1))
    bias = jnp.concatenate(
        [dot(terms, (here & (lane % group // WIN == h)).astype(BF)) for h in range(heads)]
    )
    query_at, key_at = iota((BLOCK, BLOCK), 0), iota((BLOCK, BLOCK), 1)
    near = window(query_at) == window(key_at)
    selfs = query_at == key_at
    factor = HD ** (-0.5)
    for b in range(blocks):
        rows = pl.ds(b * BLOCK, BLOCK)
        seg_keys = jnp.broadcast_to(seg[:, rows].astype(F32), (BLOCK, BLOCK))
        valid_keys = jnp.broadcast_to(valid[:, rows], (BLOCK, BLOCK)) > 0
        allowed = near & (seg_keys == seg_keys.T) & (valid_keys | selfs)
        wall = jnp.where(allowed, 0.0, NEG_FILL)
        scores = dot_nt(by_head(q[rows, :], heads), k[rows, :]) * factor + bias
        scores = jnp.where(jnp.concatenate([wall] * heads) < 0.0, NEG_FILL, scores)
        expo = jnp.exp(scores - jnp.max(scores, axis=-1, keepdims=True))
        prob = expo * (1.0 / jnp.sum(expo, axis=-1, keepdims=True))
        probs[b] = prob
        att[rows, :] = own_lanes(dot(prob.astype(BF), v[rows, :]), heads).astype(BF)


def fetch_kernel(after, also, cot, w2, *operands):
    grad_hidden = operands[-1]
    grad_hidden[...] = dot_nt(cot[...], w2[...])
    for ref in operands[:-1]:
        ref.wait()


def mlp_kernel(
    spot, a0, a1, a2, a3, p0, p1, p2, p3, x, bo, g2, s2, w1, b1, gh,
    mid, second, hidden, gpre, keep, send, att_all, wo_all,
):
    me = spot[0]
    width = a0.shape[1]
    for j, (a, p) in enumerate(((a0, p0), (a1, p1), (a2, p2), (a3, p3))):
        here = pl.ds(pl.multiple_of((me ^ j) * width, width), width)
        att_all[:, here] = a[...]
        wo_all[here, :] = p[...]
    tokens = x.shape[0]
    half = tokens // 2
    curve = (2.0 / jnp.pi) ** 0.5
    for i in range(1):
        rows = pl.ds(0, tokens)
        value = x[rows, :].astype(F32) + dot(att_all[rows, :], wo_all[...]) + row(bo)
        mid[rows, :] = value
        normed, _ = normalize(value)
        second[rows, :] = (normed * row(g2) + row(s2)).astype(BF)
        pre = dot(second[rows, :], w1[...]) + row(b1)
        square = pre * pre
        bend = jnp.tanh(curve * (pre + 0.044715 * (pre * square)))
        upper = 0.5 * (1.0 + bend)
        hidden[rows, :] = (pre * upper).astype(BF)
        slope = upper + 0.5 * pre * (1.0 - bend * bend) * (curve * (1.0 + 0.134145 * square))
        gpre[rows, :] = (gh[rows, :] * slope).astype(BF)
    send_off(mid)
    core = me % 2
    mine = pl.ds(pl.multiple_of(core * half, half), half)
    other = pl.ds(pl.multiple_of((1 - core) * half, half), half)
    send[...] = dot_nt(gpre[other, :], w1[...]).astype(BF)
    keep[...] = dot_nt(gpre[mine, :], w1[...])


def halves(flag, rows):
    near = pl.ds(pl.multiple_of(flag * rows, rows), rows)
    return near, pl.ds(pl.multiple_of((1 - flag) * rows, rows), rows)


def mlp_grad_kernel(spot, second, hidden, gpre, cot, own1, away1, own2, away2, small, grads):
    part = own1.shape[0]
    mine, other = halves(spot[2], part)
    grads[...] = dot_tn(second[...], gpre[...]).astype(BF)
    own1[...] = grads[mine, :]
    away1[...] = grads[other, :]
    mine, other = halves(spot[3], part)
    grads[...] = dot_tn(hidden[...], cot[...]).astype(BF)
    own2[...] = grads[mine, :]
    away2[...] = grads[other, :]
    which = iota(small.shape, 0)
    first = jnp.sum(gpre[...].astype(F32), axis=0, keepdims=True)
    later = jnp.sum(cot[...].astype(F32), axis=0, keepdims=True)
    small[...] = jnp.where(which == 0, first, jnp.where(which == 1, later, 0.0)).astype(BF)


def attend_back_kernel(
    spot, s2a, s2b, mid, cot, g2, wo, v, probs, k, q, first, att, wq, wk, wv, g1, s1,
    gmid, own, to_y, to_z, to_yz, gq, gk, gv, scores, sums, norm1, gsec, gproj, gatt, pay,
):
    core, place_yz = spot[0] % 2, 2 * spot[2] + spot[3]
    tokens, width = cot.shape
    half = tokens // 2
    span = wq.shape[1]
    heads = span // HD
    blocks = tokens // BLOCK
    mine, other = halves(core, half)
    gsec[mine, :] = s2a[...].astype(F32)
    gsec[other, :] = s2b[...].astype(F32)
    gain_sum = jnp.zeros((1, width), F32)
    shift_sum = jnp.zeros((1, width), F32)
    proj_sum = jnp.zeros((1, width), F32)
    for b in range(blocks):
        rows = pl.ds(b * BLOCK, BLOCK)
        grad = gsec[rows, :]
        normed, inverse = normalize(mid[rows, :])
        gain_sum += jnp.sum(grad * normed, axis=0, keepdims=True)
        shift_sum += jnp.sum(grad, axis=0, keepdims=True)
        value = cot[rows, :].astype(F32) + norm_back(grad, normed, inverse, row(g2))
        gmid[rows, :] = value
        proj_sum += jnp.sum(value, axis=0, keepdims=True)
        gproj[rows, :] = value.astype(BF)
    gatt[...] = dot_nt(gproj[...], wo[...]).astype(BF)
    factor = HD ** (-0.5)
    score_sum = jnp.zeros((heads * BLOCK, BLOCK), F32)
    for b in range(blocks):
        rows = pl.ds(b * BLOCK, BLOCK)
        grads = by_head(gatt[rows, :], heads)
        prob = probs[b]
        grad = dot_nt(grads, v[rows, :])
        gv[rows, :] = dot_tn(prob.astype(BF), grads).astype(BF)
        inner = jnp.sum(prob * grad, axis=-1, keepdims=True)
        gscore = (prob * (grad - inner)).astype(BF)
        score_sum += gscore.astype(F32)
        gq[rows, :] = (factor * own_lanes(dot(gscore, k[rows, :]), heads)).astype(BF)
        gk[rows, :] = (factor * dot_tn(gscore, by_head(q[rows, :], heads))).astype(BF)
    scores[...] = score_sum
    shift = jnp.zeros((8, width), F32)
    gain = jnp.zeros((8, width), F32)
    ones = jnp.ones((8, span), BF)
    eight = iota((8, span), 0)
    mixed = dot_tn(first[...], jnp.concatenate([gq[...], gk[...], gv[...]], axis=1))
    for j, (part, weight) in enumerate(((gq, wq), (gk, wk), (gv, wv))):
        grads = mixed[:, j * span:(j + 1) * span]
        total = jnp.sum(part[...].astype(F32), axis=0, keepdims=True)
        if j != 1:
            at = 0 if j == 0 else span
            sums[3:4, at:at + span] = total
        coarse = total.astype(BF)
        fine = (total - coarse.astype(F32)).astype(BF)
        pair = jnp.where(eight == 0, coarse, jnp.where(eight == 1, fine, jnp.zeros_like(coarse)))
        shift += dot_nt(pair, weight[...])
        product = weight[...].astype(F32) * grads
        coarse = product.astype(BF)
        gain += dot_nt(ones, coarse) + dot_nt(ones, (product - coarse.astype(F32)).astype(BF))
        grads = grads.astype(BF)
        for i in range(width // span):
            pay[j * span:(j + 1) * span, i * span:(i + 1) * span] = grads[i * span:(i + 1) * span]
    pay[3 * span:4 * span, :] = dot_tn(att[...], gproj[...]).astype(BF)
    for ref, flip in ((own, 0), (to_y, 2), (to_z, 1), (to_yz, 3)):
        ref[...] = pay[pl.ds(pl.multiple_of((place_yz ^ flip) * span, span), span), :]
    sums[3:4, 2 * span:] = jnp.zeros((1, width - 2 * span), F32)
    which = iota((ROWS, width), 0)
    shift = shift[0:1, :] + shift[1:2, :]
    gain = (gain[0:1, :] - row(s1) * shift) / row(g1)
    norm1[...] = jnp.where(which == 6, gain, jnp.where(which == 7, shift, 0.0)).astype(BF)
    sums[0:1, :] = gain_sum
    sums[1:2, :] = shift_sum
    sums[2:3, :] = proj_sum


def attend_out_kernel(spot, after, also, gq, gk, gv, wq, wk, wv, keep, send):
    half = gq.shape[0] // 2
    for where, ref in zip(halves(spot[0] % 2, half), (keep, send)):
        ref[...] = (
            dot_nt(gq[where, :], wq[...])
            + dot_nt(gk[where, :], wk[...])
            + dot_nt(gv[where, :], wv[...])
        ).astype(BF)


def mlp_out_kernel(spot, hidden, w2, keep, send):
    for where, ref in zip(halves(spot[0] % 2, hidden.shape[0] // 2), (keep, send)):
        ref[...] = dot(hidden[where, :], w2[...]).astype(BF)


def sums_kernel(after, scores, sums, pidx, small_a, small, all_sums):
    heads = scores.shape[0] // BLOCK
    at = place(iota((BLOCK, WIN), 0)) == iota((BLOCK, WIN), 1)
    fold = at.astype(F32)
    lanes = heads * WIN
    folded = jnp.zeros((WIN, lanes), F32)
    for h in range(heads):
        lane = iota((BLOCK, lanes), 1)
        lay = ((place(iota((BLOCK, lanes), 0)) == lane % WIN) & (lane // WIN == h)).astype(F32)
        once = lax.dot_general(
            fold, scores[h * BLOCK:(h + 1) * BLOCK, :], (((0,), (0,)), ((), ())),
            precision=EXACT, preferred_element_type=F32,
        )
        folded += jnp.dot(once, lay, precision=EXACT, preferred_element_type=F32)
    index = jnp.concatenate([pidx[...]] * heads, axis=1)
    slots = 64
    slot = iota((slots, lanes), 0)
    by_offset = jnp.zeros((slots, lanes), F32)
    for o in range(49):
        total = jnp.sum(jnp.where(index == o, folded, 0.0), axis=0, keepdims=True)
        by_offset = jnp.where(slot == o, total, by_offset)
    pick = (iota((8, lanes), 1) // WIN == iota((8, lanes), 0)).astype(F32)
    offsets = lax.dot_general(
        pick, by_offset, (((1,), (1,)), ((), ())), precision=EXACT, preferred_element_type=F32
    )
    all_sums[...] = jnp.zeros_like(all_sums)
    all_sums[0:2, :] = small_a[0:2, :].astype(F32)
    all_sums[2:6, :] = sums[0:4, :]
    all_sums[8:16, 0:slots] = offsets
    small[...] = all_sums[...].astype(BF)


def finish_kernel(spot, s4, r4, s2, r2, gmid, x, g1, mid, b2, layer_out, input_grad):
    core = spot[0] % 2
    half = x.shape[0] // 2
    for part, (ref, out) in enumerate(((s4, s2), (r4, r2))):
        start = core if part == 0 else 1 - core
        where = pl.ds(pl.multiple_of(start * half, half), half)
        normed, inverse = normalize(x[where, :].astype(F32))
        grad = ref[...].astype(F32)
        input_grad[where, :] = gmid[where, :] + norm_back(grad, normed, inverse, row(g1))
        mlp = out[...].astype(F32)
        layer_out[where, :] = mid[where, :] + mlp + row(b2)


def widen_kernel(spot, after, near1, far1, near2, far2, w1, w2):
    part = near1.shape[0]
    for flag, near, far, ref in ((spot[2], near1, far1, w1), (spot[3], near2, far2, w2)):
        mine, other = halves(flag, part)
        ref[mine, :] = near[...].astype(F32)
        ref[other, :] = far[...].astype(F32)
        send_off(ref)


def unpack_kernel(
    spot, after, near, from_y, from_z, from_yz,
    wq, wk, wv, wo, b1, b2, g2, s2, bo, bq, bv, rel, g1, s1, both,
):
    place_yz = 2 * spot[2] + spot[3]
    width = near.shape[1]
    span = wo.shape[0]
    for ref, flip in ((near, 0), (from_y, 2), (from_z, 1), (from_yz, 3)):
        both[place_yz ^ flip] = ref[0:span, :]
    for j, ref in enumerate((wq, wk, wv)):
        for i in range(width // span):
            block = both[j, :, i * span:(i + 1) * span]
            ref[i * span:(i + 1) * span, :] = block.astype(F32)
        send_off(ref)
    wo[...] = both[3].astype(F32)
    send_off(wo)
    sums = (near[span:, :].astype(F32) + from_y[span:, :].astype(F32)) + (
        from_z[span:, :].astype(F32) + from_yz[span:, :].astype(F32)
    )
    for at, ref in ((0, b1), (1, b2), (2, g2), (3, s2), (4, bo), (6, g1), (7, s1)):
        ref[...] = sums[at]
    bq[...] = sums[5, :span]
    bv[...] = sums[5, span:2 * span]
    rel[...] = sums[8:8 + rel.shape[0], :rel.shape[1]]


def swap(value, axis, bit, size):
    return lax.ppermute(value, axis, [(i, i ^ bit) for i in range(size)])


def shards(
    inputs,
    query_weight,
    key_weight,
    value_weight,
    query_bias,
    value_bias,
    position_bias,
    proj_weight,
    proj_bias,
    norm1_gain,
    norm1_shift,
    norm2_gain,
    norm2_shift,
    up_weight,
    up_bias,
    down_weight,
    down_bias,
    segment_ids,
    valid_mask,
    position_index,
    out_cotangent,
    dp,
    tensor,
):
    tokens, width = inputs.shape
    half = tokens // 2
    span = query_weight.shape[1]
    units = up_weight.shape[1]
    heads = span // HD
    blocks = tokens // BLOCK
    me = lax.axis_index("tensor")
    mate = lax.axis_index("dp")
    bits = [1 << i for i in range(dp.bit_length() - 1)]
    flags = [(mate >> i) & 1 for i in range(len(bits))]
    lower = [flag == 0 for flag in flags]
    sizes = [(width >> (i + 1)) * n for i in range(len(bits)) for n in (1, 2)]
    starts = {
        (i, size): (flags[i] * size).astype(jnp.uint32) for i in range(len(bits)) for size in sizes
    }
    stops = {
        at: ((1 - flags[at[0]]) * at[1]).astype(jnp.uint32) for at in starts
    }
    spot = jnp.stack(
        [me, mate]
        + flags
        + [flag.astype(jnp.int32) for flag in lower]
        + [at.astype(jnp.int32) for at in list(starts.values()) + list(stops.values())]
    )
    seg = segment_ids.reshape(1, tokens)
    valid = valid_mask.reshape(1, tokens)
    wide = (tokens, width)
    narrow = (tokens, span)

    wo_x = swap(proj_weight, "tensor", 2, tensor)
    wo_c = swap(proj_weight, "tensor", 1, tensor)
    wo_d = swap(wo_x, "tensor", 1, tensor)

    att, first, q, k, v, probs = call(
        attend_kernel,
        [
            (narrow, BF, "vmem"), (wide, BF, "vmem"), (narrow, BF, "vmem"), (narrow, BF, "vmem"),
            (narrow, BF, "vmem"), ((blocks, heads * BLOCK, BLOCK), F32, "vmem"),
        ],
        [
            (spot, "smem"), (inputs, "hbm"), (norm1_gain, "hbm"), (norm1_shift, "hbm"),
            (query_weight, "hbm"), (key_weight, "hbm"), (value_weight, "hbm"), (query_bias, "hbm"),
            (value_bias, "hbm"), (position_bias.T, "hbm"), (position_index, "hbm"), (seg, "hbm"),
            (valid, "hbm"),
        ],
        cost=20,
    )
    (
        grad_hidden, out_cotangent, down_weight, inputs, norm1_gain, norm1_shift, position_index,
        query_weight, key_weight, value_weight, proj_weight, proj_bias, norm2_gain, norm2_shift,
        up_weight, up_bias, down_bias,
    ) = call(
        fetch_kernel,
        [((tokens, units), F32, "vmem")],
        [(att, "vmem"), (wo_x, "vmem")]
        + [
            (value, "hbm")
            for value in (
                out_cotangent, down_weight, inputs, norm1_gain, norm1_shift, position_index,
                query_weight, key_weight, value_weight, proj_weight, proj_bias, norm2_gain,
                norm2_shift, up_weight, up_bias, down_bias,
            )
        ],
        exports=tuple(range(2, 18)),
        cost=0,
    )
    att_x, down_bias = lax.optimization_barrier((swap(att, "tensor", 2, tensor), down_bias))
    att_c = swap(att, "tensor", 1, tensor)
    att_d = swap(att_x, "tensor", 1, tensor)

    mid, second, hidden, gpre, keep3, send3 = call(
        mlp_kernel,
        [
            (wide, F32, "vmem"), (wide, BF, "vmem"), ((tokens, units), BF, "vmem"),
            ((tokens, units), BF, "vmem"), ((half, width), F32, "vmem"), ((half, width), BF, "vmem"),
        ],
        [
            (spot, "smem"), (att, "vmem"), (att_c, "vmem"), (att_x, "vmem"), (att_d, "vmem"),
            (proj_weight, "vmem"), (wo_c, "vmem"), (wo_x, "vmem"), (wo_d, "vmem"),
            (inputs, "vmem"), (proj_bias, "vmem"), (norm2_gain, "vmem"), (norm2_shift, "vmem"),
            (up_weight, "vmem"), (up_bias, "vmem"), (grad_hidden, "vmem"),
        ],
        scratch=[((tokens, tensor * span), BF), ((tensor * span, width), BF)],
        cost=2,
    )

    def fold(value, other):
        return (value.astype(F32) + other.astype(F32)).astype(BF)

    own1, away1, own2, away2, small_a = call(
        mlp_grad_kernel,
        [((half, width), BF, "vmem")] * 4 + [((8, width), BF, "vmem")],
        [
            (spot, "smem"), (second, "vmem"), (hidden, "vmem"), (gpre, "vmem"),
            (out_cotangent, "vmem"),
        ],
        scratch=[((width, units), BF)],
        cost=2,
    )
    come3 = swap(send3, "tensor", 1, tensor)
    come3, small_a, away1, away2 = lax.optimization_barrier((come3, small_a, away1, away2))
    pair3 = fold(keep3, come3)
    keep2, send2 = call(
        mlp_out_kernel,
        [((half, width), BF, "vmem"), ((half, width), BF, "vmem")],
        [(spot, "smem"), (hidden, "vmem"), (down_weight, "vmem")],
        cost=1,
    )
    come3, come_a, come_b, keep2, send2 = lax.optimization_barrier(
        (
            swap(pair3, "tensor", 2, tensor),
            swap(away1, "dp", bits[0], dp),
            swap(away2, "dp", bits[1], dp),
            keep2,
            send2,
        )
    )
    sum3 = fold(pair3, come3)
    rest3 = swap(sum3, "tensor", 1, tensor)

    def meet(own, along_y, along_z, along_yz):
        return (
            own,
            swap(along_y, "dp", bits[0], dp),
            swap(along_z, "dp", bits[1], dp),
            swap(along_yz, "dp", bits[0] | bits[1], dp),
        )

    def combine(parts):
        own, y, z, yz = [part.astype(F32) for part in parts]
        return ((own + y) + (z + yz)).astype(BF)

    piece = ((span, width), BF, "vmem")
    gmid, att_own, att_y, att_z, att_yz, gq, gk, gv, scores, sums, norm1 = call(
        attend_back_kernel,
        [
            (wide, F32, "vmem"), piece, piece, piece, piece, (narrow, BF, "vmem"),
            (narrow, BF, "vmem"), (narrow, BF, "vmem"), ((heads * BLOCK, BLOCK), F32, "vmem"),
            ((8, width), F32, "vmem"), ((ROWS, width), BF, "vmem"),
        ],
        [
            (spot, "smem"), (sum3, "vmem"), (rest3, "vmem"), (mid, "vmem"),
            (out_cotangent, "vmem"), (norm2_gain, "vmem"), (proj_weight, "vmem"), (v, "vmem"),
            (probs, "vmem"), (k, "vmem"), (q, "vmem"), (first, "vmem"), (att, "vmem"),
            (query_weight, "vmem"), (key_weight, "vmem"), (value_weight, "vmem"),
            (norm1_gain, "vmem"), (norm1_shift, "vmem"),
        ],
        scratch=[(wide, F32), (wide, BF), (narrow, BF), ((4 * span, width), BF)],
        cost=1,
    )
    left = jnp.uint32(0)

    def pick(value, i):
        part = value.shape[0] // 2
        return (
            lax.dynamic_slice(value, (starts[i, part], left), (part, width)),
            lax.dynamic_slice(value, (stops[i, part], left), (part, width)),
        )

    def gather(own, i):
        other = swap(own, "dp", bits[i], dp)
        return jnp.where(
            lower[i], jnp.concatenate([own, other]), jnp.concatenate([other, own])
        )

    more = range(2, len(bits))

    keep_a, away_a = pick(fold(own1, come_a), 1)
    keep_b, away_b = pick(fold(own2, come_b), 0)
    (
        come_a, come_b, att_own, att_y, att_z, att_yz, gq, gk, gv, scores, sums, norm1,
    ) = lax.optimization_barrier(
        (
            swap(away_a, "dp", bits[1], dp), swap(away_b, "dp", bits[0], dp), att_own, att_y,
            att_z, att_yz, gq, gk, gv, scores, sums, norm1,
        )
    )
    mlp_chunk = jnp.concatenate([fold(keep_a, come_a), fold(keep_b, come_b)])
    pair2 = fold(keep2, swap(send2, "tensor", 1, tensor))
    sum2 = fold(pair2, swap(pair2, "tensor", 2, tensor))
    rest2 = swap(sum2, "tensor", 1, tensor)
    att_parts = meet(att_own, att_y, att_z, att_yz)
    chunk = combine(att_parts)
    (small_b,) = call(
        sums_kernel,
        [((16, width), BF, "vmem")],
        [(att_parts[1], "vmem"), (scores, "vmem"), (sums, "vmem"), (position_index, "vmem"),
            (small_a, "vmem"),
        ],
        scratch=[((16, width), F32)],
        cost=1,
    )
    norm1, small_b = lax.optimization_barrier((norm1, small_b))
    across = [swap(norm1, "tensor", flip, tensor).astype(F32) for flip in (1, 2, 3)]
    norm1 = ((norm1.astype(F32) + across[0]) + (across[1] + across[2])).astype(BF)
    keep4, send4 = call(
        attend_out_kernel,
        [((half, width), BF, "vmem"), ((half, width), BF, "vmem")],
        [
            (spot, "smem"), (chunk, "vmem"), (small_b, "vmem"), (gq, "vmem"), (gk, "vmem"), (gv, "vmem"),
            (query_weight, "vmem"), (key_weight, "vmem"), (value_weight, "vmem"),
        ],
        cost=1,
    )

    pair4 = fold(keep4, swap(send4, "tensor", 1, tensor))
    sum4 = fold(pair4, swap(pair4, "tensor", 2, tensor))
    rest4 = swap(sum4, "tensor", 1, tensor)

    for i in more:
        mlp_chunk = fold(mlp_chunk, swap(mlp_chunk, "dp", bits[i], dp))
    chunk = jnp.concatenate([chunk, small_b + norm1])
    for i in more:
        chunk = fold(chunk, swap(chunk, "dp", bits[i], dp))
    chunks = meet(chunk, chunk, chunk, chunk)
    near1 = gather(mlp_chunk[:mlp_chunk.shape[0] // 2], 1)
    near2 = gather(mlp_chunk[mlp_chunk.shape[0] // 2:], 0)
    far1 = swap(near1, "dp", bits[0], dp)
    far2 = swap(near2, "dp", bits[1], dp)
    layer_out, input_grad = call(
        finish_kernel,
        [(wide, F32, "hbm"), (wide, F32, "hbm")],
        [
            (spot, "smem"), (sum4, "vmem"), (rest4, "vmem"), (sum2, "vmem"), (rest2, "vmem"), (gmid, "vmem"), (inputs, "vmem"),
            (norm1_gain, "vmem"), (mid, "vmem"), (down_bias, "vmem"),
        ],
        cost=2,
    )
    w1_total, w2_total = call(
        widen_kernel,
        [((width, units), F32, "hbm"), ((units, width), F32, "hbm")],
        [(spot, "smem"), (layer_out, "keep")]
        + [(value, "vmem") for value in (near1, far1, near2, far2)],
    )
    vector, short = ((width,), F32, "hbm"), ((span,), F32, "hbm")
    (
        wq_total, wk_total, wv_total, wo_total, b1_total, b2_total, g2_total, s2_total, bo_total,
        bq_total, bv_total, rel_total, g1_total, s1_total,
    ) = call(
        unpack_kernel,
        [
            ((width, span), F32, "hbm"), ((width, span), F32, "hbm"), ((width, span), F32, "hbm"),
            ((span, width), F32, "hbm"), vector, vector, vector, vector, vector, short, short,
            ((heads, position_bias.shape[0]), F32, "hbm"), vector, vector,
        ],
        [(spot, "smem"), (w1_total, "keep")] + [(value, "vmem") for value in chunks],
        scratch=[((4, span, width), BF)],
    )
    rel_total = rel_total.T

    return (
        layer_out,
        input_grad,
        wq_total,
        wk_total,
        wv_total,
        bq_total,
        bv_total,
        rel_total,
        wo_total,
        bo_total,
        g1_total,
        s1_total,
        g2_total,
        s2_total,
        w1_total,
        b1_total,
        w2_total,
        b2_total,
    )


def solution(mesh):
    dp, tensor = mesh.shape["dp"], mesh.shape["tensor"]

    def body(*args):
        return shards(*args, dp=dp, tensor=tensor)

    column, line, whole = P(None, "tensor"), P("tensor"), P()
    return jax.shard_map(
        body,
        mesh=mesh,
        in_specs=(
            P("dp", None),
            column,
            column,
            column,
            line,
            line,
            column,
            P("tensor", None),
            whole,
            whole,
            whole,
            whole,
            whole,
            column,
            line,
            P("tensor", None),
            whole,
            P("dp", None),
            P("dp", None),
            whole,
            P("dp", None),
        ),
        out_specs=(
            P("dp", None),
            P("dp", None),
            column,
            column,
            column,
            line,
            line,
            column,
            P("tensor", None),
            whole,
            whole,
            whole,
            whole,
            whole,
            column,
            line,
            P("tensor", None),
            whole,
        ),
        check_vma=False,
    )
```
